128 devices in a mesh: azim: 16 (over y, z), plane: 8 (over x, core).
Axes of the slice: x: 4, y: 4, z: 4, core: 2. Of those that a mesh axis runs over, the one named last changes fastest.
Arguments:
- state: float32 [5, 192, 32768], P(None, 'azim', 'plane'), may hold values from -6 to 6
- speed: float32 [192, 32768], P('azim', 'plane'), may hold values from -2 to 2
- sigma: float32 [192, 32768], P('azim', 'plane'), may hold values from 1 to 24576
- dissipation: float32 [192, 32768], P('azim', 'plane'), may hold values from 0.05 to 1
- fringe: int32 [192, 32768], P('azim', 'plane'), may hold values from 0 to 1, as said below
- destination: int32 [2048, 1], P(('azim', 'plane')), may hold values from 0 to 7; in each aligned block of 16 rows (0 to 15, 16 to 31, ...) at most 4 rows name the same one
- donor: int32 [2048], P(('azim', 'plane')), may hold values from 0 to 11
- receptor: int32 [2048], P(('azim', 'plane')), may hold values from 0 to 11
- offset_y: int32 [2048], P(('azim', 'plane')), may hold values from 0 to 63
- offset_x: int32 [2048], P(('azim', 'plane')), may hold values from 0 to 63
- fraction_y: float32 [2048], P(('azim', 'plane')), may hold values from 0 to 1
- fraction_x: float32 [2048], P(('azim', 'plane')), may hold values from 0 to 1
Outputs:
- update: float32 [5, 192, 32768], P(None, 'azim', 'plane')
The draws below stay inside these ranges and needn't reach their ends.
Inputs may be any that keep to these rules, and one draw needn't show every extreme that they name: The 16 entries of one device name each destination at most 4 times. `fringe`: a plane cell is a receptor at all of its 192 azimuthal rows or at none.
All inputs are finite; a program needn't handle non-finite values.
Results may differ from the reference program's by a relative error of at most 0.0003.
Values sent between devices are 32-bit elements; how exact they have to be, the bound alone decides.
A program may use at most 128 MiB of HBM per device.

```python
import math
import jax
import jax.numpy as jnp
import numpy as np
from jax import lax

FIELDS = 5
TILE = 64
CAP = 4
A_DEV = 12
TILES_DEV = 1
SLOTS = 16
NA = 192
NP = 32768
N_AZIM = 16
N_PLANE = 8


def draw_fringe(key, part):
    picks = jax.random.randint(jax.random.fold_in(key, 7), (1, NP), 0, 16)
    column = (picks == 0).astype(jnp.int32)
    return jnp.broadcast_to(column, (NA, NP)).astype(jnp.int32)


def draw_sigma(key, part):
    column_key = jax.random.fold_in(key, 11)
    row_key = jax.random.fold_in(key, 13)
    column_scale = jnp.exp(jax.random.uniform(column_key, (1, NP), jnp.float32, 0.0, jnp.log(8192.0)))
    row_factor = jax.random.uniform(row_key, (NA, NP), jnp.float32, 1.0, 3.0)
    return (column_scale * row_factor).astype(jnp.float32)


def set_ends(drawn, own_key, low, high):
    index_at = [jax.random.randint(jax.random.fold_in(own_key, axis), (), 0, length) for axis, length in enumerate(drawn.shape)]
    longest = drawn.shape.index(max(drawn.shape))
    beside = index_at[:longest] + [(index_at[longest] + 1) % drawn.shape[longest]] + index_at[longest + 1:]
    return drawn.at[tuple(index_at)].set(low).at[tuple(beside)].set(high)


def level_of(stream_key, dims, shards, low, largest):
    gain, own = 1.0, jax.random.fold_in(stream_key, 6)
    for dim, shards_of in shards:
        heights = jnp.exp(jax.random.uniform(jax.random.fold_in(own, dim), (shards_of,), jnp.float32, low / len(shards), largest / len(shards)))
        gain = gain * jnp.repeat(heights, dims[dim] // shards_of).reshape([-1 if axis == dim else 1 for axis in range(len(dims))])
    return gain


def routed_block(own_key, own, number, rows, number_of, top, reach, slope):
    ranking = jax.random.permutation(own_key, number_of)
    heavy_load, common = portions_of(number_of, rows * top, reach, slope, True), portions_of(number_of, rows * top, reach, slope, False)
    places = jnp.arange(number_of)

    def named(lengths, rotation):
        used = int((lengths > 0).sum())
        fixed = max(1, used // 4)
        shifted = fixed + (places - fixed + rotation * (used - fixed)) % max(1, number_of - fixed)
        return jnp.zeros((number_of,), jnp.int32).at[ranking[jnp.where(places < fixed, places, shifted)]].set(jnp.asarray(lengths, jnp.int32))

    lengths = jnp.where(number % 4 == 0, named(heavy_load, number // 4), named(common, number - number // 4 - 1))
    mixed = jax.random.permutation(jax.random.fold_in(own, 3), number_of)
    source_of, receiver = mixed[0:number_of // 2 * 2:2], mixed[1:number_of // 2 * 2:2]
    room = jnp.minimum(lengths[source_of] - 1, reach - lengths[receiver]) // 2
    room = jnp.where((source_of == ranking[0]) | (receiver == ranking[0]) | (lengths[receiver] == 0), 0, jnp.maximum(room, 0))
    shifted = jax.random.randint(jax.random.fold_in(own, 4), (number_of // 2,), 0, 1 << 20) % (room + 1)
    lengths = lengths.at[source_of].add(-shifted).at[receiver].add(shifted)
    items = jnp.searchsorted(jnp.cumsum(lengths), jnp.arange(rows * top), side="right").astype(jnp.int32)
    grid = items.reshape(top, rows).T
    grid = grid[jax.random.permutation(jax.random.fold_in(own, 1), rows)]
    rotation = jax.random.randint(jax.random.fold_in(own, 2), (rows, 1), 0, top)
    return jnp.take_along_axis(grid, (jnp.arange(top)[None, :] + rotation) % top, axis=1)


def portions_of(count, total, limit, skew, full):
    weights = [(1 << 20) // math.isqrt(standing ** skew) + 1 for standing in range(1, count + 1)]
    largest = limit if full else min(limit, max(-(-total // count), total * weights[0] // sum(weights)))
    least = 1 if total - largest >= count - 1 else 0
    given, spare = [largest] + [least] * (count - 1), total - largest - least * (count - 1)
    while spare > 0:
        free = [i for i in range(1, count) if given[i] < largest] or [i for i in range(1, count) if given[i] < limit]
        pool, remaining = sum([weights[i] for i in free]), spare
        for i in free:
            extra = min(limit - given[i], max(1, remaining * weights[i] // pool), spare)
            given[i] = given[i] + extra
            spare = spare - extra
    return np.array(given)


def centred(stream_key, dims, deviation, most, split=(), held_as=jnp.bfloat16):
    drawn = jax.random.normal(stream_key, dims, jnp.float32) * deviation
    if len(split) > 0:
        drawn = level_of(stream_key, dims, split, -0.22, 0.18) * drawn
    return jnp.clip(drawn, min=-most, max=most).astype(held_as)


def setup_inputs(seed: int = 0) -> dict:
    splits = jax.random.split(jax.random.key(seed), 13)
    state = centred(splits[0], (FIELDS, NA, NP), 1.0, 6.0, ((1, 16), (2, 8)), jnp.float32)
    speed = jnp.clip(jax.random.uniform(splits[1], (NA, NP), jnp.float32, -2.0, 2.0) * level_of(splits[1], (NA, NP), ((0, 16), (1, 8)), -0.4, 0.0), -2.0, 2.0)
    sigma = draw_sigma(jax.random.fold_in(splits[12], 71), 0)
    dissipation = jnp.clip(jnp.exp(math.log(1.0) - 2.9957323 * jax.random.uniform(splits[3], (NA, NP), jnp.float32) ** level_of(splits[3], (NA, NP), ((0, 16), (1, 8)), -0.2, 0.2)), 0.05, 1.0)
    fringe = draw_fringe(jax.random.fold_in(splits[12], 71), 0)
    destination_keys = jax.random.split(jax.random.fold_in(splits[5], 1), (N_AZIM * N_PLANE * SLOTS) // SLOTS)
    destination_turns = jax.random.permutation(jax.random.fold_in(splits[5], 3), (N_AZIM * N_PLANE * SLOTS) // SLOTS)
    destination = jax.vmap(lambda own, number: routed_block(jax.random.fold_in(splits[5], 2), own, number, SLOTS, N_PLANE, 1, CAP, 2))(destination_keys, destination_turns).reshape((N_AZIM * N_PLANE * SLOTS, 1))
    donor = set_ends(jax.random.randint(splits[6], (N_AZIM * N_PLANE * SLOTS,), 0, A_DEV * TILES_DEV), jax.random.fold_in(splits[6], 1), 0, (A_DEV * TILES_DEV) - 1).astype(jnp.int32)
    receptor = set_ends(jax.random.randint(splits[7], (N_AZIM * N_PLANE * SLOTS,), 0, A_DEV * TILES_DEV), jax.random.fold_in(splits[7], 1), 0, (A_DEV * TILES_DEV) - 1).astype(jnp.int32)
    offset_y = set_ends(jax.random.randint(splits[8], (N_AZIM * N_PLANE * SLOTS,), 0, TILE), jax.random.fold_in(splits[8], 1), 0, TILE - 1).astype(jnp.int32)
    offset_x = set_ends(jax.random.randint(splits[9], (N_AZIM * N_PLANE * SLOTS,), 0, TILE), jax.random.fold_in(splits[9], 1), 0, TILE - 1).astype(jnp.int32)
    fraction_y = jnp.clip(1.0 * jax.random.uniform(splits[10], (N_AZIM * N_PLANE * SLOTS,), jnp.float32) ** level_of(splits[10], (N_AZIM * N_PLANE * SLOTS,), ((0, 128),), -0.2, 0.2), 0.0, 1.0)
    fraction_x = jnp.clip(1.0 * jax.random.uniform(splits[11], (N_AZIM * N_PLANE * SLOTS,), jnp.float32) ** level_of(splits[11], (N_AZIM * N_PLANE * SLOTS,), ((0, 128),), -0.2, 0.2), 0.0, 1.0)
    return dict(state=state, speed=speed, sigma=sigma, dissipation=dissipation, fringe=fringe, destination=destination, donor=donor, receptor=receptor, offset_y=offset_y, offset_x=offset_x, fraction_y=fraction_y, fraction_x=fraction_x)


def band_factor(bands, width):
    count = 2 * width + 1

    def step(carry, row):
        pivots, upper_diagonals = carry
        current = [row[o] for o in range(count)]
        factors = []
        for j in range(width):
            factor = current[j] / pivots[j]
            factors.append(factor)
            for m in range(1, width + 1):
                current[j + m] = current[j + m] - factor * upper_diagonals[j, m - 1]
        pivot = current[width]
        upper_band_row = jnp.stack(current[width + 1:], axis=0)
        new_pivots = jnp.concatenate([pivots[1:], pivot[None]], axis=0)
        new_uppers = jnp.concatenate([upper_diagonals[1:], upper_band_row[None]], axis=0)
        return (new_pivots, new_uppers), (jnp.stack(factors, axis=0), pivot, upper_band_row)

    cells = bands.shape[2]
    start = (jnp.ones((width, cells), jnp.float32), jnp.zeros((width, width, cells), jnp.float32))
    unused, result = lax.scan(step, start, jnp.moveaxis(bands, 1, 0))
    return result


def band_apply(factored, right_side, width):
    factors, pivots, upper_diagonals = factored
    k = right_side.shape[0]
    cells = right_side.shape[2]

    def forward(carry, item):
        factor, value = item
        for j in range(width):
            value = value - factor[j][None] * carry[j]
        return jnp.concatenate([carry[1:], value[None]], axis=0), value

    start = jnp.zeros((width, k, cells), jnp.float32)
    unused, reduced = lax.scan(forward, start, (factors, jnp.moveaxis(right_side, 1, 0)))

    def backward(carry, item):
        pivot, upper, value = item
        for m in range(width):
            value = value - upper[m][None] * carry[m]
        value = value / pivot[None]
        return jnp.concatenate([value[None], carry[:-1]], axis=0), value

    unused, solved = lax.scan(backward, start, (pivots, upper_diagonals, reduced), reverse=True)
    return jnp.moveaxis(solved, 0, 1)


def small_solve(matrix, vector):
    size = len(vector)
    matrix = [list(line) for line in matrix]
    vector = list(vector)
    for p in range(size):
        for r in range(p + 1, size):
            factor = matrix[r][p] / matrix[p][p]
            for c in range(p + 1, size):
                matrix[r][c] = matrix[r][c] - factor * matrix[p][c]
            vector[r] = vector[r] - factor[None] * vector[p]
    result = [None] * size
    for r in range(size - 1, -1, -1):
        value = vector[r]
        for c in range(r + 1, size):
            value = value - matrix[r][c][None] * result[c]
        result[r] = value / matrix[r][r][None]
    return result


def periodic_solve(bands, right_side, width):
    count, n, cells = bands.shape
    index = jnp.arange(n, dtype=jnp.int32)[:, None]
    corner_columns = list(range(n - width, n)) + list(range(width))
    columns = [jnp.zeros((n, cells), jnp.float32) for c in corner_columns]
    inner = []
    for o in range(count):
        target = index + (o - width)
        inside = (target >= 0) & (target < n)
        inner.append(jnp.where(inside, bands[o], 0.0))
        wrapped = jnp.mod(target, n)
        for c in range(len(corner_columns)):
            columns[c] = columns[c] + jnp.where(jnp.logical_not(inside) & (wrapped == corner_columns[c]), bands[o], 0.0)
    factored = band_factor(jnp.stack(inner), width)
    k = right_side.shape[0]
    solved = band_apply(factored, jnp.concatenate([right_side, jnp.stack(columns)], axis=0), width)
    base = solved[:k]
    spikes = solved[k:]
    size = 2 * width
    matrix = [[spikes[c, corner_columns[r]] + (1.0 if r == c else 0.0) for c in range(size)] for r in range(size)]
    vector = [base[:, corner_columns[r]] for r in range(size)]
    coefficients = small_solve(matrix, vector)
    for c in range(size):
        base = base - spikes[c][None] * coefficients[c][:, None]
    return base


def interpolate(tiles, shift_y, shift_x, part_y, part_x):
    edge = tiles.shape[-1]
    index = jnp.arange(edge, dtype=jnp.int32)

    def weights(shift, part):
        first = jnp.mod(index[None, :] + shift[:, None], edge)
        second = jnp.mod(first + 1, edge)
        chosen = index[None, None, :]
        return ((chosen == first[:, :, None]).astype(jnp.float32) * (1.0 - part)[:, None, None]
                + (chosen == second[:, :, None]).astype(jnp.float32) * part[:, None, None])

    return jnp.einsum("sia,sfab,sjb->sfij", weights(shift_y, part_y), tiles, weights(shift_x, part_x),
                      precision=lax.Precision.HIGHEST)


def explicit_right_hand(minus_two, minus_one, middle, plus_one, plus_two, speed, sigma, dissipation):
    return (-0.5 * speed * (plus_one - minus_one) + sigma * (plus_one - 2.0 * middle + minus_one)
            - dissipation * (plus_two - 4.0 * plus_one + 6.0 * middle - 4.0 * minus_one + minus_two))


def coefficient_bands(speed, sigma, dissipation, fringe):
    keep = 1.0 - fringe.astype(jnp.float32)
    half = 0.5 * speed
    outer = keep * dissipation
    lower = keep * (-half - sigma - 4.0 * dissipation)
    upper = keep * (half - sigma - 4.0 * dissipation)
    center = 1.0 + keep * (2.0 * sigma + 10.0 * dissipation)
    return jnp.stack([outer, lower, center, upper, outer])


def reference(state, speed, sigma, dissipation, fringe, destination, donor, receptor, offset_y, offset_x, fraction_y, fraction_x):
    tile_cells = TILE * TILE
    planes = NP // tile_cells
    tiled = state.reshape(FIELDS, NA, planes, tile_cells)
    devices = N_AZIM * N_PLANE

    def one_device(carry, item):
        running_total, counts = carry
        device, target, source, landing, shift_y, shift_x, part_y, part_x = item
        azim_index = device // N_PLANE
        plane_index = device % N_PLANE
        source_row = azim_index * A_DEV + source // TILES_DEV
        source_column = plane_index * TILES_DEV + source % TILES_DEV
        tiles = jnp.moveaxis(tiled[:, source_row, source_column], 1, 0).reshape(SLOTS, FIELDS, TILE, TILE)
        donor_values = interpolate(tiles, shift_y, shift_x, part_y, part_x).reshape(SLOTS, FIELDS, tile_cells)
        target_row = azim_index * A_DEV + landing // TILES_DEV
        target_column = target * TILES_DEV + landing % TILES_DEV
        running_total = running_total.at[target_row, target_column].add(donor_values)
        counts = counts.at[target_row, target_column].add(jnp.ones((SLOTS,), jnp.float32))
        return (running_total, counts), None

    start = (jnp.zeros((NA, planes, FIELDS, tile_cells), jnp.float32), jnp.zeros((NA, planes), jnp.float32))
    items = (jnp.arange(devices, dtype=jnp.int32), destination[:, 0].reshape(devices, SLOTS),
             donor.reshape(devices, SLOTS), receptor.reshape(devices, SLOTS),
             offset_y.reshape(devices, SLOTS), offset_x.reshape(devices, SLOTS),
             fraction_y.reshape(devices, SLOTS), fraction_x.reshape(devices, SLOTS))
    (running_total, counts), unused = lax.scan(one_device, start, items)
    received = jnp.moveaxis(running_total, 2, 0).reshape(FIELDS, NA, NP)
    count_cells = jnp.repeat(counts, tile_cells, axis=1)
    explicit = explicit_right_hand(jnp.roll(state, 2, axis=1), jnp.roll(state, 1, axis=1), state,
                            jnp.roll(state, -1, axis=1), jnp.roll(state, -2, axis=1), speed, sigma, dissipation)
    relaxed = (received - count_cells * state) / (count_cells + 1.0)
    right_side = jnp.where(fringe == 1, relaxed, explicit)
    bands = coefficient_bands(speed, sigma, dissipation, fringe)
    band_blocks = jnp.moveaxis(bands.reshape(5, NA, planes, tile_cells), 2, 0)
    side_blocks = jnp.moveaxis(right_side.reshape(FIELDS, NA, planes, tile_cells), 2, 0)

    def solve_block(pair):
        return periodic_solve(pair[0], pair[1], 2)

    solved = lax.map(solve_block, (band_blocks, side_blocks))
    return jnp.moveaxis(solved, 0, 2).reshape(FIELDS, NA, NP)
```

```python
import functools

import jax
import jax.numpy as jnp
from jax import lax
from jax.experimental import pallas as pl
from jax.experimental.pallas import tpu as pltpu
from jax.sharding import PartitionSpec as P

TILE = 64
CAP = 4
FIELDS = 5
ROWS = 12
CELLS = TILE * TILE
LANES = 128
CHUNKS = CELLS // LANES
SLOTS = 16
COLS = FIELDS + 4
TIPS = 4 * COLS
BACK = 4 * FIELDS
MESH = pl.DeviceIdType.MESH
TIP_ROW = {0: 0, 1: 1, ROWS - 2: 2, ROWS - 1: 3}


def spread(source, dest, lead):
    def move(c, carry):
        lane = pl.multiple_of(c * LANES, LANES)
        row = pl.multiple_of(c * 8, 8)
        for f in range(lead):
            dest[f, 0, pl.ds(row, 8), :] = source[f, 0:8, pl.ds(lane, LANES)]
            dest[f, 1, pl.ds(row, 4), :] = source[f, 8:12, pl.ds(lane, LANES)]
        return carry

    lax.fori_loop(0, CHUNKS, move, 0, unroll=4)


def spread_flat(source, dest, slot):
    def move(c, carry):
        lane = pl.multiple_of(c * LANES, LANES)
        row = pl.multiple_of(c * 8, 8)
        dest[slot, 0, pl.ds(row, 8), :] = source[0:8, pl.ds(lane, LANES)]
        dest[slot, 1, pl.ds(row, 4), :] = source[8:12, pl.ds(lane, LANES)]
        return carry

    lax.fori_loop(0, CHUNKS, move, 0, unroll=4)


def prepare_kernel(
    destination,
    donor,
    receptor,
    offset_y,
    offset_x,
    fraction_y,
    fraction_x,
    state,
    speed,
    sigma,
    dissipation,
    packed,
    landing,
    tips,
    solved,
    cells,
    coefs,
    twice,
    counts,
):
    planes = landing.shape[0]
    spread(state, cells, FIELDS)
    for slot, source in enumerate((speed, sigma, dissipation)):
        spread_flat(source, coefs, slot)

    landing[...] = jnp.full(landing.shape, -1, jnp.int32)
    for d in range(planes):
        counts[d] = 0
    lane = lax.broadcasted_iota(jnp.int32, (CHUNKS, LANES), 1)
    column = lane & (TILE - 1)
    low_half = lane < TILE

    def one_entry(e, carry):
        target = destination[e, 0]
        rank = counts[target]
        counts[target] = rank + 1
        landing[target, pl.ds(rank, 1), :] = jnp.full((1, LANES), receptor[e], jnp.int32)
        row = donor[e]
        block = jnp.where(row >= 8, 1, 0)
        inner = row - 8 * block
        ox = offset_x[e]
        oy = offset_y[e]
        fx = fraction_x[e]
        fy = fraction_y[e]
        half = oy >> 1
        odd = (oy & 1) == 1
        even_first = jnp.where(odd, 0.0, 1.0 - fy)
        even_second = jnp.where(odd, fy, 0.0)
        odd_weight = jnp.where(odd, 1.0 - fy, fy)
        near = column + ox < TILE
        far = column + ox + 1 < TILE
        for f in range(FIELDS):
            tile = cells[f, block, pl.ds(inner, CHUNKS, stride=8), :]
            first = pltpu.roll(tile, LANES - ox, 1)
            second = pltpu.roll(tile, LANES - 1 - ox, 1)
            first = jnp.where(near, first, pltpu.roll(first, TILE, 1))
            second = jnp.where(far, second, pltpu.roll(second, TILE, 1))
            mixed = (1.0 - fx) * first + fx * second
            swapped = pltpu.roll(mixed, TILE, 1)
            twice[0, f, 0:CHUNKS, :] = mixed
            twice[0, f, CHUNKS : 2 * CHUNKS, :] = mixed
            twice[1, f, 0:CHUNKS, :] = swapped
            twice[1, f, CHUNKS : 2 * CHUNKS, :] = swapped
        for f in range(FIELDS):
            here = twice[0, f, pl.ds(half, CHUNKS), :]
            after = twice[0, f, pl.ds(half + 1, CHUNKS), :]
            odd_here = twice[1, f, pl.ds(half, CHUNKS), :]
            odd_after = twice[1, f, pl.ds(half + 1, CHUNKS), :]
            packed[target, rank, f] = (
                even_first * here
                + even_second * after
                + odd_weight * jnp.where(low_half, odd_here, odd_after)
            )
        return carry

    lax.fori_loop(0, SLOTS, one_entry, 0)

    def eliminate(part, carry):
        base = part * 64
        at = pl.ds(pl.multiple_of(part * 8, 8), 8)

        def load(ref, lead, r):
            return ref[lead, r // 8, pl.ds(base + r % 8, 8, stride=8), :]

        upper1 = []
        upper2 = []
        fields1 = fields2 = None
        for r in range(ROWS):
            c = load(coefs, 0, r)
            s = load(coefs, 1, r)
            d = load(coefs, 2, r)
            half = 0.5 * c
            common = -s - 4.0 * d
            a1 = common - half
            e1 = common + half
            centre = 1.0 + (2.0 * s + 10.0 * d)
            weight = 1.0 + 4.0 * d
            if r == 0:
                pivot, u1_top = centre, e1
            elif r == 1:
                pivot = centre - a1 * upper1[0]
                u1_top = e1 - a1 * upper2[0]
            else:
                spike_a1 = a1
                a1 = a1 - d * upper1[r - 2]
                pivot = centre - d * upper2[r - 2] - a1 * upper1[r - 1]
                u1_top = e1 - a1 * upper2[r - 1]
            inverse = 1.0 / pivot
            upper1.append(u1_top * inverse)
            upper2.append(d * inverse)
            now = []
            for k in range(FIELDS + 2):
                if k < FIELDS:
                    value = weight * load(cells, k, r)
                elif r == 0:
                    now.append((d if k == FIELDS else a1) * inverse)
                    continue
                elif r == 1 and k == FIELDS + 1:
                    value = d
                else:
                    value = None
                if r >= 1:
                    term = a1 * fields1[k]
                    value = -term if value is None else value - term
                if r >= 2:
                    value = value - d * fields2[k]
                now.append(value * inverse)
            for k in range(FIELDS + 2):
                solved[r, k, at, :] = now[k]
            fields2, fields1 = fields1, now

        later1 = later2 = None
        for r in range(ROWS - 1, -1, -1):
            now = []
            for k in range(COLS):
                if k < FIELDS + 2:
                    value = solved[r, k, at, :]
                elif r == ROWS - 1:
                    value = upper1[r] if k == FIELDS + 2 else upper2[r]
                elif r == ROWS - 2 and k == FIELDS + 2:
                    value = upper2[r]
                else:
                    value = None
                if r < ROWS - 1:
                    term = upper1[r] * later1[k]
                    value = -term if value is None else value - term
                if r < ROWS - 2:
                    value = value - upper2[r] * later2[k]
                now.append(value)
            for k in range(COLS):
                solved[r, k, at, :] = now[k]
            if r in TIP_ROW:
                for k in range(COLS):
                    tips[pl.ds(part * 8 * TIPS + TIP_ROW[r] * COLS + k, 8, stride=TIPS), :] = now[k]
            later2, later1 = later1, now
        return carry

    lax.fori_loop(0, CHUNKS // 8, eliminate, 0)


def merge(left, right):
    def pair(matrix, columns):
        return [matrix[i][0] * columns[0] + matrix[i][1] * columns[1] for i in range(2)]

    gs = slice(0, FIELDS)
    ws = slice(FIELDS, FIELDS + 2)
    vs = slice(FIELDS + 2, FIELDS + 4)
    left_v = [[left[i][FIELDS + 2 + m] for m in range(2)] for i in range(4)]
    right_w = [[right[i][FIELDS + m] for m in range(2)] for i in range(4)]
    nothing = jnp.zeros((2,) + left[0].shape[1:], jnp.float32)
    product = [
        [sum(right_w[i][m] * left_v[2 + m][j] for m in range(2)) for j in range(2)]
        for i in range(2)
    ]
    m00, m01 = 1.0 - product[0][0], -product[0][1]
    m10, m11 = -product[1][0], 1.0 - product[1][1]
    scale = 1.0 / (m00 * m11 - m01 * m10)
    inverse = [[m11 * scale, -m01 * scale], [-m10 * scale, m00 * scale]]
    known = [jnp.concatenate([left[2 + i][gs], left[2 + i][ws]], axis=0) for i in range(2)]
    through = pair(right_w[:2], known)
    raw = [
        jnp.concatenate(
            [right[i][gs] - through[i][gs], -through[i][FIELDS:], right[i][vs]], axis=0
        )
        for i in range(2)
    ]
    inner_a = pair(inverse, raw)
    from_a = pair(left_v[2:], inner_a)
    inner_b = [
        jnp.concatenate([left[2 + i][gs], left[2 + i][ws], nothing], axis=0) - from_a[i]
        for i in range(2)
    ]
    from_a = pair(left_v[:2], inner_a)
    outer_a = [
        jnp.concatenate([left[i][gs], left[i][ws], nothing], axis=0) - from_a[i] for i in range(2)
    ]
    from_b = pair(right_w[2:], inner_b)
    outer_b = [
        jnp.concatenate([right[2 + i][gs], nothing, right[2 + i][vs]], axis=0) - from_b[i]
        for i in range(2)
    ]
    return outer_a + outer_b


def close(block):
    matrix = []
    for i in range(4):
        line = [block[i][FIELDS + 2], block[i][FIELDS + 3], block[i][FIELDS], block[i][FIELDS + 1]]
        line[i] = 1.0 + line[i]
        matrix.append(line)
    values = [block[i][0:FIELDS] for i in range(4)]
    for p in range(4):
        scale = 1.0 / matrix[p][p]
        for c in range(p + 1, 4):
            matrix[p][c] = matrix[p][c] * scale
        values[p] = values[p] * scale
        for r in range(p + 1, 4):
            for c in range(p + 1, 4):
                matrix[r][c] = matrix[r][c] - matrix[r][p] * matrix[p][c]
            values[r] = values[r] - matrix[r][p] * values[p]
    for r in range(2, -1, -1):
        for c in range(r + 1, 4):
            values[r] = values[r] - matrix[r][c] * values[c]
    return values


def exchange_kernel(
    azims,
    planes,
    packed,
    landing,
    tips,
    packed_in,
    landing_in,
    borders,
    tips_in,
    ping,
    pong,
    firsts,
    answers,
    tile_send,
    tile_recv,
    land_send,
    land_recv,
    tips_send,
    tips_recv,
    back_send,
    back_recv,
    own_sem,
):
    a = lax.axis_index("azim")
    p = lax.axis_index("plane")
    per = CHUNKS // azims
    tip_rows = per * TIPS
    back_rows = per * BACK

    barrier = pltpu.get_barrier_semaphore()
    for o in range(1, planes):
        pl.semaphore_signal(
            barrier, inc=1, device_id=(a, lax.rem(p + o, planes)), device_id_type=MESH
        )
    for o in range(1, azims):
        pl.semaphore_signal(
            barrier, inc=1, device_id=(lax.rem(a + o, azims), p), device_id_type=MESH
        )
    pl.semaphore_wait(barrier, planes + azims - 2)

    def to_azim(source, dest, rows, send, recv, o):
        there = lax.rem(a + o, azims)
        return pltpu.make_async_remote_copy(
            src_ref=source.at[pl.ds(pl.multiple_of(there * rows, 8), rows), :],
            dst_ref=dest.at[pl.ds(pl.multiple_of(a * rows, 8), rows), :],
            send_sem=send.at[o],
            recv_sem=recv.at[o],
            device_id=(there, p),
            device_id_type=MESH,
        )

    def own_azim(source, dest, rows, index):
        at = pl.ds(pl.multiple_of(a * rows, 8), rows)
        return pltpu.make_async_copy(source.at[at, :], dest.at[at, :], own_sem.at[index])

    def to_plane(o):
        there = lax.rem(p + o, planes)
        return (
            pltpu.make_async_remote_copy(
                src_ref=packed.at[there],
                dst_ref=packed_in.at[p],
                send_sem=tile_send.at[o],
                recv_sem=tile_recv.at[o],
                device_id=(a, there),
                device_id_type=MESH,
            ),
            pltpu.make_async_remote_copy(
                src_ref=landing.at[there],
                dst_ref=landing_in.at[p],
                send_sem=land_send.at[o],
                recv_sem=land_recv.at[o],
                device_id=(a, there),
                device_id_type=MESH,
            ),
        )

    tip_copies = [to_azim(tips, tips_in, tip_rows, tips_send, tips_recv, o) for o in range(1, azims)]
    for copy in tip_copies:
        copy.start()
    own_tips = own_azim(tips, tips_in, tip_rows, 0)
    own_tips.start()
    tile_copies = []
    for o in range(1, planes):
        tile_copies.extend(to_plane(o))
    for copy in tile_copies:
        copy.start()
    own_tiles = pltpu.make_async_copy(packed.at[p], packed_in.at[p], own_sem.at[2])
    own_land = pltpu.make_async_copy(landing.at[p], landing_in.at[p], own_sem.at[3])
    own_tiles.start()
    own_land.start()

    own_tips.wait()
    for copy in tip_copies:
        copy.wait()

    for v in range(TIPS):
        value = tips_in[pl.ds(v, CHUNKS, stride=TIPS), :]
        ping[v, 0:CHUNKS, :] = value
        ping[v, CHUNKS : 2 * CHUNKS, :] = value

    source, dest = ping, pong
    step = 1
    while step < azims:

        def level(part, carry, source=source, dest=dest, shift=step * per):
            row = pl.multiple_of(part * 8, 8)
            left = [source[COLS * i : COLS * (i + 1), pl.ds(row, 8), :] for i in range(4)]
            right = [source[COLS * i : COLS * (i + 1), pl.ds(row + shift, 8), :] for i in range(4)]
            for i, value in enumerate(merge(left, right)):
                dest[COLS * i : COLS * (i + 1), pl.ds(row, 8), :] = value
                dest[COLS * i : COLS * (i + 1), pl.ds(row + CHUNKS, 8), :] = value
            return carry

        lax.fori_loop(0, CHUNKS // 8, level, 0)
        source, dest = dest, source
        step *= 2

    def last(part, carry):
        row = pl.multiple_of(part * 8, 8)
        block = [source[COLS * i : COLS * (i + 1), pl.ds(row, 8), :] for i in range(4)]
        values = close(block)
        for i in range(2):
            firsts[FIELDS * i : FIELDS * (i + 1), pl.ds(row, 8), :] = values[i]
            firsts[FIELDS * i : FIELDS * (i + 1), pl.ds(row + CHUNKS, 8), :] = values[i]
            for f in range(FIELDS):
                answers[pl.ds(part * 8 * BACK + i * FIELDS + f, 8, stride=BACK), :] = values[2 + i][f]
        return carry

    lax.fori_loop(0, CHUNKS // 8, last, 0)
    for v in range(2 * FIELDS):
        answers[pl.ds(2 * FIELDS + v, CHUNKS, stride=BACK), :] = firsts[v, per : per + CHUNKS, :]

    back_copies = [
        to_azim(answers, borders, back_rows, back_send, back_recv, o) for o in range(1, azims)
    ]
    for copy in back_copies:
        copy.start()
    own_back = own_azim(answers, borders, back_rows, 1)
    own_back.start()
    own_back.wait()
    for copy in back_copies:
        copy.wait()
    own_tiles.wait()
    own_land.wait()
    for copy in tile_copies:
        copy.wait()


def finish_kernel(landing, packed, borders, solved, state, fringe, out, cells, mask, total, counts):
    planes = landing.shape[0]
    spread(state, cells, FIELDS)
    for c in range(CHUNKS):
        mask[c : c + 1, :] = fringe[0:1, c * LANES : (c + 1) * LANES]
    for r in range(ROWS):
        counts[r] = 0.0
    total[...] = jnp.zeros(total.shape, jnp.float32)

    def add(slot, carry):
        d = slot // CAP
        k = slot - d * CAP
        row = landing[d, k, 0]

        @pl.when(row >= 0)
        def _():
            total[row] = total[row] + packed[d, k]
            counts[row] = counts[row] + 1.0

        return carry

    lax.fori_loop(0, planes * CAP, add, 0)

    def part_of(part, carry):
        at = pl.ds(pl.multiple_of(part * 8, 8), 8)
        chosen = mask[at, :] == 1
        previous = [
            [
                borders[pl.ds(part * 8 * BACK + i * FIELDS + f, 8, stride=BACK), :]
                for f in range(FIELDS)
            ]
            for i in range(2)
        ]
        following = [
            [
                borders[pl.ds(part * 8 * BACK + (2 + i) * FIELDS + f, 8, stride=BACK), :]
                for f in range(FIELDS)
            ]
            for i in range(2)
        ]
        for r in range(ROWS):
            w = [solved[r, FIELDS + i, at, :] for i in range(2)]
            v = [solved[r, FIELDS + 2 + i, at, :] for i in range(2)]
            count = counts[r]
            for f in range(FIELDS):
                where = (f, r // 8, pl.ds(part * 64 + r % 8, 8, stride=8))
                q = cells[where + (slice(None),)]
                value = solved[r, f, at, :] - q
                for i in range(2):
                    value = value - w[i] * previous[i][f] - v[i] * following[i][f]
                relaxed = (total[r, f, at, :] - count * q) / (count + 1.0)
                cells[where + (slice(None),)] = jnp.where(chosen, relaxed, value)
        return carry

    lax.fori_loop(0, CHUNKS // 8, part_of, 0)

    def move(c, carry):
        lane = pl.multiple_of(c * LANES, LANES)
        row = pl.multiple_of(c * 8, 8)
        for f in range(FIELDS):
            out[f, 0:8, pl.ds(lane, LANES)] = cells[f, 0, pl.ds(row, 8), :]
            out[f, 8:12, pl.ds(lane, LANES)] = cells[f, 1, pl.ds(row, 4), :]
        return carry

    lax.fori_loop(0, CHUNKS, move, 0, unroll=4)


def f32(*shape):
    return jax.ShapeDtypeStruct(shape, jnp.float32)


def local(
    state,
    speed,
    sigma,
    dissipation,
    fringe,
    destination,
    donor,
    receptor,
    offset_y,
    offset_x,
    fraction_y,
    fraction_x,
):
    azims = lax.axis_size("azim")
    planes = lax.axis_size("plane")
    vmem = pl.BlockSpec(memory_space=pltpu.VMEM)
    smem = pl.BlockSpec(memory_space=pltpu.SMEM)
    anywhere = pl.BlockSpec(memory_space=pl.ANY)
    packed, landing, tips, solved = pl.pallas_call(
        prepare_kernel,
        out_shape=(
            f32(planes, CAP, FIELDS, CHUNKS, LANES),
            jax.ShapeDtypeStruct((planes, 8, LANES), jnp.int32),
            f32(CHUNKS * TIPS, LANES),
            f32(ROWS, COLS, CHUNKS, LANES),
        ),
        in_specs=[smem] * 7 + [vmem] * 4,
        out_specs=(vmem,) * 4,
        scratch_shapes=[
            pltpu.VMEM((FIELDS, 2, CHUNKS * 8, LANES), jnp.float32),
            pltpu.VMEM((3, 2, CHUNKS * 8, LANES), jnp.float32),
            pltpu.VMEM((2, FIELDS, 2 * CHUNKS, LANES), jnp.float32),
            pltpu.SMEM((planes,), jnp.int32),
        ],
        compiler_params=pltpu.CompilerParams(vmem_limit_bytes=32 * 2**20),
        name="prepare",
    )(
        destination,
        donor,
        receptor,
        offset_y,
        offset_x,
        fraction_y,
        fraction_x,
        state,
        speed,
        sigma,
        dissipation,
    )
    packed_in, landing_in, borders = pl.pallas_call(
        functools.partial(exchange_kernel, azims, planes),
        out_shape=(
            f32(planes, CAP, FIELDS, CHUNKS, LANES),
            jax.ShapeDtypeStruct((planes, 8, LANES), jnp.int32),
            f32(CHUNKS * BACK, LANES),
        ),
        in_specs=[anywhere, anywhere, vmem],
        out_specs=(anywhere, anywhere, vmem),
        scratch_shapes=[
            pltpu.VMEM((CHUNKS * TIPS, LANES), jnp.float32),
            pltpu.VMEM((TIPS, 2 * CHUNKS, LANES), jnp.float32),
            pltpu.VMEM((TIPS, 2 * CHUNKS, LANES), jnp.float32),
            pltpu.VMEM((2 * FIELDS, 2 * CHUNKS, LANES), jnp.float32),
            pltpu.VMEM((CHUNKS * BACK, LANES), jnp.float32),
            pltpu.SemaphoreType.DMA((planes,)),
            pltpu.SemaphoreType.DMA((planes,)),
            pltpu.SemaphoreType.DMA((planes,)),
            pltpu.SemaphoreType.DMA((planes,)),
            pltpu.SemaphoreType.DMA((azims,)),
            pltpu.SemaphoreType.DMA((azims,)),
            pltpu.SemaphoreType.DMA((azims,)),
            pltpu.SemaphoreType.DMA((azims,)),
            pltpu.SemaphoreType.DMA((4,)),
        ],
        compiler_params=pltpu.CompilerParams(
            collective_id=0, has_side_effects=True, vmem_limit_bytes=32 * 2**20
        ),
        name="exchange",
    )(packed, landing, tips)
    return pl.pallas_call(
        finish_kernel,
        out_shape=f32(FIELDS, ROWS, CELLS),
        in_specs=[smem] + [vmem] * 5,
        out_specs=vmem,
        scratch_shapes=[
            pltpu.VMEM((FIELDS, 2, CHUNKS * 8, LANES), jnp.float32),
            pltpu.VMEM((CHUNKS, LANES), jnp.int32),
            pltpu.VMEM((ROWS, FIELDS, CHUNKS, LANES), jnp.float32),
            pltpu.SMEM((ROWS,), jnp.float32),
        ],
        compiler_params=pltpu.CompilerParams(vmem_limit_bytes=32 * 2**20),
        name="finish",
    )(landing_in, packed_in, borders, solved, state, fringe)


def solution(mesh):
    in_specs = (
        P(None, "azim", "plane"),
        P("azim", "plane"),
        P("azim", "plane"),
        P("azim", "plane"),
        P("azim", "plane"),
        P(("azim", "plane"), None),
        P(("azim", "plane")),
        P(("azim", "plane")),
        P(("azim", "plane")),
        P(("azim", "plane")),
        P(("azim", "plane")),
        P(("azim", "plane")),
    )
    out_specs = P(None, "azim", "plane")
    return jax.shard_map(local, mesh=mesh, in_specs=in_specs, out_specs=out_specs, check_vma=False)
```

```python
import functools

import jax
import jax.numpy as jnp
from jax import lax
from jax.experimental import pallas as pl
from jax.experimental.pallas import tpu as pltpu
from jax.sharding import PartitionSpec as P

TILE = 64
CAP = 4
FIELDS = 5
ROWS = 12
CELLS = TILE * TILE
LANES = 128
CHUNKS = CELLS // LANES
SLOTS = 16
COLS = FIELDS + 4
TIPS = 4 * COLS
BACK = 4 * FIELDS
MESH = pl.DeviceIdType.MESH
TIP_ROW = {0: 0, 1: 1, ROWS - 2: 2, ROWS - 1: 3}


def spread(source, dest):
    def move(c, carry):
        lane = pl.multiple_of(c * LANES, LANES)
        row = pl.multiple_of(c * 8, 8)
        for f in range(source.shape[0]):
            dest[f, 0, pl.ds(row, 8), :] = source[f, 0:8, pl.ds(lane, LANES)]
            dest[f, 1, pl.ds(row, 4), :] = source[f, 8:12, pl.ds(lane, LANES)]
        return carry

    lax.fori_loop(0, CHUNKS, move, 0, unroll=4)


def eliminate(cells, coefs, solved, tips, part):
    base = part * 64
    at = pl.ds(pl.multiple_of(part * 8, 8), 8)

    def load(ref, lead, r):
        return ref[lead, r // 8, pl.ds(base + r % 8, 8, stride=8), :]

    upper1 = []
    upper2 = []
    fields1 = fields2 = None
    for r in range(ROWS):
        c = load(coefs, 0, r)
        s = load(coefs, 1, r)
        d = load(coefs, 2, r)
        half = 0.5 * c
        common = -s - 4.0 * d
        a1 = common - half
        e1 = common + half
        centre = 1.0 + (2.0 * s + 10.0 * d)
        weight = 1.0 + 4.0 * d
        if r == 0:
            pivot, u1_top = centre, e1
        elif r == 1:
            pivot = centre - a1 * upper1[0]
            u1_top = e1 - a1 * upper2[0]
        else:
            a1 = a1 - d * upper1[r - 2]
            pivot = centre - d * upper2[r - 2] - a1 * upper1[r - 1]
            u1_top = e1 - a1 * upper2[r - 1]
        inverse = 1.0 / pivot
        upper1.append(u1_top * inverse)
        upper2.append(d * inverse)
        now = []
        for k in range(FIELDS + 2):
            if k < FIELDS:
                value = weight * load(cells, k, r)
            elif r == 0:
                now.append((d if k == FIELDS else a1) * inverse)
                continue
            elif r == 1 and k == FIELDS + 1:
                value = d
            else:
                value = None
            if r >= 1:
                term = a1 * fields1[k]
                value = -term if value is None else value - term
            if r >= 2:
                value = value - d * fields2[k]
            now.append(value * inverse)
        for k in range(FIELDS + 2):
            solved[r, k, at, :] = now[k]
        fields2, fields1 = fields1, now

    later1 = later2 = None
    for r in range(ROWS - 1, -1, -1):
        now = []
        for k in range(COLS):
            if k < FIELDS + 2:
                value = solved[r, k, at, :]
            elif r == ROWS - 1:
                value = upper1[r] if k == FIELDS + 2 else upper2[r]
            elif r == ROWS - 2 and k == FIELDS + 2:
                value = upper2[r]
            else:
                value = None
            if r < ROWS - 1:
                term = upper1[r] * later1[k]
                value = -term if value is None else value - term
            if r < ROWS - 2:
                value = value - upper2[r] * later2[k]
            now.append(value)
        for k in range(COLS):
            solved[r, k, at, :] = now[k]
        if r in TIP_ROW:
            for k in range(COLS):
                tips[pl.ds(part * 8 * TIPS + TIP_ROW[r] * COLS + k, 8, stride=TIPS), :] = now[k]
        later2, later1 = later1, now


def merge(left, right):
    def pair(matrix, columns):
        return [matrix[i][0] * columns[0] + matrix[i][1] * columns[1] for i in range(2)]

    gs = slice(0, FIELDS)
    ws = slice(FIELDS, FIELDS + 2)
    vs = slice(FIELDS + 2, FIELDS + 4)
    left_v = [[left[i][FIELDS + 2 + m] for m in range(2)] for i in range(4)]
    right_w = [[right[i][FIELDS + m] for m in range(2)] for i in range(4)]
    nothing = jnp.zeros((2,) + left[0].shape[1:], jnp.float32)
    product = [
        [sum(right_w[i][m] * left_v[2 + m][j] for m in range(2)) for j in range(2)]
        for i in range(2)
    ]
    m00, m01 = 1.0 - product[0][0], -product[0][1]
    m10, m11 = -product[1][0], 1.0 - product[1][1]
    scale = 1.0 / (m00 * m11 - m01 * m10)
    inverse = [[m11 * scale, -m01 * scale], [-m10 * scale, m00 * scale]]
    known = [jnp.concatenate([left[2 + i][gs], left[2 + i][ws]], axis=0) for i in range(2)]
    through = pair(right_w[:2], known)
    raw = [
        jnp.concatenate(
            [right[i][gs] - through[i][gs], -through[i][FIELDS:], right[i][vs]], axis=0
        )
        for i in range(2)
    ]
    inner_a = pair(inverse, raw)
    from_a = pair(left_v[2:], inner_a)
    inner_b = [
        jnp.concatenate([left[2 + i][gs], left[2 + i][ws], nothing], axis=0) - from_a[i]
        for i in range(2)
    ]
    from_a = pair(left_v[:2], inner_a)
    outer_a = [
        jnp.concatenate([left[i][gs], left[i][ws], nothing], axis=0) - from_a[i] for i in range(2)
    ]
    from_b = pair(right_w[2:], inner_b)
    outer_b = [
        jnp.concatenate([right[2 + i][gs], nothing, right[2 + i][vs]], axis=0) - from_b[i]
        for i in range(2)
    ]
    return outer_a + outer_b


def close(block):
    matrix = []
    for i in range(4):
        line = [block[i][FIELDS + 2], block[i][FIELDS + 3], block[i][FIELDS], block[i][FIELDS + 1]]
        line[i] = 1.0 + line[i]
        matrix.append(line)
    values = [block[i][0:FIELDS] for i in range(4)]
    for p in range(4):
        scale = 1.0 / matrix[p][p]
        for c in range(p + 1, 4):
            matrix[p][c] = matrix[p][c] * scale
        values[p] = values[p] * scale
        for r in range(p + 1, 4):
            for c in range(p + 1, 4):
                matrix[r][c] = matrix[r][c] - matrix[r][p] * matrix[p][c]
            values[r] = values[r] - matrix[r][p] * values[p]
    for r in range(2, -1, -1):
        for c in range(r + 1, 4):
            values[r] = values[r] - matrix[r][c] * values[c]
    return values


def exchange_kernel(
    azims,
    planes,
    destination_hbm,
    donor_hbm,
    receptor_hbm,
    offset_y_hbm,
    offset_x_hbm,
    fraction_y_hbm,
    fraction_x_hbm,
    state_hbm,
    speed_hbm,
    sigma_hbm,
    dissipation_hbm,
    packed_in,
    landing_in,
    update,
    destination,
    donor,
    receptor,
    offset_y,
    offset_x,
    fraction_y,
    fraction_x,
    entries,
    state,
    raw_coefs,
    cells,
    coefs,
    twice,
    packed,
    landing,
    solved,
    tips,
    tips_in,
    ping,
    pong,
    firsts,
    answers,
    borders,
    small_sem,
    large_sem,
    tile_send,
    tile_recv,
    land_send,
    land_recv,
    tips_send,
    tips_recv,
    back_send,
    back_recv,
    own_sem,
):
    a = lax.axis_index("azim")
    p = lax.axis_index("plane")
    per = CHUNKS // azims
    tip_rows = per * TIPS
    back_rows = per * BACK
    chips = planes // 2

    small = [
        pltpu.make_async_copy(source, dest, small_sem.at[i])
        for i, (source, dest) in enumerate(
            (
                (destination_hbm, destination),
                (donor_hbm, donor),
                (receptor_hbm, receptor),
                (offset_y_hbm, offset_y),
                (offset_x_hbm, offset_x),
                (fraction_y_hbm, fraction_y),
                (fraction_x_hbm, fraction_x),
            )
        )
    ]
    large = [
        pltpu.make_async_copy(source, dest, large_sem.at[i])
        for i, (source, dest) in enumerate(
            (
                (state_hbm, state),
                (speed_hbm, raw_coefs.at[0]),
                (sigma_hbm, raw_coefs.at[1]),
                (dissipation_hbm, raw_coefs.at[2]),
            )
        )
    ]
    for copy in small:
        copy.start()
    for copy in large:
        copy.start()

    barrier = pltpu.get_barrier_semaphore()
    for o in range(1, planes):
        pl.semaphore_signal(
            barrier, inc=1, device_id=(a, lax.rem(p + o, planes)), device_id_type=MESH
        )
    for o in range(1, azims):
        pl.semaphore_signal(
            barrier, inc=1, device_id=(lax.rem(a + o, azims), p), device_id_type=MESH
        )

    def to_azim(source, dest, rows, send, recv, o):
        there = lax.rem(a + o, azims)
        return pltpu.make_async_remote_copy(
            src_ref=source.at[pl.ds(pl.multiple_of(there * rows, 8), rows), :],
            dst_ref=dest.at[pl.ds(pl.multiple_of(a * rows, 8), rows), :],
            send_sem=send.at[o],
            recv_sem=recv.at[o],
            device_id=(there, p),
            device_id_type=MESH,
        )

    def own_azim(source, dest, rows, index):
        at = pl.ds(pl.multiple_of(a * rows, 8), rows)
        return pltpu.make_async_copy(source.at[at, :], dest.at[at, :], own_sem.at[index])

    def plane_peer(i):
        chip = lax.rem(p // 2 + chips - 1 - lax.rem(i, chips), chips)
        core = lax.rem(p + 1 - i // chips, 2)
        return chip * 2 + core

    def to_plane(i):
        there = plane_peer(i)
        return (
            pltpu.make_async_remote_copy(
                src_ref=packed.at[i],
                dst_ref=packed_in.at[p],
                send_sem=tile_send.at[i],
                recv_sem=tile_recv.at[i],
                device_id=(a, there),
                device_id_type=MESH,
            ),
            pltpu.make_async_remote_copy(
                src_ref=landing.at[i],
                dst_ref=landing_in.at[p],
                send_sem=land_send.at[i],
                recv_sem=land_recv.at[i],
                device_id=(a, there),
                device_id_type=MESH,
            ),
        )

    lane = lax.broadcasted_iota(jnp.int32, (CHUNKS, LANES), 1)
    column = lane & (TILE - 1)
    low_half = lane < TILE

    for copy in small:
        copy.wait()
    large[0].wait()
    spread(state, cells)
    pl.semaphore_wait(barrier, planes + azims - 2)

    def fill(i, carry):
        target = plane_peer(i)
        seen = jnp.int32(0)
        found = [jnp.int32(-1)] * CAP
        for e in range(SLOTS):
            match = destination[e] == target
            for k in range(CAP):
                found[k] = jnp.where(match & (seen == k), e, found[k])
            seen = seen + jnp.where(match, 1, 0)
        for k in range(CAP):
            entries[k] = found[k]

        def one_slot(k, inner_carry):
            entry = entries[k]
            e = jnp.maximum(entry, 0)
            place = jnp.where(entry >= 0, receptor[e], -1)
            landing[i, pl.ds(k, 1), :] = jnp.full((1, LANES), place, jnp.int32)
            row = donor[e]
            block = jnp.where(row >= 8, 1, 0)
            inner = row - 8 * block
            ox = offset_x[e]
            oy = offset_y[e]
            fx = fraction_x[e]
            fy = fraction_y[e]
            half = oy >> 1
            odd = (oy & 1) == 1
            even_first = jnp.where(odd, 0.0, 1.0 - fy)
            even_second = jnp.where(odd, fy, 0.0)
            odd_weight = jnp.where(odd, 1.0 - fy, fy)
            near = column + ox < TILE
            far = column + ox + 1 < TILE
            for f in range(FIELDS):
                tile = cells[f, block, pl.ds(inner, CHUNKS, stride=8), :]
                first = pltpu.roll(tile, LANES - ox, 1)
                second = pltpu.roll(tile, LANES - 1 - ox, 1)
                first = jnp.where(near, first, pltpu.roll(first, TILE, 1))
                second = jnp.where(far, second, pltpu.roll(second, TILE, 1))
                mixed = (1.0 - fx) * first + fx * second
                swapped = pltpu.roll(mixed, TILE, 1)
                twice[0, f, 0:CHUNKS, :] = mixed
                twice[0, f, CHUNKS : 2 * CHUNKS, :] = mixed
                twice[1, f, 0:CHUNKS, :] = swapped
                twice[1, f, CHUNKS : 2 * CHUNKS, :] = swapped
            for f in range(FIELDS):
                here = twice[0, f, pl.ds(half, CHUNKS), :]
                after = twice[0, f, pl.ds(half + 1, CHUNKS), :]
                odd_here = twice[1, f, pl.ds(half, CHUNKS), :]
                odd_after = twice[1, f, pl.ds(half + 1, CHUNKS), :]
                packed[i, k, f] = (
                    even_first * here
                    + even_second * after
                    + odd_weight * jnp.where(low_half, odd_here, odd_after)
                )
            return inner_carry

        lax.fori_loop(0, CAP, one_slot, 0)

        @pl.when(i < planes - 1)
        def _():
            for copy in to_plane(i):
                copy.start()

        return carry

    landing[...] = jnp.full(landing.shape, -1, jnp.int32)
    lax.fori_loop(0, planes, fill, 0)
    own_tiles = pltpu.make_async_copy(packed.at[planes - 1], packed_in.at[p], own_sem.at[2])
    own_land = pltpu.make_async_copy(landing.at[planes - 1], landing_in.at[p], own_sem.at[3])
    own_tiles.start()
    own_land.start()

    for copy in large[1:]:
        copy.wait()
    spread(raw_coefs, coefs)

    def one_part(part, carry):
        eliminate(cells, coefs, solved, tips, part)
        return carry

    lax.fori_loop(0, CHUNKS // 8, one_part, 0)

    tip_copies = [to_azim(tips, tips_in, tip_rows, tips_send, tips_recv, o) for o in range(1, azims)]
    for copy in tip_copies:
        copy.start()
    own_tips = own_azim(tips, tips_in, tip_rows, 0)
    own_tips.start()
    own_tips.wait()
    for copy in tip_copies:
        copy.wait()

    for v in range(TIPS):
        value = tips_in[pl.ds(v, CHUNKS, stride=TIPS), :]
        ping[v, 0:CHUNKS, :] = value
        ping[v, CHUNKS : 2 * CHUNKS, :] = value

    source, dest = ping, pong
    step = 1
    while step < azims:

        def level(part, carry, source=source, dest=dest, shift=step * per):
            row = pl.multiple_of(part * 8, 8)
            left = [source[COLS * i : COLS * (i + 1), pl.ds(row, 8), :] for i in range(4)]
            right = [source[COLS * i : COLS * (i + 1), pl.ds(row + shift, 8), :] for i in range(4)]
            for i, value in enumerate(merge(left, right)):
                dest[COLS * i : COLS * (i + 1), pl.ds(row, 8), :] = value
                dest[COLS * i : COLS * (i + 1), pl.ds(row + CHUNKS, 8), :] = value
            return carry

        lax.fori_loop(0, CHUNKS // 8, level, 0)
        source, dest = dest, source
        step *= 2

    def last(part, carry):
        row = pl.multiple_of(part * 8, 8)
        block = [source[COLS * i : COLS * (i + 1), pl.ds(row, 8), :] for i in range(4)]
        values = close(block)
        for i in range(2):
            firsts[FIELDS * i : FIELDS * (i + 1), pl.ds(row, 8), :] = values[i]
            firsts[FIELDS * i : FIELDS * (i + 1), pl.ds(row + CHUNKS, 8), :] = values[i]
            for f in range(FIELDS):
                answers[pl.ds(part * 8 * BACK + i * FIELDS + f, 8, stride=BACK), :] = values[2 + i][f]
        return carry

    lax.fori_loop(0, CHUNKS // 8, last, 0)
    for v in range(2 * FIELDS):
        answers[pl.ds(2 * FIELDS + v, CHUNKS, stride=BACK), :] = firsts[v, per : per + CHUNKS, :]

    back_copies = [
        to_azim(answers, borders, back_rows, back_send, back_recv, o) for o in range(1, azims)
    ]
    for copy in back_copies:
        copy.start()
    own_back = own_azim(answers, borders, back_rows, 1)
    own_back.start()
    own_back.wait()
    for copy in back_copies:
        copy.wait()

    def compose(part, carry):
        at = pl.ds(pl.multiple_of(part * 8, 8), 8)

        def border(i, f):
            return borders[pl.ds(part * 8 * BACK + i * FIELDS + f, 8, stride=BACK), :]

        for f in range(FIELDS):
            outside = [border(i, f) for i in range(4)]
            for r in range(ROWS):
                value = solved[r, f, at, :]
                for i in range(4):
                    value = value - solved[r, FIELDS + i, at, :] * outside[i]
                cells[f, r // 8, pl.ds(part * 64 + r % 8, 8, stride=8), :] = value
        return carry

    lax.fori_loop(0, CHUNKS // 8, compose, 0)

    def move(c, carry):
        at = pl.ds(pl.multiple_of(c * LANES, LANES), LANES)
        row = pl.multiple_of(c * 8, 8)
        for f in range(FIELDS):
            update[f, 0:8, at] = cells[f, 0, pl.ds(row, 8), :] - state[f, 0:8, at]
            update[f, 8:12, at] = cells[f, 1, pl.ds(row, 4), :] - state[f, 8:12, at]
        return carry

    lax.fori_loop(0, CHUNKS, move, 0, unroll=4)

    own_tiles.wait()
    own_land.wait()

    def settle(i, carry):
        for copy in to_plane(i):
            copy.wait()
        return carry

    lax.fori_loop(0, planes - 1, settle, 0)


def finish_kernel(landing, packed, update, state, fringe, out_hbm, out, rows, cells, total, places, counts, sems):
    planes = landing.shape[0]
    fetch = pltpu.make_async_copy(landing, places, sems.at[FIELDS])
    fetch.start()
    for r in range(ROWS):
        counts[r] = 0.0
    total[...] = jnp.zeros(total.shape, jnp.float32)
    fetch.wait()

    def add(slot, carry):
        d = slot // CAP
        k = slot - d * CAP
        row = places[d, k, 0]

        @pl.when(row >= 0)
        def _():
            total[row] = total[row] + packed[d, k]
            counts[row] = counts[row] + 1.0

        return carry

    lax.fori_loop(0, planes * CAP, add, 0)

    for b in range(2):
        line = lax.broadcasted_iota(jnp.int32, (8, LANES), 0) + 8 * b
        number = jnp.zeros((8, LANES), jnp.float32)
        for r in range(8 * b, min(8 * b + 8, ROWS)):
            number = jnp.where(line == r, counts[r], number)
        rows[2 * b] = number
        rows[2 * b + 1] = 1.0 / (number + 1.0)

    copies = []
    for f in range(FIELDS):
        for r in range(ROWS):
            cells[r // 8, pl.ds(r % 8, CHUNKS, stride=8), :] = total[r, f]

        def move(c, carry, f=f):
            at = pl.ds(pl.multiple_of(c * LANES, LANES), LANES)
            row = pl.multiple_of(c * 8, 8)
            for b, (low, high) in enumerate(((0, 8), (8, ROWS))):
                size = high - low
                q = state[f, low:high, at]
                relaxed = (cells[b, pl.ds(row, size), :] - rows[2 * b, 0:size, :] * q) * rows[
                    2 * b + 1, 0:size, :
                ]
                out[f, low:high, at] = jnp.where(
                    fringe[low:high, at] == 1, relaxed, update[f, low:high, at]
                )
            return carry

        lax.fori_loop(0, CHUNKS, move, 0, unroll=4)
        copy = pltpu.make_async_copy(out.at[f], out_hbm.at[f], sems.at[f])
        copy.start()
        copies.append(copy)
    for copy in copies:
        copy.wait()


def f32(*shape):
    return jax.ShapeDtypeStruct(shape, jnp.float32)


def local(
    state,
    speed,
    sigma,
    dissipation,
    fringe,
    destination,
    donor,
    receptor,
    offset_y,
    offset_x,
    fraction_y,
    fraction_x,
):
    azims = lax.axis_size("azim")
    planes = lax.axis_size("plane")
    vmem = pl.BlockSpec(memory_space=pltpu.VMEM)
    hbm = pl.BlockSpec(memory_space=pltpu.HBM)
    number = pltpu.VMEM
    packed_in, landing_in, update = pl.pallas_call(
        functools.partial(exchange_kernel, azims, planes),
        out_shape=(
            f32(planes, CAP, FIELDS, CHUNKS, LANES),
            jax.ShapeDtypeStruct((planes, 8, LANES), jnp.int32),
            f32(FIELDS, ROWS, CELLS),
        ),
        in_specs=[hbm] * 11,
        out_specs=(vmem,) * 3,
        scratch_shapes=[pltpu.SMEM((SLOTS,), jnp.int32)] * 5
        + [pltpu.SMEM((SLOTS,), jnp.float32)] * 2
        + [
            pltpu.SMEM((CAP,), jnp.int32),
            number((FIELDS, ROWS, CELLS), jnp.float32),
            number((3, ROWS, CELLS), jnp.float32),
            number((FIELDS, 2, CHUNKS * 8, LANES), jnp.float32),
            number((3, 2, CHUNKS * 8, LANES), jnp.float32),
            number((2, FIELDS, 2 * CHUNKS, LANES), jnp.float32),
            number((planes, CAP, FIELDS, CHUNKS, LANES), jnp.float32),
            number((planes, 8, LANES), jnp.int32),
            number((ROWS, COLS, CHUNKS, LANES), jnp.float32),
            number((CHUNKS * TIPS, LANES), jnp.float32),
            number((CHUNKS * TIPS, LANES), jnp.float32),
            number((TIPS, 2 * CHUNKS, LANES), jnp.float32),
            number((TIPS, 2 * CHUNKS, LANES), jnp.float32),
            number((2 * FIELDS, 2 * CHUNKS, LANES), jnp.float32),
            number((CHUNKS * BACK, LANES), jnp.float32),
            number((CHUNKS * BACK, LANES), jnp.float32),
            pltpu.SemaphoreType.DMA((7,)),
            pltpu.SemaphoreType.DMA((4,)),
            pltpu.SemaphoreType.DMA((planes,)),
            pltpu.SemaphoreType.DMA((planes,)),
            pltpu.SemaphoreType.DMA((planes,)),
            pltpu.SemaphoreType.DMA((planes,)),
            pltpu.SemaphoreType.DMA((azims,)),
            pltpu.SemaphoreType.DMA((azims,)),
            pltpu.SemaphoreType.DMA((azims,)),
            pltpu.SemaphoreType.DMA((azims,)),
            pltpu.SemaphoreType.DMA((4,)),
        ],
        compiler_params=pltpu.CompilerParams(
            collective_id=0, has_side_effects=True, vmem_limit_bytes=40 * 2**20
        ),
        name="exchange",
    )(
        *(
            pltpu.with_memory_space_constraint(value, pltpu.HBM)
            for value in (
                destination.reshape(SLOTS),
                donor,
                receptor,
                offset_y,
                offset_x,
                fraction_y,
                fraction_x,
                state,
                speed,
                sigma,
                dissipation,
            )
        )
    )
    return pl.pallas_call(
        finish_kernel,
        out_shape=f32(FIELDS, ROWS, CELLS),
        in_specs=[vmem] * 5,
        out_specs=hbm,
        scratch_shapes=[
            number((FIELDS, ROWS, CELLS), jnp.float32),
            number((4, 8, LANES), jnp.float32),
            number((2, CHUNKS * 8, LANES), jnp.float32),
            number((ROWS, FIELDS, CHUNKS, LANES), jnp.float32),
            pltpu.SMEM((planes, 8, LANES), jnp.int32),
            pltpu.SMEM((ROWS,), jnp.float32),
            pltpu.SemaphoreType.DMA((FIELDS + 1,)),
        ],
        compiler_params=pltpu.CompilerParams(vmem_limit_bytes=32 * 2**20),
        name="finish",
    )(landing_in, packed_in, update, state, fringe)


def solution(mesh):
    in_specs = (
        P(None, "azim", "plane"),
        P("azim", "plane"),
        P("azim", "plane"),
        P("azim", "plane"),
        P("azim", "plane"),
        P(("azim", "plane"), None),
        P(("azim", "plane")),
        P(("azim", "plane")),
        P(("azim", "plane")),
        P(("azim", "plane")),
        P(("azim", "plane")),
        P(("azim", "plane")),
    )
    out_specs = P(None, "azim", "plane")
    return jax.shard_map(local, mesh=mesh, in_specs=in_specs, out_specs=out_specs, check_vma=False)
```

```python
import functools

import jax
import jax.numpy as jnp
from jax import lax
from jax.experimental import pallas as pl
from jax.experimental.pallas import tpu as pltpu
from jax.sharding import PartitionSpec as P

TILE = 64
CAP = 4
FIELDS = 5
ROWS = 12
CELLS = TILE * TILE
LANES = 128
CHUNKS = CELLS // LANES
SLOTS = 16
COLS = FIELDS + 4
TIPS = 4 * COLS
BACK = 4 * FIELDS
MESH = pl.DeviceIdType.MESH
TIP_ROW = {0: 0, 1: 1, ROWS - 2: 2, ROWS - 1: 3}


def spread(source, dest):
    def move(c, carry):
        lane = pl.multiple_of(c * LANES, LANES)
        row = pl.multiple_of(c * 8, 8)
        for f in range(source.shape[0]):
            dest[f, 0, pl.ds(row, 8), :] = source[f, 0:8, pl.ds(lane, LANES)]
            dest[f, 1, pl.ds(row, 4), :] = source[f, 8:12, pl.ds(lane, LANES)]
        return carry

    lax.fori_loop(0, CHUNKS, move, 0, unroll=4)


def eliminate(cells, coefs, solved, tips, part):
    base = part * 64
    at = pl.ds(pl.multiple_of(part * 8, 8), 8)

    def load(ref, lead, r):
        return ref[lead, r // 8, pl.ds(base + r % 8, 8, stride=8), :]

    upper1 = []
    upper2 = []
    fields1 = fields2 = None
    for r in range(ROWS):
        c = load(coefs, 0, r)
        s = load(coefs, 1, r)
        d = load(coefs, 2, r)
        half = 0.5 * c
        common = -s - 4.0 * d
        a1 = common - half
        e1 = common + half
        centre = 1.0 + (2.0 * s + 10.0 * d)
        weight = 1.0 + 4.0 * d
        if r == 0:
            pivot, u1_top = centre, e1
        elif r == 1:
            pivot = centre - a1 * upper1[0]
            u1_top = e1 - a1 * upper2[0]
        else:
            a1 = a1 - d * upper1[r - 2]
            pivot = centre - d * upper2[r - 2] - a1 * upper1[r - 1]
            u1_top = e1 - a1 * upper2[r - 1]
        inverse = 1.0 / pivot
        upper1.append(u1_top * inverse)
        upper2.append(d * inverse)
        now = []
        for k in range(FIELDS + 2):
            if k < FIELDS:
                value = weight * load(cells, k, r)
            elif r == 0:
                now.append((d if k == FIELDS else a1) * inverse)
                continue
            elif r == 1 and k == FIELDS + 1:
                value = d
            else:
                value = None
            if r >= 1:
                term = a1 * fields1[k]
                value = -term if value is None else value - term
            if r >= 2:
                value = value - d * fields2[k]
            now.append(value * inverse)
        for k in range(FIELDS + 2):
            solved[r, k, at, :] = now[k]
        fields2, fields1 = fields1, now

    later1 = later2 = None
    for r in range(ROWS - 1, -1, -1):
        now = []
        for k in range(COLS):
            if k < FIELDS + 2:
                value = solved[r, k, at, :]
            elif r == ROWS - 1:
                value = upper1[r] if k == FIELDS + 2 else upper2[r]
            elif r == ROWS - 2 and k == FIELDS + 2:
                value = upper2[r]
            else:
                value = None
            if r < ROWS - 1:
                term = upper1[r] * later1[k]
                value = -term if value is None else value - term
            if r < ROWS - 2:
                value = value - upper2[r] * later2[k]
            now.append(value)
        for k in range(COLS):
            solved[r, k, at, :] = now[k]
        if r in TIP_ROW:
            for k in range(COLS):
                tips[pl.ds(part * 8 * TIPS + TIP_ROW[r] * COLS + k, 8, stride=TIPS), :] = now[k]
        later2, later1 = later1, now


def merge(left, right):
    def pair(matrix, columns):
        return [matrix[i][0] * columns[0] + matrix[i][1] * columns[1] for i in range(2)]

    gs = slice(0, FIELDS)
    ws = slice(FIELDS, FIELDS + 2)
    vs = slice(FIELDS + 2, FIELDS + 4)
    left_v = [[left[i][FIELDS + 2 + m] for m in range(2)] for i in range(4)]
    right_w = [[right[i][FIELDS + m] for m in range(2)] for i in range(4)]
    nothing = jnp.zeros((2,) + left[0].shape[1:], jnp.float32)
    product = [
        [sum(right_w[i][m] * left_v[2 + m][j] for m in range(2)) for j in range(2)]
        for i in range(2)
    ]
    m00, m01 = 1.0 - product[0][0], -product[0][1]
    m10, m11 = -product[1][0], 1.0 - product[1][1]
    scale = 1.0 / (m00 * m11 - m01 * m10)
    inverse = [[m11 * scale, -m01 * scale], [-m10 * scale, m00 * scale]]
    known = [jnp.concatenate([left[2 + i][gs], left[2 + i][ws]], axis=0) for i in range(2)]
    through = pair(right_w[:2], known)
    raw = [
        jnp.concatenate(
            [right[i][gs] - through[i][gs], -through[i][FIELDS:], right[i][vs]], axis=0
        )
        for i in range(2)
    ]
    inner_a = pair(inverse, raw)
    from_a = pair(left_v[2:], inner_a)
    inner_b = [
        jnp.concatenate([left[2 + i][gs], left[2 + i][ws], nothing], axis=0) - from_a[i]
        for i in range(2)
    ]
    from_a = pair(left_v[:2], inner_a)
    outer_a = [
        jnp.concatenate([left[i][gs], left[i][ws], nothing], axis=0) - from_a[i] for i in range(2)
    ]
    from_b = pair(right_w[2:], inner_b)
    outer_b = [
        jnp.concatenate([right[2 + i][gs], nothing, right[2 + i][vs]], axis=0) - from_b[i]
        for i in range(2)
    ]
    return outer_a + outer_b


def close(block):
    matrix = []
    for i in range(4):
        line = [block[i][FIELDS + 2], block[i][FIELDS + 3], block[i][FIELDS], block[i][FIELDS + 1]]
        line[i] = 1.0 + line[i]
        matrix.append(line)
    values = [block[i][0:FIELDS] for i in range(4)]
    for p in range(4):
        scale = 1.0 / matrix[p][p]
        for c in range(p + 1, 4):
            matrix[p][c] = matrix[p][c] * scale
        values[p] = values[p] * scale
        for r in range(p + 1, 4):
            for c in range(p + 1, 4):
                matrix[r][c] = matrix[r][c] - matrix[r][p] * matrix[p][c]
            values[r] = values[r] - matrix[r][p] * values[p]
    for r in range(2, -1, -1):
        for c in range(r + 1, 4):
            values[r] = values[r] - matrix[r][c] * values[c]
    return values


def exchange_kernel(
    azims,
    planes,
    destination_hbm,
    donor_hbm,
    receptor_hbm,
    offset_y_hbm,
    offset_x_hbm,
    fraction_y_hbm,
    fraction_x_hbm,
    state_hbm,
    speed_hbm,
    sigma_hbm,
    dissipation_hbm,
    packed_in,
    landing_in,
    update,
    destination,
    donor,
    receptor,
    offset_y,
    offset_x,
    fraction_y,
    fraction_x,
    entries,
    state,
    raw_coefs,
    cells,
    coefs,
    twice,
    packed,
    landing,
    solved,
    tips,
    tips_in,
    ping,
    pong,
    firsts,
    answers,
    borders,
    small_sem,
    large_sem,
    tile_send,
    tile_recv,
    land_send,
    land_recv,
    tips_send,
    tips_recv,
    back_send,
    back_recv,
    own_sem,
    ready,
    go,
):
    a = lax.axis_index("azim")
    p = lax.axis_index("plane")
    per = CHUNKS // azims
    tip_rows = per * TIPS
    back_rows = per * BACK
    chips = planes // 2

    small = [
        pltpu.make_async_copy(source, dest, small_sem.at[i])
        for i, (source, dest) in enumerate(
            (
                (destination_hbm, destination),
                (donor_hbm, donor),
                (receptor_hbm, receptor),
                (offset_y_hbm, offset_y),
                (offset_x_hbm, offset_x),
                (fraction_y_hbm, fraction_y),
                (fraction_x_hbm, fraction_x),
            )
        )
    ]
    large = [
        pltpu.make_async_copy(source, dest, large_sem.at[i])
        for i, (source, dest) in enumerate(
            (
                (state_hbm, state),
                (speed_hbm, raw_coefs.at[0]),
                (sigma_hbm, raw_coefs.at[1]),
                (dissipation_hbm, raw_coefs.at[2]),
            )
        )
    ]
    for copy in small:
        copy.start()
    for copy in large:
        copy.start()

    barrier = pltpu.get_barrier_semaphore()
    for o in range(1, planes):
        there = lax.rem(p + o, planes)

        @pl.when(there != 0)
        def _():
            pl.semaphore_signal(barrier, inc=1, device_id=(a, there), device_id_type=MESH)

    def to_azim(source, dest, rows, send, recv, o):
        there = lax.rem(a + o, azims)
        return pltpu.make_async_remote_copy(
            src_ref=source.at[pl.ds(pl.multiple_of(there * rows, 8), rows), :],
            dst_ref=dest.at[pl.ds(pl.multiple_of(a * rows, 8), rows), :],
            send_sem=send.at[o],
            recv_sem=recv.at[o],
            device_id=(there, p),
            device_id_type=MESH,
        )

    def own_azim(source, dest, rows, index):
        at = pl.ds(pl.multiple_of(a * rows, 8), rows)
        return pltpu.make_async_copy(source.at[at, :], dest.at[at, :], own_sem.at[index])

    def plane_peer(i):
        chip = lax.rem(p // 2 + chips - 1 - lax.rem(i, chips), chips)
        core = lax.rem(p + 1 - i // chips, 2)
        return chip * 2 + core

    def to_plane(i):
        there = plane_peer(i)
        return (
            pltpu.make_async_remote_copy(
                src_ref=packed.at[i],
                dst_ref=packed_in.at[p],
                send_sem=tile_send.at[i],
                recv_sem=tile_recv.at[i],
                device_id=(a, there),
                device_id_type=MESH,
            ),
            pltpu.make_async_remote_copy(
                src_ref=landing.at[i],
                dst_ref=landing_in.at[p],
                send_sem=land_send.at[i],
                recv_sem=land_recv.at[i],
                device_id=(a, there),
                device_id_type=MESH,
            ),
        )

    lane = lax.broadcasted_iota(jnp.int32, (CHUNKS, LANES), 1)
    column = lane & (TILE - 1)
    low_half = lane < TILE

    for copy in small:
        copy.wait()
    large[0].wait()
    spread(state, cells)

    @pl.when(p != 0)
    def _():
        pl.semaphore_wait(barrier, planes - 1)
        pl.semaphore_signal(ready, inc=1, device_id=(a, 0), device_id_type=MESH)

    @pl.when(p == 0)
    def _():
        pl.semaphore_wait(ready, planes - 1)
        for o in range(1, azims):
            pl.semaphore_signal(
                barrier, inc=1, device_id=(lax.rem(a + o, azims), p), device_id_type=MESH
            )


    def fill(i, carry):
        target = plane_peer(i)
        seen = jnp.int32(0)
        found = [jnp.int32(-1)] * CAP
        for e in range(SLOTS):
            match = destination[e] == target
            for k in range(CAP):
                found[k] = jnp.where(match & (seen == k), e, found[k])
            seen = seen + jnp.where(match, 1, 0)
        for k in range(CAP):
            entries[k] = found[k]

        def one_slot(k, inner_carry):
            entry = entries[k]
            e = jnp.maximum(entry, 0)
            place = jnp.where(entry >= 0, receptor[e], -1)
            landing[i, pl.ds(k, 1), :] = jnp.full((1, LANES), place, jnp.int32)
            row = donor[e]
            block = jnp.where(row >= 8, 1, 0)
            inner = row - 8 * block
            ox = offset_x[e]
            oy = offset_y[e]
            fx = fraction_x[e]
            fy = fraction_y[e]
            half = oy >> 1
            odd = (oy & 1) == 1
            even_first = jnp.where(odd, 0.0, 1.0 - fy)
            even_second = jnp.where(odd, fy, 0.0)
            odd_weight = jnp.where(odd, 1.0 - fy, fy)
            near = column + ox < TILE
            far = column + ox + 1 < TILE
            for f in range(FIELDS):
                tile = cells[f, block, pl.ds(inner, CHUNKS, stride=8), :]
                first = pltpu.roll(tile, LANES - ox, 1)
                second = pltpu.roll(tile, LANES - 1 - ox, 1)
                first = jnp.where(near, first, pltpu.roll(first, TILE, 1))
                second = jnp.where(far, second, pltpu.roll(second, TILE, 1))
                mixed = (1.0 - fx) * first + fx * second
                swapped = pltpu.roll(mixed, TILE, 1)
                twice[0, f, 0:CHUNKS, :] = mixed
                twice[0, f, CHUNKS : 2 * CHUNKS, :] = mixed
                twice[1, f, 0:CHUNKS, :] = swapped
                twice[1, f, CHUNKS : 2 * CHUNKS, :] = swapped
            for f in range(FIELDS):
                here = twice[0, f, pl.ds(half, CHUNKS), :]
                after = twice[0, f, pl.ds(half + 1, CHUNKS), :]
                odd_here = twice[1, f, pl.ds(half, CHUNKS), :]
                odd_after = twice[1, f, pl.ds(half + 1, CHUNKS), :]
                packed[i, k, f] = (
                    even_first * here
                    + even_second * after
                    + odd_weight * jnp.where(low_half, odd_here, odd_after)
                )
            return inner_carry

        lax.fori_loop(0, CAP, one_slot, 0)

        @pl.when(i < planes - 1)
        def _():
            for copy in to_plane(i):
                copy.start()

        return carry

    landing[...] = jnp.full(landing.shape, -1, jnp.int32)
    lax.fori_loop(0, planes, fill, 0)
    own_tiles = pltpu.make_async_copy(packed.at[planes - 1], packed_in.at[p], own_sem.at[2])
    own_land = pltpu.make_async_copy(landing.at[planes - 1], landing_in.at[p], own_sem.at[3])
    own_tiles.start()
    own_land.start()

    for copy in large[1:]:
        copy.wait()
    spread(raw_coefs, coefs)

    def one_part(part, carry):
        eliminate(cells, coefs, solved, tips, part)
        return carry

    lax.fori_loop(0, CHUNKS // 8, one_part, 0)

    @pl.when(p == 0)
    def _():
        pl.semaphore_wait(barrier, azims - 1)
        for o in range(1, planes):
            pl.semaphore_signal(go, inc=1, device_id=(a, o), device_id_type=MESH)

    @pl.when(p != 0)
    def _():
        pl.semaphore_wait(go, 1)

    tip_copies = [to_azim(tips, tips_in, tip_rows, tips_send, tips_recv, o) for o in range(1, azims)]
    for copy in tip_copies:
        copy.start()
    own_tips = own_azim(tips, tips_in, tip_rows, 0)
    own_tips.start()
    own_tips.wait()
    for copy in tip_copies:
        copy.wait()

    for v in range(TIPS):
        value = tips_in[pl.ds(v, CHUNKS, stride=TIPS), :]
        ping[v, 0:CHUNKS, :] = value
        ping[v, CHUNKS : 2 * CHUNKS, :] = value

    source, dest = ping, pong
    step = 1
    while step < azims:

        def level(part, carry, source=source, dest=dest, shift=step * per):
            row = pl.multiple_of(part * 8, 8)
            left = [source[COLS * i : COLS * (i + 1), pl.ds(row, 8), :] for i in range(4)]
            right = [source[COLS * i : COLS * (i + 1), pl.ds(row + shift, 8), :] for i in range(4)]
            for i, value in enumerate(merge(left, right)):
                dest[COLS * i : COLS * (i + 1), pl.ds(row, 8), :] = value
                dest[COLS * i : COLS * (i + 1), pl.ds(row + CHUNKS, 8), :] = value
            return carry

        lax.fori_loop(0, CHUNKS // 8, level, 0)
        source, dest = dest, source
        step *= 2

    def last(part, carry):
        row = pl.multiple_of(part * 8, 8)
        block = [source[COLS * i : COLS * (i + 1), pl.ds(row, 8), :] for i in range(4)]
        values = close(block)
        for i in range(2):
            firsts[FIELDS * i : FIELDS * (i + 1), pl.ds(row, 8), :] = values[i]
            firsts[FIELDS * i : FIELDS * (i + 1), pl.ds(row + CHUNKS, 8), :] = values[i]
            for f in range(FIELDS):
                answers[pl.ds(part * 8 * BACK + i * FIELDS + f, 8, stride=BACK), :] = values[2 + i][f]
        return carry

    lax.fori_loop(0, CHUNKS // 8, last, 0)
    for v in range(2 * FIELDS):
        answers[pl.ds(2 * FIELDS + v, CHUNKS, stride=BACK), :] = firsts[v, per : per + CHUNKS, :]

    back_copies = [
        to_azim(answers, borders, back_rows, back_send, back_recv, o) for o in range(1, azims)
    ]
    for copy in back_copies:
        copy.start()
    own_back = own_azim(answers, borders, back_rows, 1)
    own_back.start()
    own_back.wait()
    for copy in back_copies:
        copy.wait()

    def compose(part, carry):
        at = pl.ds(pl.multiple_of(part * 8, 8), 8)

        def border(i, f):
            return borders[pl.ds(part * 8 * BACK + i * FIELDS + f, 8, stride=BACK), :]

        for f in range(FIELDS):
            outside = [border(i, f) for i in range(4)]
            for r in range(ROWS):
                value = solved[r, f, at, :]
                for i in range(4):
                    value = value - solved[r, FIELDS + i, at, :] * outside[i]
                cells[f, r // 8, pl.ds(part * 64 + r % 8, 8, stride=8), :] = value
        return carry

    lax.fori_loop(0, CHUNKS // 8, compose, 0)

    def move(c, carry):
        at = pl.ds(pl.multiple_of(c * LANES, LANES), LANES)
        row = pl.multiple_of(c * 8, 8)
        for f in range(FIELDS):
            update[f, 0:8, at] = cells[f, 0, pl.ds(row, 8), :] - state[f, 0:8, at]
            update[f, 8:12, at] = cells[f, 1, pl.ds(row, 4), :] - state[f, 8:12, at]
        return carry

    lax.fori_loop(0, CHUNKS, move, 0, unroll=4)

    own_tiles.wait()
    own_land.wait()

    def settle(i, carry):
        for copy in to_plane(i):
            copy.wait()
        return carry

    lax.fori_loop(0, planes - 1, settle, 0)


def finish_kernel(landing, packed, update, state, fringe, out_hbm, out, rows, cells, total, places, counts, sems):
    planes = landing.shape[0]
    fetch = pltpu.make_async_copy(landing, places, sems.at[FIELDS])
    fetch.start()
    for r in range(ROWS):
        counts[r] = 0.0
    total[...] = jnp.zeros(total.shape, jnp.float32)
    fetch.wait()

    def add(slot, carry):
        d = slot // CAP
        k = slot - d * CAP
        row = places[d, k, 0]

        @pl.when(row >= 0)
        def _():
            total[row] = total[row] + packed[d, k]
            counts[row] = counts[row] + 1.0

        return carry

    lax.fori_loop(0, planes * CAP, add, 0)

    for b in range(2):
        line = lax.broadcasted_iota(jnp.int32, (8, LANES), 0) + 8 * b
        number = jnp.zeros((8, LANES), jnp.float32)
        for r in range(8 * b, min(8 * b + 8, ROWS)):
            number = jnp.where(line == r, counts[r], number)
        rows[2 * b] = number
        rows[2 * b + 1] = 1.0 / (number + 1.0)

    copies = []
    for f in range(FIELDS):
        for r in range(ROWS):
            cells[r // 8, pl.ds(r % 8, CHUNKS, stride=8), :] = total[r, f]

        def move(c, carry, f=f):
            at = pl.ds(pl.multiple_of(c * LANES, LANES), LANES)
            row = pl.multiple_of(c * 8, 8)
            for b, (low, high) in enumerate(((0, 8), (8, ROWS))):
                size = high - low
                q = state[f, low:high, at]
                relaxed = (cells[b, pl.ds(row, size), :] - rows[2 * b, 0:size, :] * q) * rows[
                    2 * b + 1, 0:size, :
                ]
                out[f, low:high, at] = jnp.where(
                    fringe[low:high, at] == 1, relaxed, update[f, low:high, at]
                )
            return carry

        lax.fori_loop(0, CHUNKS, move, 0, unroll=4)
        copy = pltpu.make_async_copy(out.at[f], out_hbm.at[f], sems.at[f])
        copy.start()
        copies.append(copy)
    for copy in copies:
        copy.wait()


def f32(*shape):
    return jax.ShapeDtypeStruct(shape, jnp.float32)


def local(
    state,
    speed,
    sigma,
    dissipation,
    fringe,
    destination,
    donor,
    receptor,
    offset_y,
    offset_x,
    fraction_y,
    fraction_x,
):
    azims = lax.axis_size("azim")
    planes = lax.axis_size("plane")
    vmem = pl.BlockSpec(memory_space=pltpu.VMEM)
    hbm = pl.BlockSpec(memory_space=pltpu.HBM)
    number = pltpu.VMEM
    packed_in, landing_in, update = pl.pallas_call(
        functools.partial(exchange_kernel, azims, planes),
        out_shape=(
            f32(planes, CAP, FIELDS, CHUNKS, LANES),
            jax.ShapeDtypeStruct((planes, 8, LANES), jnp.int32),
            f32(FIELDS, ROWS, CELLS),
        ),
        in_specs=[hbm] * 11,
        out_specs=(vmem,) * 3,
        scratch_shapes=[pltpu.SMEM((SLOTS,), jnp.int32)] * 5
        + [pltpu.SMEM((SLOTS,), jnp.float32)] * 2
        + [
            pltpu.SMEM((CAP,), jnp.int32),
            number((FIELDS, ROWS, CELLS), jnp.float32),
            number((3, ROWS, CELLS), jnp.float32),
            number((FIELDS, 2, CHUNKS * 8, LANES), jnp.float32),
            number((3, 2, CHUNKS * 8, LANES), jnp.float32),
            number((2, FIELDS, 2 * CHUNKS, LANES), jnp.float32),
            number((planes, CAP, FIELDS, CHUNKS, LANES), jnp.float32),
            number((planes, 8, LANES), jnp.int32),
            number((ROWS, COLS, CHUNKS, LANES), jnp.float32),
            number((CHUNKS * TIPS, LANES), jnp.float32),
            number((CHUNKS * TIPS, LANES), jnp.float32),
            number((TIPS, 2 * CHUNKS, LANES), jnp.float32),
            number((TIPS, 2 * CHUNKS, LANES), jnp.float32),
            number((2 * FIELDS, 2 * CHUNKS, LANES), jnp.float32),
            number((CHUNKS * BACK, LANES), jnp.float32),
            number((CHUNKS * BACK, LANES), jnp.float32),
            pltpu.SemaphoreType.DMA((7,)),
            pltpu.SemaphoreType.DMA((4,)),
            pltpu.SemaphoreType.DMA((planes,)),
            pltpu.SemaphoreType.DMA((planes,)),
            pltpu.SemaphoreType.DMA((planes,)),
            pltpu.SemaphoreType.DMA((planes,)),
            pltpu.SemaphoreType.DMA((azims,)),
            pltpu.SemaphoreType.DMA((azims,)),
            pltpu.SemaphoreType.DMA((azims,)),
            pltpu.SemaphoreType.DMA((azims,)),
            pltpu.SemaphoreType.DMA((4,)),
            pltpu.SemaphoreType.REGULAR,
            pltpu.SemaphoreType.REGULAR,
        ],
        compiler_params=pltpu.CompilerParams(
            collective_id=0, has_side_effects=True, vmem_limit_bytes=40 * 2**20
        ),
        name="exchange",
    )(
        *(
            pltpu.with_memory_space_constraint(value, pltpu.HBM)
            for value in (
                destination.reshape(SLOTS),
                donor,
                receptor,
                offset_y,
                offset_x,
                fraction_y,
                fraction_x,
                state,
                speed,
                sigma,
                dissipation,
            )
        )
    )
    return pl.pallas_call(
        finish_kernel,
        out_shape=f32(FIELDS, ROWS, CELLS),
        in_specs=[vmem] * 5,
        out_specs=hbm,
        scratch_shapes=[
            number((FIELDS, ROWS, CELLS), jnp.float32),
            number((4, 8, LANES), jnp.float32),
            number((2, CHUNKS * 8, LANES), jnp.float32),
            number((ROWS, FIELDS, CHUNKS, LANES), jnp.float32),
            pltpu.SMEM((planes, 8, LANES), jnp.int32),
            pltpu.SMEM((ROWS,), jnp.float32),
            pltpu.SemaphoreType.DMA((FIELDS + 1,)),
        ],
        compiler_params=pltpu.CompilerParams(vmem_limit_bytes=32 * 2**20),
        name="finish",
    )(landing_in, packed_in, update, state, fringe)


def solution(mesh):
    in_specs = (
        P(None, "azim", "plane"),
        P("azim", "plane"),
        P("azim", "plane"),
        P("azim", "plane"),
        P("azim", "plane"),
        P(("azim", "plane"), None),
        P(("azim", "plane")),
        P(("azim", "plane")),
        P(("azim", "plane")),
        P(("azim", "plane")),
        P(("azim", "plane")),
        P(("azim", "plane")),
    )
    out_specs = P(None, "azim", "plane")
    return jax.shard_map(local, mesh=mesh, in_specs=in_specs, out_specs=out_specs, check_vma=False)
```

```python
import functools

import jax
import jax.numpy as jnp
from jax import lax
from jax.experimental import pallas as pl
from jax.experimental.pallas import tpu as pltpu
from jax.sharding import PartitionSpec as P

TILE = 64
CAP = 4
FIELDS = 5
ROWS = 12
CELLS = TILE * TILE
LANES = 128
CHUNKS = CELLS // LANES
SLOTS = 16
COLS = FIELDS + 4
TIPS = 4 * COLS
BACK = 4 * FIELDS
MESH = pl.DeviceIdType.MESH
TIP_ROW = {0: 0, 1: 1, ROWS - 2: 2, ROWS - 1: 3}


def spread(source, dest):
    def move(c, carry):
        lane = pl.multiple_of(c * LANES, LANES)
        row = pl.multiple_of(c * 8, 8)
        for f in range(source.shape[0]):
            dest[f, 0, pl.ds(row, 8), :] = source[f, 0:8, pl.ds(lane, LANES)]
            dest[f, 1, pl.ds(row, 4), :] = source[f, 8:12, pl.ds(lane, LANES)]
        return carry

    lax.fori_loop(0, CHUNKS, move, 0, unroll=4)


def spread_twice(source, dest):
    def move(c, carry):
        lane = pl.multiple_of(c * LANES, LANES)
        row = pl.multiple_of(c * 8, 8)
        upper = source[0:8, pl.ds(lane, LANES)]
        lower = source[8:12, pl.ds(lane, LANES)]
        for again in range(2):
            dest[0, pl.ds(row + again * CHUNKS * 8, 8), :] = upper
            dest[1, pl.ds(row + again * CHUNKS * 8, 4), :] = lower
        return carry

    lax.fori_loop(0, CHUNKS, move, 0, unroll=8)


def eliminate(cells, coefs, solved, tips, part):
    base = part * 64
    at = pl.ds(pl.multiple_of(part * 8, 8), 8)

    def load(ref, lead, r):
        return ref[lead, r // 8, pl.ds(base + r % 8, 8, stride=8), :]

    upper1 = []
    upper2 = []
    fields1 = fields2 = None
    for r in range(ROWS):
        c = load(coefs, 0, r)
        s = load(coefs, 1, r)
        d = load(coefs, 2, r)
        half = 0.5 * c
        common = -s - 4.0 * d
        a1 = common - half
        e1 = common + half
        centre = 1.0 + (2.0 * s + 10.0 * d)
        weight = 1.0 + 4.0 * d
        if r == 0:
            pivot, u1_top = centre, e1
        elif r == 1:
            pivot = centre - a1 * upper1[0]
            u1_top = e1 - a1 * upper2[0]
        else:
            a1 = a1 - d * upper1[r - 2]
            pivot = centre - d * upper2[r - 2] - a1 * upper1[r - 1]
            u1_top = e1 - a1 * upper2[r - 1]
        inverse = 1.0 / pivot
        upper1.append(u1_top * inverse)
        upper2.append(d * inverse)
        now = []
        for k in range(FIELDS + 2):
            if k < FIELDS:
                value = weight * load(cells, k, r)
            elif r == 0:
                now.append((d if k == FIELDS else a1) * inverse)
                continue
            elif r == 1 and k == FIELDS + 1:
                value = d
            else:
                value = None
            if r >= 1:
                term = a1 * fields1[k]
                value = -term if value is None else value - term
            if r >= 2:
                value = value - d * fields2[k]
            now.append(value * inverse)
        for k in range(FIELDS + 2):
            solved[r, k, at, :] = now[k]
        fields2, fields1 = fields1, now

    later1 = later2 = None
    for r in range(ROWS - 1, -1, -1):
        now = []
        for k in range(COLS):
            if k < FIELDS + 2:
                value = solved[r, k, at, :]
            elif r == ROWS - 1:
                value = upper1[r] if k == FIELDS + 2 else upper2[r]
            elif r == ROWS - 2 and k == FIELDS + 2:
                value = upper2[r]
            else:
                value = None
            if r < ROWS - 1:
                term = upper1[r] * later1[k]
                value = -term if value is None else value - term
            if r < ROWS - 2:
                value = value - upper2[r] * later2[k]
            now.append(value)
        for k in range(COLS):
            solved[r, k, at, :] = now[k]
        if r in TIP_ROW:
            for k in range(COLS):
                tips[pl.ds(part * 8 * TIPS + TIP_ROW[r] * COLS + k, 8, stride=TIPS), :] = now[k]
        later2, later1 = later1, now


def merge(left, right):
    def pair(matrix, columns):
        return [matrix[i][0] * columns[0] + matrix[i][1] * columns[1] for i in range(2)]

    gs = slice(0, FIELDS)
    ws = slice(FIELDS, FIELDS + 2)
    vs = slice(FIELDS + 2, FIELDS + 4)
    left_v = [[left[i][FIELDS + 2 + m] for m in range(2)] for i in range(4)]
    right_w = [[right[i][FIELDS + m] for m in range(2)] for i in range(4)]
    nothing = jnp.zeros((2,) + left[0].shape[1:], jnp.float32)
    product = [
        [sum(right_w[i][m] * left_v[2 + m][j] for m in range(2)) for j in range(2)]
        for i in range(2)
    ]
    m00, m01 = 1.0 - product[0][0], -product[0][1]
    m10, m11 = -product[1][0], 1.0 - product[1][1]
    scale = 1.0 / (m00 * m11 - m01 * m10)
    inverse = [[m11 * scale, -m01 * scale], [-m10 * scale, m00 * scale]]
    known = [jnp.concatenate([left[2 + i][gs], left[2 + i][ws]], axis=0) for i in range(2)]
    through = pair(right_w[:2], known)
    raw = [
        jnp.concatenate(
            [right[i][gs] - through[i][gs], -through[i][FIELDS:], right[i][vs]], axis=0
        )
        for i in range(2)
    ]
    inner_a = pair(inverse, raw)
    from_a = pair(left_v[2:], inner_a)
    inner_b = [
        jnp.concatenate([left[2 + i][gs], left[2 + i][ws], nothing], axis=0) - from_a[i]
        for i in range(2)
    ]
    from_a = pair(left_v[:2], inner_a)
    outer_a = [
        jnp.concatenate([left[i][gs], left[i][ws], nothing], axis=0) - from_a[i] for i in range(2)
    ]
    from_b = pair(right_w[2:], inner_b)
    outer_b = [
        jnp.concatenate([right[2 + i][gs], nothing, right[2 + i][vs]], axis=0) - from_b[i]
        for i in range(2)
    ]
    return outer_a + outer_b


def close(block):
    matrix = []
    for i in range(4):
        line = [block[i][FIELDS + 2], block[i][FIELDS + 3], block[i][FIELDS], block[i][FIELDS + 1]]
        line[i] = 1.0 + line[i]
        matrix.append(line)
    values = [block[i][0:FIELDS] for i in range(4)]
    for p in range(4):
        scale = 1.0 / matrix[p][p]
        for c in range(p + 1, 4):
            matrix[p][c] = matrix[p][c] * scale
        values[p] = values[p] * scale
        for r in range(p + 1, 4):
            for c in range(p + 1, 4):
                matrix[r][c] = matrix[r][c] - matrix[r][p] * matrix[p][c]
            values[r] = values[r] - matrix[r][p] * values[p]
    for r in range(2, -1, -1):
        for c in range(r + 1, 4):
            values[r] = values[r] - matrix[r][c] * values[c]
    return values


def exchange_kernel(
    azims,
    planes,
    destination_hbm,
    donor_hbm,
    receptor_hbm,
    offset_y_hbm,
    offset_x_hbm,
    fraction_y_hbm,
    fraction_x_hbm,
    state_hbm,
    speed_hbm,
    sigma_hbm,
    dissipation_hbm,
    packed_in,
    landing_in,
    update,
    destination,
    donor,
    receptor,
    offset_y,
    offset_x,
    fraction_y,
    fraction_x,
    entries,
    state,
    raw_coefs,
    cells,
    coefs,
    packed,
    landing,
    solved,
    tips,
    tips_in,
    ping,
    pong,
    firsts,
    answers,
    borders,
    small_sem,
    large_sem,
    tile_send,
    tile_recv,
    land_send,
    land_recv,
    tips_send,
    tips_recv,
    back_send,
    back_recv,
    own_sem,
    ready,
    beyond,
    go,
):
    a = lax.axis_index("azim")
    p = lax.axis_index("plane")
    per = CHUNKS // azims
    tip_rows = per * TIPS
    back_rows = per * BACK
    chips = planes // 2

    small = [
        pltpu.make_async_copy(source, dest, small_sem.at[i])
        for i, (source, dest) in enumerate(
            (
                (destination_hbm, destination),
                (donor_hbm, donor),
                (receptor_hbm, receptor),
                (offset_y_hbm, offset_y),
                (offset_x_hbm, offset_x),
                (fraction_y_hbm, fraction_y),
                (fraction_x_hbm, fraction_x),
            )
        )
    ]
    large = [
        pltpu.make_async_copy(source, dest, large_sem.at[i])
        for i, (source, dest) in enumerate(
            [(state_hbm.at[f], state.at[f]) for f in range(FIELDS)]
            + [
                (speed_hbm, raw_coefs.at[0]),
                (sigma_hbm, raw_coefs.at[1]),
                (dissipation_hbm, raw_coefs.at[2]),
            ]
        )
    ]
    for copy in small:
        copy.start()
    for copy in large:
        copy.start()

    barrier = pltpu.get_barrier_semaphore()
    near = [(0, 1), (1, 0), (1, 1), (chips - 1, 0), (chips - 1, 1)]
    leader = p == 0

    def plane_at(ahead, flip):
        return lax.rem(p // 2 + ahead, chips) * 2 + lax.rem(p + flip, 2)

    for ahead, flip in near:
        there = plane_at(ahead, flip)

        @pl.when(there != 0)
        def _():
            pl.semaphore_signal(barrier, inc=1, device_id=(a, there), device_id_type=MESH)

    def to_azim(source, dest, rows, send, recv, o):
        there = lax.rem(a + o, azims)
        return pltpu.make_async_remote_copy(
            src_ref=source.at[pl.ds(pl.multiple_of(there * rows, 8), rows), :],
            dst_ref=dest.at[pl.ds(pl.multiple_of(a * rows, 8), rows), :],
            send_sem=send.at[o],
            recv_sem=recv.at[o],
            device_id=(there, p),
            device_id_type=MESH,
        )

    def own_azim(source, dest, rows, index):
        at = pl.ds(pl.multiple_of(a * rows, 8), rows)
        return pltpu.make_async_copy(source.at[at, :], dest.at[at, :], own_sem.at[index])

    def plane_peer(i):
        late = i // 4
        pair = i // 2 - 2 * late
        odd = i - 2 * (i // 2)
        ahead = (1 - late) * (chips - 1 - (chips - 2) * odd) + late * (chips // 2) * (1 - pair)
        flip = (1 - late) * (1 - pair) + late * (1 - odd)
        return plane_at(ahead, flip)

    def to_plane(i):
        there = plane_peer(i)
        return (
            pltpu.make_async_remote_copy(
                src_ref=packed.at[i],
                dst_ref=packed_in.at[p],
                send_sem=tile_send.at[i],
                recv_sem=tile_recv.at[i],
                device_id=(a, there),
                device_id_type=MESH,
            ),
            pltpu.make_async_remote_copy(
                src_ref=landing.at[i],
                dst_ref=landing_in.at[p],
                send_sem=land_send.at[i],
                recv_sem=land_recv.at[i],
                device_id=(a, there),
                device_id_type=MESH,
            ),
        )

    lane = lax.broadcasted_iota(jnp.int32, (CHUNKS, LANES), 1)
    high_half = lane >= TILE
    spot = lax.broadcasted_iota(jnp.int32, (1, LANES), 1)

    for copy in small:
        copy.wait()

    def search(i, carry):
        target = plane_peer(i)
        seen = jnp.int32(0)
        found = [jnp.int32(-1)] * CAP
        for e in range(SLOTS):
            match = destination[e] == target
            for k in range(CAP):
                found[k] = jnp.where(match & (seen == k), e, found[k])
            seen = seen + jnp.where(match, 1, 0)
        for k in range(CAP):
            entries[i * CAP + k] = found[k]
        return carry

    lax.fori_loop(0, planes, search, 0)
    for f in range(FIELDS):
        large[f].wait()
        spread_twice(state.at[f], cells.at[f])

    @pl.when(jnp.logical_not(leader))
    def _():
        pl.semaphore_wait(barrier, len(near))

    @pl.when(jnp.logical_not(leader) & (p // 2 != chips // 2))
    def _():
        pl.semaphore_signal(ready, inc=1, device_id=(a, 0), device_id_type=MESH)

    @pl.when(leader)
    def _():
        pl.semaphore_wait(ready, len(near))

    for ahead in (1, chips - 1):
        pl.semaphore_signal(beyond, inc=1, device_id=(a, plane_at(ahead, 0)), device_id_type=MESH)

    wide = lax.broadcasted_iota(jnp.int32, (LANES, 2 * LANES), 1)
    second = wide // LANES
    wide_lane = wide & (LANES - 1)
    from_lane = lax.broadcasted_iota(jnp.int32, (LANES, 2 * LANES), 0)

    def fill(i, carry):
        places = jnp.full((1, LANES), -1, jnp.int32)
        for k in range(CAP):
            entry = entries[i * CAP + k]
            e = jnp.maximum(entry, 0)
            places = jnp.where(spot == k, jnp.where(entry >= 0, receptor[e], -1), places)
            row = donor[e]
            block = jnp.where(row >= 8, 1, 0)
            ox = offset_x[e]
            oy = offset_y[e]
            fx = fraction_x[e]
            fy = fraction_y[e]
            start = row - 8 * block + 8 * (oy >> 1)
            odd = (oy & 1) == 1
            even_first = jnp.where(odd, 0.0, 1.0 - fy)
            even_second = jnp.where(odd, fy, 0.0)
            odd_weight = jnp.where(odd, 1.0 - fy, fy)
            pick = (wide_lane & TILE) + ((wide_lane + ox + second) & (TILE - 1))
            chosen = jnp.where(from_lane == pick, 1.0, 0.0).astype(jnp.bfloat16)
            values = []
            for f in range(FIELDS):
                here = cells[f, block, pl.ds(start, CHUNKS, stride=8), :]
                after = cells[f, block, pl.ds(start + 8, CHUNKS, stride=8), :]
                between = pltpu.roll(jnp.where(high_half, here, after), TILE, 1)
                values.append(even_first * here + even_second * after + odd_weight * between)
            value = jnp.concatenate(values, axis=0)
            high = value.astype(jnp.bfloat16)
            rest = value - high.astype(jnp.float32)
            middle = rest.astype(jnp.bfloat16)
            low = (rest - middle.astype(jnp.float32)).astype(jnp.bfloat16)
            moved = jnp.dot(
                jnp.concatenate([high, middle, low], axis=1),
                jnp.concatenate([chosen, chosen, chosen], axis=0),
                preferred_element_type=jnp.float32,
            )
            mixed = (1.0 - fx) * moved[:, :LANES] + fx * moved[:, LANES:]
            for f in range(FIELDS):
                packed[i, k, f] = mixed[f * CHUNKS : (f + 1) * CHUNKS]
        landing[i] = places

        @pl.when(i < planes - 1)
        def _():
            for copy in to_plane(i):
                copy.start()

        return carry

    lax.fori_loop(0, planes // 2, fill, 0)
    pl.semaphore_wait(beyond, 2)

    @pl.when(leader)
    def _():
        for o in range(1, azims):
            pl.semaphore_signal(
                barrier, inc=1, device_id=(lax.rem(a + o, azims), p), device_id_type=MESH
            )

    lax.fori_loop(planes // 2, planes, fill, 0)
    own_tiles = pltpu.make_async_copy(packed.at[planes - 1], packed_in.at[p], own_sem.at[2])
    own_land = pltpu.make_async_copy(landing.at[planes - 1], landing_in.at[p], own_sem.at[3])
    own_tiles.start()
    own_land.start()

    for copy in large[FIELDS:]:
        copy.wait()
    spread(raw_coefs, coefs)

    def one_part(part, carry):
        eliminate(cells, coefs, solved, tips, part)
        return carry

    lax.fori_loop(0, CHUNKS // 8, one_part, 0)

    @pl.when(leader)
    def _():
        pl.semaphore_wait(barrier, azims - 1)
        for o in range(1, planes):
            pl.semaphore_signal(go, inc=1, device_id=(a, o), device_id_type=MESH)

    @pl.when(jnp.logical_not(leader))
    def _():
        pl.semaphore_wait(go, 1)

    tip_copies = [to_azim(tips, tips_in, tip_rows, tips_send, tips_recv, o) for o in range(1, azims)]
    for copy in tip_copies:
        copy.start()
    own_tips = own_azim(tips, tips_in, tip_rows, 0)
    own_tips.start()
    own_tips.wait()
    for copy in tip_copies:
        copy.wait()

    for v in range(TIPS):
        value = tips_in[pl.ds(v, CHUNKS, stride=TIPS), :]
        ping[v, 0:CHUNKS, :] = value
        ping[v, CHUNKS : 2 * CHUNKS, :] = value

    source, dest = ping, pong
    step = 1
    while step < azims:

        def level(part, carry, source=source, dest=dest, shift=step * per):
            row = pl.multiple_of(part * 8, 8)
            left = [source[COLS * i : COLS * (i + 1), pl.ds(row, 8), :] for i in range(4)]
            right = [source[COLS * i : COLS * (i + 1), pl.ds(row + shift, 8), :] for i in range(4)]
            for i, value in enumerate(merge(left, right)):
                dest[COLS * i : COLS * (i + 1), pl.ds(row, 8), :] = value
                dest[COLS * i : COLS * (i + 1), pl.ds(row + CHUNKS, 8), :] = value
            return carry

        lax.fori_loop(0, CHUNKS // 8, level, 0)
        source, dest = dest, source
        step *= 2

    def last(part, carry):
        row = pl.multiple_of(part * 8, 8)
        block = [source[COLS * i : COLS * (i + 1), pl.ds(row, 8), :] for i in range(4)]
        values = close(block)
        for i in range(2):
            firsts[FIELDS * i : FIELDS * (i + 1), pl.ds(row, 8), :] = values[i]
            firsts[FIELDS * i : FIELDS * (i + 1), pl.ds(row + CHUNKS, 8), :] = values[i]
            for f in range(FIELDS):
                answers[pl.ds(part * 8 * BACK + i * FIELDS + f, 8, stride=BACK), :] = values[2 + i][f]
        return carry

    lax.fori_loop(0, CHUNKS // 8, last, 0)
    for v in range(2 * FIELDS):
        answers[pl.ds(2 * FIELDS + v, CHUNKS, stride=BACK), :] = firsts[v, per : per + CHUNKS, :]

    back_copies = [
        to_azim(answers, borders, back_rows, back_send, back_recv, o) for o in range(1, azims)
    ]
    for copy in back_copies:
        copy.start()
    own_back = own_azim(answers, borders, back_rows, 1)
    own_back.start()
    own_back.wait()
    for copy in back_copies:
        copy.wait()

    def compose(part, carry):
        at = pl.ds(pl.multiple_of(part * 8, 8), 8)

        def border(i, f):
            return borders[pl.ds(part * 8 * BACK + i * FIELDS + f, 8, stride=BACK), :]

        for f in range(FIELDS):
            outside = [border(i, f) for i in range(4)]
            for r in range(ROWS):
                value = solved[r, f, at, :]
                for i in range(4):
                    value = value - solved[r, FIELDS + i, at, :] * outside[i]
                cells[f, r // 8, pl.ds(part * 64 + r % 8, 8, stride=8), :] = value
        return carry

    lax.fori_loop(0, CHUNKS // 8, compose, 0)

    def move(c, carry):
        at = pl.ds(pl.multiple_of(c * LANES, LANES), LANES)
        row = pl.multiple_of(c * 8, 8)
        for f in range(FIELDS):
            update[f, 0:8, at] = cells[f, 0, pl.ds(row, 8), :] - state[f, 0:8, at]
            update[f, 8:12, at] = cells[f, 1, pl.ds(row, 4), :] - state[f, 8:12, at]
        return carry

    lax.fori_loop(0, CHUNKS, move, 0, unroll=4)

    own_tiles.wait()
    own_land.wait()

    def settle(i, carry):
        for copy in to_plane(i):
            copy.wait()
        return carry

    lax.fori_loop(0, planes - 1, settle, 0)


def finish_kernel(landing, packed, update, state, fringe, out_hbm, out, rows, cells, total, places, counts, sems):
    planes = landing.shape[0]
    fetch = pltpu.make_async_copy(landing, places, sems.at[FIELDS])
    fetch.start()
    for r in range(ROWS):
        counts[r] = 0.0
    total[...] = jnp.zeros(total.shape, jnp.float32)
    fetch.wait()

    def add(slot, carry):
        d = slot // CAP
        k = slot - d * CAP
        row = places[d, 0, k]

        @pl.when(row >= 0)
        def _():
            total[row] = total[row] + packed[d, k]
            counts[row] = counts[row] + 1.0

        return carry

    lax.fori_loop(0, planes * CAP, add, 0)

    for b in range(2):
        line = lax.broadcasted_iota(jnp.int32, (8, LANES), 0) + 8 * b
        number = jnp.zeros((8, LANES), jnp.float32)
        for r in range(8 * b, min(8 * b + 8, ROWS)):
            number = jnp.where(line == r, counts[r], number)
        rows[2 * b] = number
        rows[2 * b + 1] = 1.0 / (number + 1.0)

    copies = []
    for f in range(FIELDS):
        for r in range(ROWS):
            cells[r // 8, pl.ds(r % 8, CHUNKS, stride=8), :] = total[r, f]

        def move(c, carry, f=f):
            at = pl.ds(pl.multiple_of(c * LANES, LANES), LANES)
            row = pl.multiple_of(c * 8, 8)
            for b, (low, high) in enumerate(((0, 8), (8, ROWS))):
                size = high - low
                q = state[f, low:high, at]
                relaxed = (cells[b, pl.ds(row, size), :] - rows[2 * b, 0:size, :] * q) * rows[
                    2 * b + 1, 0:size, :
                ]
                out[f, low:high, at] = jnp.where(
                    fringe[low:high, at] == 1, relaxed, update[f, low:high, at]
                )
            return carry

        lax.fori_loop(0, CHUNKS, move, 0, unroll=4)
        copy = pltpu.make_async_copy(out.at[f], out_hbm.at[f], sems.at[f])
        copy.start()
        copies.append(copy)
    for copy in copies:
        copy.wait()


def f32(*shape):
    return jax.ShapeDtypeStruct(shape, jnp.float32)


def local(
    state,
    speed,
    sigma,
    dissipation,
    fringe,
    destination,
    donor,
    receptor,
    offset_y,
    offset_x,
    fraction_y,
    fraction_x,
):
    azims = lax.axis_size("azim")
    planes = lax.axis_size("plane")
    vmem = pl.BlockSpec(memory_space=pltpu.VMEM)
    hbm = pl.BlockSpec(memory_space=pltpu.HBM)
    number = pltpu.VMEM
    packed_in, landing_in, update = pl.pallas_call(
        functools.partial(exchange_kernel, azims, planes),
        out_shape=(
            f32(planes, CAP, FIELDS, CHUNKS, LANES),
            jax.ShapeDtypeStruct((planes, 1, LANES), jnp.int32),
            f32(FIELDS, ROWS, CELLS),
        ),
        in_specs=[hbm] * 11,
        out_specs=(vmem,) * 3,
        scratch_shapes=[pltpu.SMEM((SLOTS,), jnp.int32)] * 5
        + [pltpu.SMEM((SLOTS,), jnp.float32)] * 2
        + [
            pltpu.SMEM((planes * CAP,), jnp.int32),
            number((FIELDS, ROWS, CELLS), jnp.float32),
            number((3, ROWS, CELLS), jnp.float32),
            number((FIELDS, 2, 2 * CHUNKS * 8, LANES), jnp.float32),
            number((3, 2, CHUNKS * 8, LANES), jnp.float32),
            number((planes, CAP, FIELDS, CHUNKS, LANES), jnp.float32),
            number((planes, 1, LANES), jnp.int32),
            number((ROWS, COLS, CHUNKS, LANES), jnp.float32),
            number((CHUNKS * TIPS, LANES), jnp.float32),
            number((CHUNKS * TIPS, LANES), jnp.float32),
            number((TIPS, 2 * CHUNKS, LANES), jnp.float32),
            number((TIPS, 2 * CHUNKS, LANES), jnp.float32),
            number((2 * FIELDS, 2 * CHUNKS, LANES), jnp.float32),
            number((CHUNKS * BACK, LANES), jnp.float32),
            number((CHUNKS * BACK, LANES), jnp.float32),
            pltpu.SemaphoreType.DMA((7,)),
            pltpu.SemaphoreType.DMA((FIELDS + 3,)),
            pltpu.SemaphoreType.DMA((planes,)),
            pltpu.SemaphoreType.DMA((planes,)),
            pltpu.SemaphoreType.DMA((planes,)),
            pltpu.SemaphoreType.DMA((planes,)),
            pltpu.SemaphoreType.DMA((azims,)),
            pltpu.SemaphoreType.DMA((azims,)),
            pltpu.SemaphoreType.DMA((azims,)),
            pltpu.SemaphoreType.DMA((azims,)),
            pltpu.SemaphoreType.DMA((4,)),
            pltpu.SemaphoreType.REGULAR,
            pltpu.SemaphoreType.REGULAR,
            pltpu.SemaphoreType.REGULAR,
        ],
        compiler_params=pltpu.CompilerParams(
            collective_id=0, has_side_effects=True, vmem_limit_bytes=40 * 2**20
        ),
        name="exchange",
    )(
        *(
            pltpu.with_memory_space_constraint(value, pltpu.HBM)
            for value in (
                destination.reshape(SLOTS),
                donor,
                receptor,
                offset_y,
                offset_x,
                fraction_y,
                fraction_x,
                state,
                speed,
                sigma,
                dissipation,
            )
        )
    )
    return pl.pallas_call(
        finish_kernel,
        out_shape=f32(FIELDS, ROWS, CELLS),
        in_specs=[vmem] * 5,
        out_specs=hbm,
        scratch_shapes=[
            number((FIELDS, ROWS, CELLS), jnp.float32),
            number((4, 8, LANES), jnp.float32),
            number((2, CHUNKS * 8, LANES), jnp.float32),
            number((ROWS, FIELDS, CHUNKS, LANES), jnp.float32),
            pltpu.SMEM((planes, 1, LANES), jnp.int32),
            pltpu.SMEM((ROWS,), jnp.float32),
            pltpu.SemaphoreType.DMA((FIELDS + 1,)),
        ],
        compiler_params=pltpu.CompilerParams(vmem_limit_bytes=32 * 2**20),
        name="finish",
    )(landing_in, packed_in, update, state, fringe)


def solution(mesh):
    in_specs = (
        P(None, "azim", "plane"),
        P("azim", "plane"),
        P("azim", "plane"),
        P("azim", "plane"),
        P("azim", "plane"),
        P(("azim", "plane"), None),
        P(("azim", "plane")),
        P(("azim", "plane")),
        P(("azim", "plane")),
        P(("azim", "plane")),
        P(("azim", "plane")),
        P(("azim", "plane")),
    )
    out_specs = P(None, "azim", "plane")
    return jax.shard_map(local, mesh=mesh, in_specs=in_specs, out_specs=out_specs, check_vma=False)
```

```python
import functools

import jax
import jax.numpy as jnp
from jax import lax
from jax.experimental import pallas as pl
from jax.experimental.pallas import tpu as pltpu
from jax.sharding import PartitionSpec as P

TILE = 64
CAP = 4
FIELDS = 5
ROWS = 12
CELLS = TILE * TILE
LANES = 128
CHUNKS = CELLS // LANES
SLOTS = 16
COLS = FIELDS + 4
TIPS = 4 * COLS
BACK = 4 * FIELDS
MESH = pl.DeviceIdType.MESH
GROUPS = ((0, 3), (3, FIELDS))
PLACES = 8
SPREAD = CHUNKS * ROWS
TIP_ROW = {0: 0, 1: 1, ROWS - 2: 2, ROWS - 1: 3}


def spread(source, dest):
    def move(c, carry):
        lane = pl.multiple_of(c * LANES, LANES)
        row = pl.multiple_of(c * 8, 8)
        for f in range(source.shape[0]):
            dest[f, 0, pl.ds(row, 8), :] = source[f, 0:8, pl.ds(lane, LANES)]
            dest[f, 1, pl.ds(row, 4), :] = source[f, 8:12, pl.ds(lane, LANES)]
        return carry

    lax.fori_loop(0, CHUNKS, move, 0, unroll=4)


def spread_twice(source, dest):
    def move(j, carry):
        lane = pl.multiple_of(j * 2 * LANES, 2 * LANES)
        row = pl.multiple_of(j * 2 * ROWS, 8)
        value = jnp.concatenate(
            [source[:, pl.ds(lane, LANES)], source[:, pl.ds(lane + LANES, LANES)]], axis=0
        )
        dest[pl.ds(row, 2 * ROWS), :] = value
        dest[pl.ds(row + SPREAD, 2 * ROWS), :] = value
        return carry

    lax.fori_loop(0, CHUNKS // 2, move, 0, unroll=4)


def eliminate(cells, coefs, solved, tips, part):
    base = part * 64
    at = pl.ds(pl.multiple_of(part * 8, 8), 8)

    def load(ref, lead, r):
        return ref[lead, r // 8, pl.ds(base + r % 8, 8, stride=8), :]

    def load_cells(k, r):
        return cells[k, pl.ds(part * 8 * ROWS + r, 8, stride=ROWS), :]

    upper1 = []
    upper2 = []
    fields1 = fields2 = None
    for r in range(ROWS):
        c = load(coefs, 0, r)
        s = load(coefs, 1, r)
        d = load(coefs, 2, r)
        half = 0.5 * c
        common = -s - 4.0 * d
        a1 = common - half
        e1 = common + half
        centre = 1.0 + (2.0 * s + 10.0 * d)
        weight = 1.0 + 4.0 * d
        if r == 0:
            pivot, u1_top = centre, e1
        elif r == 1:
            pivot = centre - a1 * upper1[0]
            u1_top = e1 - a1 * upper2[0]
        else:
            a1 = a1 - d * upper1[r - 2]
            pivot = centre - d * upper2[r - 2] - a1 * upper1[r - 1]
            u1_top = e1 - a1 * upper2[r - 1]
        inverse = 1.0 / pivot
        upper1.append(u1_top * inverse)
        upper2.append(d * inverse)
        now = []
        for k in range(FIELDS + 2):
            if k < FIELDS:
                value = weight * load_cells(k, r)
            elif r == 0:
                now.append((d if k == FIELDS else a1) * inverse)
                continue
            elif r == 1 and k == FIELDS + 1:
                value = d
            else:
                value = None
            if r >= 1:
                term = a1 * fields1[k]
                value = -term if value is None else value - term
            if r >= 2:
                value = value - d * fields2[k]
            now.append(value * inverse)
        for k in range(FIELDS + 2):
            solved[r, k, at, :] = now[k]
        fields2, fields1 = fields1, now

    later1 = later2 = None
    for r in range(ROWS - 1, -1, -1):
        now = []
        for k in range(COLS):
            if k < FIELDS + 2:
                value = solved[r, k, at, :]
            elif r == ROWS - 1:
                value = upper1[r] if k == FIELDS + 2 else upper2[r]
            elif r == ROWS - 2 and k == FIELDS + 2:
                value = upper2[r]
            else:
                value = None
            if r < ROWS - 1:
                term = upper1[r] * later1[k]
                value = -term if value is None else value - term
            if r < ROWS - 2:
                value = value - upper2[r] * later2[k]
            now.append(value)
        for k in range(COLS):
            solved[r, k, at, :] = now[k]
        if r in TIP_ROW:
            for k in range(COLS):
                tips[pl.ds(part * 8 * TIPS + TIP_ROW[r] * COLS + k, 8, stride=TIPS), :] = now[k]
        later2, later1 = later1, now


def merge(left, right):
    def pair(matrix, columns):
        return [matrix[i][0] * columns[0] + matrix[i][1] * columns[1] for i in range(2)]

    gs = slice(0, FIELDS)
    ws = slice(FIELDS, FIELDS + 2)
    vs = slice(FIELDS + 2, FIELDS + 4)
    left_v = [[left[i][FIELDS + 2 + m] for m in range(2)] for i in range(4)]
    right_w = [[right[i][FIELDS + m] for m in range(2)] for i in range(4)]
    nothing = jnp.zeros((2,) + left[0].shape[1:], jnp.float32)
    product = [
        [sum(right_w[i][m] * left_v[2 + m][j] for m in range(2)) for j in range(2)]
        for i in range(2)
    ]
    m00, m01 = 1.0 - product[0][0], -product[0][1]
    m10, m11 = -product[1][0], 1.0 - product[1][1]
    scale = 1.0 / (m00 * m11 - m01 * m10)
    inverse = [[m11 * scale, -m01 * scale], [-m10 * scale, m00 * scale]]
    known = [jnp.concatenate([left[2 + i][gs], left[2 + i][ws]], axis=0) for i in range(2)]
    through = pair(right_w[:2], known)
    raw = [
        jnp.concatenate(
            [right[i][gs] - through[i][gs], -through[i][FIELDS:], right[i][vs]], axis=0
        )
        for i in range(2)
    ]
    inner_a = pair(inverse, raw)
    from_a = pair(left_v[2:], inner_a)
    inner_b = [
        jnp.concatenate([left[2 + i][gs], left[2 + i][ws], nothing], axis=0) - from_a[i]
        for i in range(2)
    ]
    from_a = pair(left_v[:2], inner_a)
    outer_a = [
        jnp.concatenate([left[i][gs], left[i][ws], nothing], axis=0) - from_a[i] for i in range(2)
    ]
    from_b = pair(right_w[2:], inner_b)
    outer_b = [
        jnp.concatenate([right[2 + i][gs], nothing, right[2 + i][vs]], axis=0) - from_b[i]
        for i in range(2)
    ]
    return outer_a + outer_b


def close(block):
    matrix = []
    for i in range(4):
        line = [block[i][FIELDS + 2], block[i][FIELDS + 3], block[i][FIELDS], block[i][FIELDS + 1]]
        line[i] = 1.0 + line[i]
        matrix.append(line)
    values = [block[i][0:FIELDS] for i in range(4)]
    for p in range(4):
        scale = 1.0 / matrix[p][p]
        for c in range(p + 1, 4):
            matrix[p][c] = matrix[p][c] * scale
        values[p] = values[p] * scale
        for r in range(p + 1, 4):
            for c in range(p + 1, 4):
                matrix[r][c] = matrix[r][c] - matrix[r][p] * matrix[p][c]
            values[r] = values[r] - matrix[r][p] * values[p]
    for r in range(2, -1, -1):
        for c in range(r + 1, 4):
            values[r] = values[r] - matrix[r][c] * values[c]
    return values


def exchange_kernel(
    azims,
    planes,
    destination_hbm,
    donor_hbm,
    receptor_hbm,
    offset_y_hbm,
    offset_x_hbm,
    fraction_y_hbm,
    fraction_x_hbm,
    state_hbm,
    speed_hbm,
    sigma_hbm,
    dissipation_hbm,
    arrived0,
    arrived1,
    landing_in,
    update,
    destination,
    donor,
    receptor,
    offset_y,
    offset_x,
    fraction_y,
    fraction_x,
    entries,
    integers,
    reals,
    state,
    raw_coefs,
    result,
    cells,
    cells0,
    cells1,
    coefs,
    packed0,
    packed1,
    landing,
    integers_out,
    reals_out,
    integers_in,
    reals_in,
    solved,
    tips,
    tips_in,
    ping,
    pong,
    firsts,
    answers,
    borders,
    small_sem,
    large_sem,
    raw_send,
    raw_recv,
    table_send,
    table_recv,
    table_sem,
    tile_send,
    tile_recv,
    land_send,
    land_recv,
    tips_send,
    tips_recv,
    back_send,
    back_recv,
    own_sem,
    ready,
    beyond,
    go,
):
    a = lax.axis_index("azim")
    p = lax.axis_index("plane")
    per = CHUNKS // azims
    tip_rows = per * TIPS
    back_rows = per * BACK
    chips = planes // 2
    core = lax.rem(p, 2)
    groups = (0, 1)
    arrived = (arrived0, arrived1)
    packed = (packed0, packed1)
    raw_cells = (cells0, cells1)

    small = [
        pltpu.make_async_copy(source, dest, small_sem.at[i])
        for i, (source, dest) in enumerate(
            (
                (destination_hbm, destination),
                (donor_hbm, donor),
                (receptor_hbm, receptor),
                (offset_y_hbm, offset_y),
                (offset_x_hbm, offset_x),
                (fraction_y_hbm, fraction_y),
                (fraction_x_hbm, fraction_x),
            )
        )
    ]
    large = [
        pltpu.make_async_copy(source, dest, large_sem.at[i])
        for i, (source, dest) in enumerate(
            [(state_hbm.at[f], state.at[f]) for f in range(FIELDS)]
            + [
                (speed_hbm, raw_coefs.at[0]),
                (sigma_hbm, raw_coefs.at[1]),
                (dissipation_hbm, raw_coefs.at[2]),
            ]
        )
    ]
    for copy in small:
        copy.start()
    for copy in large:
        copy.start()

    barrier = pltpu.get_barrier_semaphore()
    near = [(0, 1), (1, 0), (1, 1), (chips - 1, 0), (chips - 1, 1)]
    leader = p == 0

    def plane_at(ahead, flip):
        return lax.rem(p // 2 + ahead, chips) * 2 + lax.rem(p + flip, 2)

    def remote(source, dest, send, recv, there):
        return pltpu.make_async_remote_copy(
            src_ref=source,
            dst_ref=dest,
            send_sem=send,
            recv_sem=recv,
            device_id=(a, there),
            device_id_type=MESH,
        )

    onward = (1 + core * (chips - 2), chips - 1 - core * (chips - 2))
    behind = (onward[1], onward[0])

    for ahead, flip in near:
        there = plane_at(ahead, flip)

        @pl.when(there != 0)
        def _():
            pl.semaphore_signal(barrier, inc=1, device_id=(a, there), device_id_type=MESH)

    def to_azim(source, dest, rows, send, recv, o):
        there = lax.rem(a + o, azims)
        return pltpu.make_async_remote_copy(
            src_ref=source.at[pl.ds(pl.multiple_of(there * rows, 8), rows), :],
            dst_ref=dest.at[pl.ds(pl.multiple_of(a * rows, 8), rows), :],
            send_sem=send.at[o],
            recv_sem=recv.at[o],
            device_id=(there, p),
            device_id_type=MESH,
        )

    def own_azim(source, dest, rows, index):
        at = pl.ds(pl.multiple_of(a * rows, 8), rows)
        return pltpu.make_async_copy(source.at[at, :], dest.at[at, :], own_sem.at[index])

    def raw_copy(g):
        low, high = GROUPS[g]
        return remote(
            cells.at[low:high, 0:SPREAD, :],
            raw_cells[g].at[:, 0:SPREAD, :],
            raw_send.at[g],
            raw_recv.at[g],
            plane_at(onward[g], 0),
        )

    def table_copies(g):
        there = plane_at(onward[g], 0)
        return (
            remote(integers_out, integers_in.at[g], table_send.at[2 * g], table_recv.at[2 * g], there),
            remote(
                reals_out, reals_in.at[g], table_send.at[2 * g + 1], table_recv.at[2 * g + 1], there
            ),
        )

    def tile_copy(g, place, owner, ahead, flip):
        index = g * PLACES + place
        return remote(
            packed[g].at[place],
            arrived[g].at[owner],
            tile_send.at[index],
            tile_recv.at[index],
            plane_at(ahead, flip),
        )

    def land_copy(index, owner, ahead, flip):
        return remote(
            landing.at[index],
            landing_in.at[owner],
            land_send.at[index],
            land_recv.at[index],
            plane_at(ahead, flip),
        )

    def direct_copy(g, flip):
        return tile_copy(g, flip, p, behind[g], flip)

    def relay_copy(g, u):
        return tile_copy(g, 2 + u, plane_at(behind[g], 0), (1 - u // 2) * onward[g], u - 2 * (u // 2))

    def mate_copy(g):
        return tile_copy(g, 6, p, 0, 1)

    spot = lax.broadcasted_iota(jnp.int32, (1, LANES), 1)
    for copy in small:
        copy.wait()
    for line, source in enumerate((destination, donor, receptor, offset_y, offset_x)):
        value = jnp.zeros((1, LANES), jnp.int32)
        for e in range(SLOTS):
            value = jnp.where(spot == e, source[e], value)
        integers_out[line : line + 1, :] = value
    for line, source in enumerate((fraction_y, fraction_x)):
        value = jnp.zeros((1, LANES), jnp.float32)
        for e in range(SLOTS):
            value = jnp.where(spot == e, source[e], value)
        reals_out[line : line + 1, :] = value

    for f in range(FIELDS):
        large[f].wait()
        spread_twice(state.at[f], cells.at[f])

    @pl.when(jnp.logical_not(leader))
    def _():
        pl.semaphore_wait(barrier, len(near))

    @pl.when(jnp.logical_not(leader) & (p // 2 != chips // 2))
    def _():
        pl.semaphore_signal(ready, inc=1, device_id=(a, 0), device_id_type=MESH)

    @pl.when(leader)
    def _():
        pl.semaphore_wait(ready, len(near))

    for g in groups:
        for copy in table_copies(g):
            copy.start()
    for g in groups:
        raw_copy(g).start()
    for ahead in (1, chips - 1):
        pl.semaphore_signal(beyond, inc=1, device_id=(a, plane_at(ahead, 0)), device_id_type=MESH)

    def search(named, target, base):
        seen = jnp.int32(0)
        found = [jnp.int32(-1)] * CAP
        for e in range(SLOTS):
            match = named(e) == target
            for k in range(CAP):
                found[k] = jnp.where(match & (seen == k), e, found[k])
            seen = seen + jnp.where(match, 1, 0)
        for k in range(CAP):
            entries[base + k] = found[k]

    lane = lax.broadcasted_iota(jnp.int32, (CHUNKS, LANES), 1)
    high_half = lane >= TILE
    wide = lax.broadcasted_iota(jnp.int32, (LANES, 2 * LANES), 1)
    second = wide // LANES
    wide_lane = wide & (LANES - 1)
    from_lane = lax.broadcasted_iota(jnp.int32, (LANES, 2 * LANES), 0)

    def places_of(base, receptor_of):
        places = jnp.full((1, LANES), -1, jnp.int32)
        for k in range(CAP):
            entry = entries[base + k]
            place = jnp.where(entry >= 0, receptor_of(jnp.maximum(entry, 0)), -1)
            places = jnp.where(spot == k, place, places)
        return places

    def fill(base, table, blocks, dests):
        donor_of, oy_of, ox_of, fy_of, fx_of = table
        for k in range(CAP):
            e = jnp.maximum(entries[base + k], 0)
            row = donor_of(e)
            ox = ox_of(e)
            oy = oy_of(e)
            fx = fx_of(e)
            fy = fy_of(e)
            start = row + ROWS * (oy >> 1)
            odd = (oy & 1) == 1
            even_first = jnp.where(odd, 0.0, 1.0 - fy)
            even_second = jnp.where(odd, fy, 0.0)
            odd_weight = jnp.where(odd, 1.0 - fy, fy)
            pick = (wide_lane & TILE) + ((wide_lane + ox + second) & (TILE - 1))
            chosen = jnp.where(from_lane == pick, 1.0, 0.0).astype(jnp.bfloat16)
            values = []
            for source, f in blocks:
                here = source[f, pl.ds(start, CHUNKS, stride=ROWS), :]
                after = source[f, pl.ds(start + ROWS, CHUNKS, stride=ROWS), :]
                between = pltpu.roll(jnp.where(high_half, here, after), TILE, 1)
                values.append(even_first * here + even_second * after + odd_weight * between)
            value = jnp.concatenate(values, axis=0)
            high = value.astype(jnp.bfloat16)
            rest = value - high.astype(jnp.float32)
            middle = rest.astype(jnp.bfloat16)
            low = (rest - middle.astype(jnp.float32)).astype(jnp.bfloat16)
            moved = jnp.dot(
                jnp.concatenate([high, middle, low], axis=1),
                jnp.concatenate([chosen, chosen, chosen], axis=0),
                preferred_element_type=jnp.float32,
            )
            mixed = (1.0 - fx) * moved[:, :LANES] + fx * moved[:, LANES:]
            for n, (dest, place, f) in enumerate(dests):
                dest[place, k, f] = mixed[n * CHUNKS : (n + 1) * CHUNKS]

    own_table = tuple(
        functools.partial(lambda ref, e: ref[e], ref)
        for ref in (donor, offset_y, offset_x, fraction_y, fraction_x)
    )
    for g in groups:

        def find(flip, carry, g=g):
            search(lambda e: destination[e], plane_at(behind[g], flip), (2 * g + flip) * CAP)
            return carry

        lax.fori_loop(0, 2, find, 0)

    def find_near(flip, carry):
        search(lambda e: destination[e], plane_at(0, flip), (4 + flip) * CAP)
        return carry

    lax.fori_loop(0, 2, find_near, 0)
    for index in range(4):
        landing[index] = places_of(index * CAP, lambda e: receptor[e])
    landing[4] = places_of(5 * CAP, lambda e: receptor[e])
    landing[5] = places_of(4 * CAP, lambda e: receptor[e])
    near_land = [land_copy(2 * g + flip, p, behind[g], flip) for g in groups for flip in range(2)]
    near_land.append(land_copy(4, p, 0, 1))
    for copy in near_land:
        copy.start()
    own_land = pltpu.make_async_copy(landing.at[5], landing_in.at[p], own_sem.at[3])
    own_land.start()

    def widths(g):
        return range(GROUPS[g][1] - GROUPS[g][0])

    for g in groups:

        def fill_direct(flip, carry, g=g):
            fill(
                (2 * g + flip) * CAP,
                own_table,
                [(cells, GROUPS[g][0] + f) for f in widths(g)],
                [(packed[g], flip, f) for f in widths(g)],
            )
            return carry

        lax.fori_loop(0, 2, fill_direct, 0)

    def fill_near(flip, carry):
        fill(
            (4 + flip) * CAP,
            own_table,
            [(cells, f) for f in range(FIELDS)],
            [(packed[g], 7 - flip, f) for g in groups for f in widths(g)],
        )
        return carry

    lax.fori_loop(0, 2, fill_near, 0)
    own_tiles = [
        pltpu.make_async_copy(packed[g].at[7], arrived[g].at[p], own_sem.at[4 + g]) for g in groups
    ]
    for g in groups:
        mate_copy(g).start()
        own_tiles[g].start()

    pl.semaphore_wait(beyond, 2)

    @pl.when(leader)
    def _():
        for o in range(1, azims):
            pl.semaphore_signal(
                barrier, inc=1, device_id=(lax.rem(a + o, azims), p), device_id_type=MESH
            )

    for copy in large[FIELDS:]:
        copy.wait()
    spread(raw_coefs, coefs)

    def one_part(part, carry):
        eliminate(cells, coefs, solved, tips, part)
        return carry

    lax.fori_loop(0, CHUNKS // 8, one_part, 0)

    @pl.when(leader)
    def _():
        pl.semaphore_wait(barrier, azims - 1)
        for o in range(1, planes):
            pl.semaphore_signal(go, inc=1, device_id=(a, o), device_id_type=MESH)

    @pl.when(jnp.logical_not(leader))
    def _():
        pl.semaphore_wait(go, 1)

    tip_copies = [to_azim(tips, tips_in, tip_rows, tips_send, tips_recv, o) for o in range(1, azims)]
    for copy in tip_copies:
        copy.start()
    own_tips = own_azim(tips, tips_in, tip_rows, 0)
    own_tips.start()

    for g in groups:
        raw_copy(g).wait_send()
    for flip in range(2):
        for g in groups:
            direct_copy(g, flip).start()

    fetches = []
    for g in groups:
        for copy in table_copies(g):
            copy.wait()
        fetches.append(pltpu.make_async_copy(integers_in.at[g], integers.at[g], table_sem.at[2 * g]))
        fetches.append(pltpu.make_async_copy(reals_in.at[g], reals.at[g], table_sem.at[2 * g + 1]))
    for copy in fetches:
        copy.start()
    for copy in fetches:
        copy.wait()
    for g in groups:

        def find_relay(u, carry, g=g):
            target = plane_at((1 - u // 2) * onward[g], u - 2 * (u // 2))
            search(lambda e: integers[g, 0, e], target, (6 + 4 * g + u) * CAP)
            return carry

        lax.fori_loop(0, 4, find_relay, 0)
    far_land = []
    for u in range(2):
        landing[6 + u] = places_of((6 + u) * CAP, lambda e: integers[0, 2, e])
        far_land.append(land_copy(6 + u, plane_at(behind[0], 0), onward[0], u))
        far_land[-1].start()

    relay_own = [
        pltpu.make_async_copy(
            packed[g].at[4], arrived[g].at[plane_at(behind[g], 0)], own_sem.at[6 + g]
        )
        for g in groups
    ]
    for g in groups:
        raw_copy(g).wait_recv()
        for f in widths(g):
            raw_cells[g][f, SPREAD:, :] = raw_cells[g][f, 0:SPREAD, :]
        relay_table = (
            lambda e, g=g: integers[g, 1, e],
            lambda e, g=g: integers[g, 3, e],
            lambda e, g=g: integers[g, 4, e],
            lambda e, g=g: reals[g, 0, e],
            lambda e, g=g: reals[g, 1, e],
        )

        def fill_relay(u, carry, g=g, relay_table=relay_table):
            fill(
                (6 + 4 * g + u) * CAP,
                relay_table,
                [(raw_cells[g], f) for f in widths(g)],
                [(packed[g], 2 + u, f) for f in widths(g)],
            )

            @pl.when(u != 2)
            def _():
                relay_copy(g, u).start()

            @pl.when(u == 2)
            def _():
                relay_own[g].start()

            return carry

        lax.fori_loop(0, 4, fill_relay, 0)

    own_tips.wait()
    for copy in tip_copies:
        copy.wait()

    for v in range(TIPS):
        value = tips_in[pl.ds(v, CHUNKS, stride=TIPS), :]
        ping[v, 0:CHUNKS, :] = value
        ping[v, CHUNKS : 2 * CHUNKS, :] = value

    source, dest = ping, pong
    step = 1
    while step < azims:

        def level(part, carry, source=source, dest=dest, shift=step * per):
            row = pl.multiple_of(part * 8, 8)
            left = [source[COLS * i : COLS * (i + 1), pl.ds(row, 8), :] for i in range(4)]
            right = [source[COLS * i : COLS * (i + 1), pl.ds(row + shift, 8), :] for i in range(4)]
            for i, value in enumerate(merge(left, right)):
                dest[COLS * i : COLS * (i + 1), pl.ds(row, 8), :] = value
                dest[COLS * i : COLS * (i + 1), pl.ds(row + CHUNKS, 8), :] = value
            return carry

        lax.fori_loop(0, CHUNKS // 8, level, 0)
        source, dest = dest, source
        step *= 2

    def last(part, carry):
        row = pl.multiple_of(part * 8, 8)
        block = [source[COLS * i : COLS * (i + 1), pl.ds(row, 8), :] for i in range(4)]
        values = close(block)
        for i in range(2):
            firsts[FIELDS * i : FIELDS * (i + 1), pl.ds(row, 8), :] = values[i]
            firsts[FIELDS * i : FIELDS * (i + 1), pl.ds(row + CHUNKS, 8), :] = values[i]
            for f in range(FIELDS):
                answers[pl.ds(part * 8 * BACK + i * FIELDS + f, 8, stride=BACK), :] = values[2 + i][f]
        return carry

    lax.fori_loop(0, CHUNKS // 8, last, 0)
    for v in range(2 * FIELDS):
        answers[pl.ds(2 * FIELDS + v, CHUNKS, stride=BACK), :] = firsts[v, per : per + CHUNKS, :]

    back_copies = [
        to_azim(answers, borders, back_rows, back_send, back_recv, o) for o in range(1, azims)
    ]
    for copy in back_copies:
        copy.start()
    own_back = own_azim(answers, borders, back_rows, 1)
    own_back.start()
    own_back.wait()
    for copy in back_copies:
        copy.wait()

    def compose(part, carry):
        at = pl.ds(pl.multiple_of(part * 8, 8), 8)

        def border(i, f):
            return borders[pl.ds(part * 8 * BACK + i * FIELDS + f, 8, stride=BACK), :]

        for f in range(FIELDS):
            outside = [border(i, f) for i in range(4)]
            for r in range(ROWS):
                value = solved[r, f, at, :]
                for i in range(4):
                    value = value - solved[r, FIELDS + i, at, :] * outside[i]
                result[f, r // 8, pl.ds(part * 64 + r % 8, 8, stride=8), :] = value
        return carry

    lax.fori_loop(0, CHUNKS // 8, compose, 0)

    def move(c, carry):
        at = pl.ds(pl.multiple_of(c * LANES, LANES), LANES)
        row = pl.multiple_of(c * 8, 8)
        for f in range(FIELDS):
            update[f, 0:8, at] = result[f, 0, pl.ds(row, 8), :] - state[f, 0:8, at]
            update[f, 8:12, at] = result[f, 1, pl.ds(row, 4), :] - state[f, 8:12, at]
        return carry

    lax.fori_loop(0, CHUNKS, move, 0, unroll=4)

    for copy in [own_land] + own_tiles + relay_own + near_land + far_land:
        copy.wait()
    for g in groups:
        mate_copy(g).wait()
        for flip in range(2):
            direct_copy(g, flip).wait()
        for u in (3, 0, 1):
            relay_copy(g, u).wait()


def finish_kernel(landing, arrived0, arrived1, update, state, fringe, out_hbm, out, rows, cells, total, places, counts, sems):
    planes = landing.shape[0]
    fetch = pltpu.make_async_copy(landing, places, sems.at[FIELDS])
    fetch.start()
    for r in range(ROWS):
        counts[r] = 0.0
    total[...] = jnp.zeros(total.shape, jnp.float32)
    fetch.wait()

    def add(slot, carry):
        d = slot // CAP
        k = slot - d * CAP
        row = places[d, 0, k]

        @pl.when(row >= 0)
        def _():
            for (low, high), source in zip(GROUPS, (arrived0, arrived1)):
                total[row, low:high] = total[row, low:high] + source[d, k]
            counts[row] = counts[row] + 1.0

        return carry

    lax.fori_loop(0, planes * CAP, add, 0)

    for b in range(2):
        line = lax.broadcasted_iota(jnp.int32, (8, LANES), 0) + 8 * b
        number = jnp.zeros((8, LANES), jnp.float32)
        for r in range(8 * b, min(8 * b + 8, ROWS)):
            number = jnp.where(line == r, counts[r], number)
        rows[2 * b] = number
        rows[2 * b + 1] = 1.0 / (number + 1.0)

    copies = []
    for f in range(FIELDS):
        for r in range(ROWS):
            cells[r // 8, pl.ds(r % 8, CHUNKS, stride=8), :] = total[r, f]

        def move(c, carry, f=f):
            at = pl.ds(pl.multiple_of(c * LANES, LANES), LANES)
            row = pl.multiple_of(c * 8, 8)
            for b, (low, high) in enumerate(((0, 8), (8, ROWS))):
                size = high - low
                q = state[f, low:high, at]
                relaxed = (cells[b, pl.ds(row, size), :] - rows[2 * b, 0:size, :] * q) * rows[
                    2 * b + 1, 0:size, :
                ]
                out[f, low:high, at] = jnp.where(
                    fringe[low:high, at] == 1, relaxed, update[f, low:high, at]
                )
            return carry

        lax.fori_loop(0, CHUNKS, move, 0, unroll=4)
        copy = pltpu.make_async_copy(out.at[f], out_hbm.at[f], sems.at[f])
        copy.start()
        copies.append(copy)
    for copy in copies:
        copy.wait()


def f32(*shape):
    return jax.ShapeDtypeStruct(shape, jnp.float32)


def local(
    state,
    speed,
    sigma,
    dissipation,
    fringe,
    destination,
    donor,
    receptor,
    offset_y,
    offset_x,
    fraction_y,
    fraction_x,
):
    azims = lax.axis_size("azim")
    planes = lax.axis_size("plane")
    vmem = pl.BlockSpec(memory_space=pltpu.VMEM)
    hbm = pl.BlockSpec(memory_space=pltpu.HBM)
    number = pltpu.VMEM
    wide0, wide1 = (high - low for low, high in GROUPS)
    arrived0, arrived1, landing_in, update = pl.pallas_call(
        functools.partial(exchange_kernel, azims, planes),
        out_shape=(
            f32(planes, CAP, wide0, CHUNKS, LANES),
            f32(planes, CAP, wide1, CHUNKS, LANES),
            jax.ShapeDtypeStruct((planes, 1, LANES), jnp.int32),
            f32(FIELDS, ROWS, CELLS),
        ),
        in_specs=[hbm] * 11,
        out_specs=(vmem,) * 4,
        scratch_shapes=[pltpu.SMEM((SLOTS,), jnp.int32)] * 5
        + [pltpu.SMEM((SLOTS,), jnp.float32)] * 2
        + [
            pltpu.SMEM((14 * CAP,), jnp.int32),
            pltpu.SMEM((2, 8, LANES), jnp.int32),
            pltpu.SMEM((2, 8, LANES), jnp.float32),
            number((FIELDS, ROWS, CELLS), jnp.float32),
            number((3, ROWS, CELLS), jnp.float32),
            number((FIELDS, 2, CHUNKS * 8, LANES), jnp.float32),
            number((FIELDS, 2 * SPREAD, LANES), jnp.float32),
            number((wide0, 2 * SPREAD, LANES), jnp.float32),
            number((wide1, 2 * SPREAD, LANES), jnp.float32),
            number((3, 2, CHUNKS * 8, LANES), jnp.float32),
            number((PLACES, CAP, wide0, CHUNKS, LANES), jnp.float32),
            number((PLACES, CAP, wide1, CHUNKS, LANES), jnp.float32),
            number((8, 1, LANES), jnp.int32),
            number((8, LANES), jnp.int32),
            number((8, LANES), jnp.float32),
            number((2, 8, LANES), jnp.int32),
            number((2, 8, LANES), jnp.float32),
            number((ROWS, COLS, CHUNKS, LANES), jnp.float32),
            number((CHUNKS * TIPS, LANES), jnp.float32),
            number((CHUNKS * TIPS, LANES), jnp.float32),
            number((TIPS, 2 * CHUNKS, LANES), jnp.float32),
            number((TIPS, 2 * CHUNKS, LANES), jnp.float32),
            number((2 * FIELDS, 2 * CHUNKS, LANES), jnp.float32),
            number((CHUNKS * BACK, LANES), jnp.float32),
            number((CHUNKS * BACK, LANES), jnp.float32),
            pltpu.SemaphoreType.DMA((7,)),
            pltpu.SemaphoreType.DMA((FIELDS + 3,)),
            pltpu.SemaphoreType.DMA((2,)),
            pltpu.SemaphoreType.DMA((2,)),
            pltpu.SemaphoreType.DMA((4,)),
            pltpu.SemaphoreType.DMA((4,)),
            pltpu.SemaphoreType.DMA((4,)),
            pltpu.SemaphoreType.DMA((2 * PLACES,)),
            pltpu.SemaphoreType.DMA((2 * PLACES,)),
            pltpu.SemaphoreType.DMA((8,)),
            pltpu.SemaphoreType.DMA((8,)),
            pltpu.SemaphoreType.DMA((azims,)),
            pltpu.SemaphoreType.DMA((azims,)),
            pltpu.SemaphoreType.DMA((azims,)),
            pltpu.SemaphoreType.DMA((azims,)),
            pltpu.SemaphoreType.DMA((8,)),
            pltpu.SemaphoreType.REGULAR,
            pltpu.SemaphoreType.REGULAR,
            pltpu.SemaphoreType.REGULAR,
        ],
        compiler_params=pltpu.CompilerParams(
            collective_id=0, has_side_effects=True, vmem_limit_bytes=40 * 2**20
        ),
        name="exchange",
    )(
        *(
            pltpu.with_memory_space_constraint(value, pltpu.HBM)
            for value in (
                destination.reshape(SLOTS),
                donor,
                receptor,
                offset_y,
                offset_x,
                fraction_y,
                fraction_x,
                state,
                speed,
                sigma,
                dissipation,
            )
        )
    )
    return pl.pallas_call(
        finish_kernel,
        out_shape=f32(FIELDS, ROWS, CELLS),
        in_specs=[vmem] * 6,
        out_specs=hbm,
        scratch_shapes=[
            number((FIELDS, ROWS, CELLS), jnp.float32),
            number((4, 8, LANES), jnp.float32),
            number((2, CHUNKS * 8, LANES), jnp.float32),
            number((ROWS, FIELDS, CHUNKS, LANES), jnp.float32),
            pltpu.SMEM((planes, 1, LANES), jnp.int32),
            pltpu.SMEM((ROWS,), jnp.float32),
            pltpu.SemaphoreType.DMA((FIELDS + 1,)),
        ],
        compiler_params=pltpu.CompilerParams(vmem_limit_bytes=32 * 2**20),
        name="finish",
    )(landing_in, arrived0, arrived1, update, state, fringe)


def solution(mesh):
    in_specs = (
        P(None, "azim", "plane"),
        P("azim", "plane"),
        P("azim", "plane"),
        P("azim", "plane"),
        P("azim", "plane"),
        P(("azim", "plane"), None),
        P(("azim", "plane")),
        P(("azim", "plane")),
        P(("azim", "plane")),
        P(("azim", "plane")),
        P(("azim", "plane")),
        P(("azim", "plane")),
    )
    out_specs = P(None, "azim", "plane")
    return jax.shard_map(local, mesh=mesh, in_specs=in_specs, out_specs=out_specs, check_vma=False)
```

```python
import functools

import jax
import jax.numpy as jnp
from jax import lax
from jax.experimental import pallas as pl
from jax.experimental.pallas import tpu as pltpu
from jax.sharding import PartitionSpec as P

TILE = 64
CAP = 4
FIELDS = 5
ROWS = 12
CELLS = TILE * TILE
LANES = 128
CHUNKS = CELLS // LANES
SLOTS = 16
COLS = FIELDS + 4
TIPS = 4 * COLS
BACK = 4 * FIELDS
MESH = pl.DeviceIdType.MESH
GROUPS = ((0, 3), (3, FIELDS))
PLACES = 8
SPREAD = CHUNKS * ROWS
TIP_ROW = {0: 0, 1: 1, ROWS - 2: 2, ROWS - 1: 3}


def spread(source, dest):
    def move(c, carry):
        lane = pl.multiple_of(c * LANES, LANES)
        row = pl.multiple_of(c * 8, 8)
        for f in range(source.shape[0]):
            dest[f, 0, pl.ds(row, 8), :] = source[f, 0:8, pl.ds(lane, LANES)]
            dest[f, 1, pl.ds(row, 4), :] = source[f, 8:12, pl.ds(lane, LANES)]
        return carry

    lax.fori_loop(0, CHUNKS, move, 0, unroll=4)


def spread_twice(source, dest):
    def move(j, carry):
        lane = pl.multiple_of(j * 2 * LANES, 2 * LANES)
        row = pl.multiple_of(j * 2 * ROWS, 8)
        value = jnp.concatenate(
            [source[:, pl.ds(lane, LANES)], source[:, pl.ds(lane + LANES, LANES)]], axis=0
        )
        dest[pl.ds(row, 2 * ROWS), :] = value
        dest[pl.ds(row + SPREAD, 2 * ROWS), :] = value
        return carry

    lax.fori_loop(0, CHUNKS // 2, move, 0, unroll=4)


def eliminate(cells, coefs, solved, tips, part):
    base = part * 64
    at = pl.ds(pl.multiple_of(part * 8, 8), 8)

    def load(ref, lead, r):
        return ref[lead, r // 8, pl.ds(base + r % 8, 8, stride=8), :]

    def load_cells(k, r):
        return cells[k, pl.ds(part * 8 * ROWS + r, 8, stride=ROWS), :]

    upper1 = []
    upper2 = []
    fields1 = fields2 = None
    for r in range(ROWS):
        c = load(coefs, 0, r)
        s = load(coefs, 1, r)
        d = load(coefs, 2, r)
        half = 0.5 * c
        common = -s - 4.0 * d
        a1 = common - half
        e1 = common + half
        centre = 1.0 + (2.0 * s + 10.0 * d)
        weight = 1.0 + 4.0 * d
        if r == 0:
            pivot, u1_top = centre, e1
        elif r == 1:
            pivot = centre - a1 * upper1[0]
            u1_top = e1 - a1 * upper2[0]
        else:
            a1 = a1 - d * upper1[r - 2]
            pivot = centre - d * upper2[r - 2] - a1 * upper1[r - 1]
            u1_top = e1 - a1 * upper2[r - 1]
        inverse = 1.0 / pivot
        upper1.append(u1_top * inverse)
        upper2.append(d * inverse)
        now = []
        for k in range(FIELDS + 2):
            if k < FIELDS:
                value = weight * load_cells(k, r)
            elif r == 0:
                now.append((d if k == FIELDS else a1) * inverse)
                continue
            elif r == 1 and k == FIELDS + 1:
                value = d
            else:
                value = None
            if r >= 1:
                term = a1 * fields1[k]
                value = -term if value is None else value - term
            if r >= 2:
                value = value - d * fields2[k]
            now.append(value * inverse)
        for k in range(FIELDS + 2):
            solved[r, k, at, :] = now[k]
        fields2, fields1 = fields1, now

    later1 = later2 = None
    for r in range(ROWS - 1, -1, -1):
        now = []
        for k in range(COLS):
            if k < FIELDS + 2:
                value = solved[r, k, at, :]
            elif r == ROWS - 1:
                value = upper1[r] if k == FIELDS + 2 else upper2[r]
            elif r == ROWS - 2 and k == FIELDS + 2:
                value = upper2[r]
            else:
                value = None
            if r < ROWS - 1:
                term = upper1[r] * later1[k]
                value = -term if value is None else value - term
            if r < ROWS - 2:
                value = value - upper2[r] * later2[k]
            now.append(value)
        for k in range(COLS):
            solved[r, k, at, :] = now[k]
        if r in TIP_ROW:
            for k in range(COLS):
                tips[pl.ds(part * 8 * TIPS + TIP_ROW[r] * COLS + k, 8, stride=TIPS), :] = now[k]
        later2, later1 = later1, now


def merge(left, right):
    def pair(matrix, columns):
        return [matrix[i][0] * columns[0] + matrix[i][1] * columns[1] for i in range(2)]

    gs = slice(0, FIELDS)
    ws = slice(FIELDS, FIELDS + 2)
    vs = slice(FIELDS + 2, FIELDS + 4)
    left_v = [[left[i][FIELDS + 2 + m] for m in range(2)] for i in range(4)]
    right_w = [[right[i][FIELDS + m] for m in range(2)] for i in range(4)]
    nothing = jnp.zeros((2,) + left[0].shape[1:], jnp.float32)
    product = [
        [sum(right_w[i][m] * left_v[2 + m][j] for m in range(2)) for j in range(2)]
        for i in range(2)
    ]
    m00, m01 = 1.0 - product[0][0], -product[0][1]
    m10, m11 = -product[1][0], 1.0 - product[1][1]
    scale = 1.0 / (m00 * m11 - m01 * m10)
    inverse = [[m11 * scale, -m01 * scale], [-m10 * scale, m00 * scale]]
    known = [jnp.concatenate([left[2 + i][gs], left[2 + i][ws]], axis=0) for i in range(2)]
    through = pair(right_w[:2], known)
    raw = [
        jnp.concatenate(
            [right[i][gs] - through[i][gs], -through[i][FIELDS:], right[i][vs]], axis=0
        )
        for i in range(2)
    ]
    inner_a = pair(inverse, raw)
    from_a = pair(left_v[2:], inner_a)
    inner_b = [
        jnp.concatenate([left[2 + i][gs], left[2 + i][ws], nothing], axis=0) - from_a[i]
        for i in range(2)
    ]
    from_a = pair(left_v[:2], inner_a)
    outer_a = [
        jnp.concatenate([left[i][gs], left[i][ws], nothing], axis=0) - from_a[i] for i in range(2)
    ]
    from_b = pair(right_w[2:], inner_b)
    outer_b = [
        jnp.concatenate([right[2 + i][gs], nothing, right[2 + i][vs]], axis=0) - from_b[i]
        for i in range(2)
    ]
    return outer_a + outer_b


def close(block):
    matrix = []
    for i in range(4):
        line = [block[i][FIELDS + 2], block[i][FIELDS + 3], block[i][FIELDS], block[i][FIELDS + 1]]
        line[i] = 1.0 + line[i]
        matrix.append(line)
    values = [block[i][0:FIELDS] for i in range(4)]
    for p in range(4):
        scale = 1.0 / matrix[p][p]
        for c in range(p + 1, 4):
            matrix[p][c] = matrix[p][c] * scale
        values[p] = values[p] * scale
        for r in range(p + 1, 4):
            for c in range(p + 1, 4):
                matrix[r][c] = matrix[r][c] - matrix[r][p] * matrix[p][c]
            values[r] = values[r] - matrix[r][p] * values[p]
    for r in range(2, -1, -1):
        for c in range(r + 1, 4):
            values[r] = values[r] - matrix[r][c] * values[c]
    return values


def exchange_kernel(
    azims,
    planes,
    destination_hbm,
    donor_hbm,
    receptor_hbm,
    offset_y_hbm,
    offset_x_hbm,
    fraction_y_hbm,
    fraction_x_hbm,
    state_hbm,
    speed_hbm,
    sigma_hbm,
    dissipation_hbm,
    arrived0,
    arrived1,
    landing_in,
    update,
    destination,
    donor,
    receptor,
    offset_y,
    offset_x,
    fraction_y,
    fraction_x,
    entries,
    integers,
    reals,
    state,
    raw_coefs,
    result,
    cells,
    cells0,
    cells1,
    coefs,
    packed0,
    packed1,
    landing,
    integers_out,
    reals_out,
    integers_in,
    reals_in,
    solved,
    tips,
    tips_in,
    ping,
    pong,
    firsts,
    answers,
    borders,
    small_sem,
    large_sem,
    raw_send,
    raw_recv,
    table_send,
    table_recv,
    table_sem,
    tile_send,
    tile_recv,
    land_send,
    land_recv,
    tips_send,
    tips_recv,
    back_send,
    back_recv,
    own_sem,
    mated,
    ready,
    go,
):
    a = lax.axis_index("azim")
    p = lax.axis_index("plane")
    per = CHUNKS // azims
    tip_rows = per * TIPS
    back_rows = per * BACK
    chips = planes // 2
    core = lax.rem(p, 2)
    groups = (0, 1)
    arrived = (arrived0, arrived1)
    packed = (packed0, packed1)
    raw_cells = (cells0, cells1)

    small = [
        pltpu.make_async_copy(source, dest, small_sem.at[i])
        for i, (source, dest) in enumerate(
            (
                (destination_hbm, destination),
                (donor_hbm, donor),
                (receptor_hbm, receptor),
                (offset_y_hbm, offset_y),
                (offset_x_hbm, offset_x),
                (fraction_y_hbm, fraction_y),
                (fraction_x_hbm, fraction_x),
            )
        )
    ]
    large = [
        pltpu.make_async_copy(source, dest, large_sem.at[i])
        for i, (source, dest) in enumerate(
            [(state_hbm.at[f], state.at[f]) for f in range(FIELDS)]
            + [
                (speed_hbm, raw_coefs.at[0]),
                (sigma_hbm, raw_coefs.at[1]),
                (dissipation_hbm, raw_coefs.at[2]),
            ]
        )
    ]
    for copy in small:
        copy.start()
    for copy in large:
        copy.start()

    barrier = pltpu.get_barrier_semaphore()
    near = [(0, 1), (1, 0), (1, 1), (chips - 1, 0), (chips - 1, 1)]

    def plane_at(ahead, flip):
        return lax.rem(p // 2 + ahead, chips) * 2 + lax.rem(p + flip, 2)

    def remote(source, dest, send, recv, there):
        return pltpu.make_async_remote_copy(
            src_ref=source,
            dst_ref=dest,
            send_sem=send,
            recv_sem=recv,
            device_id=(a, there),
            device_id_type=MESH,
        )

    onward = (1 + core * (chips - 2), chips - 1 - core * (chips - 2))
    behind = (onward[1], onward[0])

    for ahead, flip in near:

        @pl.when(lax.rem(core + flip, 2) == 1)
        def _():
            pl.semaphore_signal(
                barrier, inc=1, device_id=(a, plane_at(ahead, flip)), device_id_type=MESH
            )

    def to_azim(source, dest, rows, send, recv, o):
        there = lax.rem(a + o, azims)
        return pltpu.make_async_remote_copy(
            src_ref=source.at[pl.ds(pl.multiple_of(there * rows, 8), rows), :],
            dst_ref=dest.at[pl.ds(pl.multiple_of(a * rows, 8), rows), :],
            send_sem=send.at[o],
            recv_sem=recv.at[o],
            device_id=(there, p),
            device_id_type=MESH,
        )

    def own_azim(source, dest, rows, index):
        at = pl.ds(pl.multiple_of(a * rows, 8), rows)
        return pltpu.make_async_copy(source.at[at, :], dest.at[at, :], own_sem.at[index])

    def raw_copy(g):
        low, high = GROUPS[g]
        return remote(
            cells.at[low:high, 0:SPREAD, :],
            raw_cells[g].at[:, 0:SPREAD, :],
            raw_send.at[g],
            raw_recv.at[g],
            plane_at(onward[g], 0),
        )

    def table_copies(g):
        there = plane_at(onward[g], 0)
        return (
            remote(integers_out, integers_in.at[g], table_send.at[2 * g], table_recv.at[2 * g], there),
            remote(
                reals_out, reals_in.at[g], table_send.at[2 * g + 1], table_recv.at[2 * g + 1], there
            ),
        )

    def tile_copy(g, place, owner, ahead, flip):
        index = g * PLACES + place
        return remote(
            packed[g].at[place],
            arrived[g].at[owner],
            tile_send.at[index],
            tile_recv.at[index],
            plane_at(ahead, flip),
        )

    def land_copy(index, owner, ahead, flip):
        return remote(
            landing.at[index],
            landing_in.at[owner],
            land_send.at[index],
            land_recv.at[index],
            plane_at(ahead, flip),
        )

    def direct_copy(g, flip):
        return tile_copy(g, flip, p, behind[g], flip)

    def relay_copy(g, u):
        return tile_copy(g, 2 + u, plane_at(behind[g], 0), (1 - u // 2) * onward[g], u - 2 * (u // 2))

    def mate_copy(g):
        return tile_copy(g, 6, p, 0, 1)

    spot = lax.broadcasted_iota(jnp.int32, (1, LANES), 1)
    for copy in small:
        copy.wait()
    for line, source in enumerate((destination, donor, receptor, offset_y, offset_x)):
        value = jnp.zeros((1, LANES), jnp.int32)
        for e in range(SLOTS):
            value = jnp.where(spot == e, source[e], value)
        integers_out[line : line + 1, :] = value
    for line, source in enumerate((fraction_y, fraction_x)):
        value = jnp.zeros((1, LANES), jnp.float32)
        for e in range(SLOTS):
            value = jnp.where(spot == e, source[e], value)
        reals_out[line : line + 1, :] = value

    for f in range(FIELDS):
        large[f].wait()
        spread_twice(state.at[f], cells.at[f])

    @pl.when(core == 1)
    def _():
        pl.semaphore_wait(barrier, len(near))
        pl.semaphore_signal(mated, inc=1, device_id=(a, plane_at(0, 1)), device_id_type=MESH)
        for ahead in (1, chips - 1):
            pl.semaphore_signal(ready, inc=1, device_id=(a, plane_at(ahead, 1)), device_id_type=MESH)

    @pl.when(core == 0)
    def _():
        pl.semaphore_wait(mated, 1)
        for o in range(1, azims):
            pl.semaphore_signal(
                barrier, inc=1, device_id=(lax.rem(a + o, azims), p), device_id_type=MESH
            )
        pl.semaphore_wait(ready, 2)

    for g in groups:
        for copy in table_copies(g):
            copy.start()
    for g in groups:
        raw_copy(g).start()
    for copy in large[FIELDS:]:
        copy.wait()
    spread(raw_coefs, coefs)

    def one_part(part, carry):
        eliminate(cells, coefs, solved, tips, part)
        return carry

    lax.fori_loop(0, CHUNKS // 8, one_part, 0)

    def search(named, target, base):
        seen = jnp.int32(0)
        found = [jnp.int32(-1)] * CAP
        for e in range(SLOTS):
            match = named(e) == target
            for k in range(CAP):
                found[k] = jnp.where(match & (seen == k), e, found[k])
            seen = seen + jnp.where(match, 1, 0)
        for k in range(CAP):
            entries[base + k] = found[k]

    lane = lax.broadcasted_iota(jnp.int32, (CHUNKS, LANES), 1)
    high_half = lane >= TILE
    wide = lax.broadcasted_iota(jnp.int32, (LANES, 2 * LANES), 1)
    second = wide // LANES
    wide_lane = wide & (LANES - 1)
    from_lane = lax.broadcasted_iota(jnp.int32, (LANES, 2 * LANES), 0)

    def places_of(base, receptor_of):
        places = jnp.full((1, LANES), -1, jnp.int32)
        for k in range(CAP):
            entry = entries[base + k]
            place = jnp.where(entry >= 0, receptor_of(jnp.maximum(entry, 0)), -1)
            places = jnp.where(spot == k, place, places)
        return places

    def fill(base, table, blocks, dests):
        donor_of, oy_of, ox_of, fy_of, fx_of = table
        for k in range(CAP):
            e = jnp.maximum(entries[base + k], 0)
            row = donor_of(e)
            ox = ox_of(e)
            oy = oy_of(e)
            fx = fx_of(e)
            fy = fy_of(e)
            start = row + ROWS * (oy >> 1)
            odd = (oy & 1) == 1
            even_first = jnp.where(odd, 0.0, 1.0 - fy)
            even_second = jnp.where(odd, fy, 0.0)
            odd_weight = jnp.where(odd, 1.0 - fy, fy)
            pick = (wide_lane & TILE) + ((wide_lane + ox + second) & (TILE - 1))
            chosen = jnp.where(from_lane == pick, 1.0, 0.0).astype(jnp.bfloat16)
            values = []
            for source, f in blocks:
                here = source[f, pl.ds(start, CHUNKS, stride=ROWS), :]
                after = source[f, pl.ds(start + ROWS, CHUNKS, stride=ROWS), :]
                between = pltpu.roll(jnp.where(high_half, here, after), TILE, 1)
                values.append(even_first * here + even_second * after + odd_weight * between)
            value = jnp.concatenate(values, axis=0)
            high = value.astype(jnp.bfloat16)
            rest = value - high.astype(jnp.float32)
            middle = rest.astype(jnp.bfloat16)
            low = (rest - middle.astype(jnp.float32)).astype(jnp.bfloat16)
            moved = jnp.dot(
                jnp.concatenate([high, middle, low], axis=1),
                jnp.concatenate([chosen, chosen, chosen], axis=0),
                preferred_element_type=jnp.float32,
            )
            mixed = (1.0 - fx) * moved[:, :LANES] + fx * moved[:, LANES:]
            for n, (dest, place, f) in enumerate(dests):
                dest[place, k, f] = mixed[n * CHUNKS : (n + 1) * CHUNKS]

    own_table = tuple(
        functools.partial(lambda ref, e: ref[e], ref)
        for ref in (donor, offset_y, offset_x, fraction_y, fraction_x)
    )
    for g in groups:

        def find(flip, carry, g=g):
            search(lambda e: destination[e], plane_at(behind[g], flip), (2 * g + flip) * CAP)
            return carry

        lax.fori_loop(0, 2, find, 0)

    def find_near(flip, carry):
        search(lambda e: destination[e], plane_at(0, flip), (4 + flip) * CAP)
        return carry

    lax.fori_loop(0, 2, find_near, 0)
    for index in range(4):
        landing[index] = places_of(index * CAP, lambda e: receptor[e])
    landing[4] = places_of(5 * CAP, lambda e: receptor[e])
    landing[5] = places_of(4 * CAP, lambda e: receptor[e])
    near_land = [land_copy(2 * g + flip, p, behind[g], flip) for g in groups for flip in range(2)]
    near_land.append(land_copy(4, p, 0, 1))
    for copy in near_land:
        copy.start()
    own_land = pltpu.make_async_copy(landing.at[5], landing_in.at[p], own_sem.at[3])
    own_land.start()

    def widths(g):
        return range(GROUPS[g][1] - GROUPS[g][0])

    for g in groups:

        def fill_direct(flip, carry, g=g):
            fill(
                (2 * g + flip) * CAP,
                own_table,
                [(cells, GROUPS[g][0] + f) for f in widths(g)],
                [(packed[g], flip, f) for f in widths(g)],
            )
            return carry

        lax.fori_loop(0, 2, fill_direct, 0)

    def fill_near(flip, carry):
        fill(
            (4 + flip) * CAP,
            own_table,
            [(cells, f) for f in range(FIELDS)],
            [(packed[g], 7 - flip, f) for g in groups for f in widths(g)],
        )
        return carry

    lax.fori_loop(0, 2, fill_near, 0)
    own_tiles = [
        pltpu.make_async_copy(packed[g].at[7], arrived[g].at[p], own_sem.at[4 + g]) for g in groups
    ]
    for g in groups:
        mate_copy(g).start()
        own_tiles[g].start()

    @pl.when(core == 0)
    def _():
        pl.semaphore_wait(barrier, azims - 1)
        pl.semaphore_signal(go, inc=1, device_id=(a, plane_at(0, 1)), device_id_type=MESH)

    @pl.when(core == 1)
    def _():
        pl.semaphore_wait(go, 1)

    tip_copies = [to_azim(tips, tips_in, tip_rows, tips_send, tips_recv, o) for o in range(1, azims)]
    for copy in tip_copies:
        copy.start()
    own_tips = own_azim(tips, tips_in, tip_rows, 0)
    own_tips.start()

    for g in groups:
        raw_copy(g).wait_send()
    for flip in range(2):
        for g in groups:
            direct_copy(g, flip).start()

    fetches = []
    for g in groups:
        for copy in table_copies(g):
            copy.wait()
        fetches.append(pltpu.make_async_copy(integers_in.at[g], integers.at[g], table_sem.at[2 * g]))
        fetches.append(pltpu.make_async_copy(reals_in.at[g], reals.at[g], table_sem.at[2 * g + 1]))
    for copy in fetches:
        copy.start()
    for copy in fetches:
        copy.wait()
    for g in groups:

        def find_relay(u, carry, g=g):
            target = plane_at((1 - u // 2) * onward[g], u - 2 * (u // 2))
            search(lambda e: integers[g, 0, e], target, (6 + 4 * g + u) * CAP)
            return carry

        lax.fori_loop(0, 4, find_relay, 0)
    far_land = []
    for u in range(2):
        landing[6 + u] = places_of((6 + u) * CAP, lambda e: integers[0, 2, e])
        far_land.append(land_copy(6 + u, plane_at(behind[0], 0), onward[0], u))
        far_land[-1].start()

    relay_own = [
        pltpu.make_async_copy(
            packed[g].at[4], arrived[g].at[plane_at(behind[g], 0)], own_sem.at[6 + g]
        )
        for g in groups
    ]
    for g in groups:
        raw_copy(g).wait_recv()
        for f in widths(g):
            raw_cells[g][f, SPREAD:, :] = raw_cells[g][f, 0:SPREAD, :]
        relay_table = (
            lambda e, g=g: integers[g, 1, e],
            lambda e, g=g: integers[g, 3, e],
            lambda e, g=g: integers[g, 4, e],
            lambda e, g=g: reals[g, 0, e],
            lambda e, g=g: reals[g, 1, e],
        )

        def fill_relay(u, carry, g=g, relay_table=relay_table):
            fill(
                (6 + 4 * g + u) * CAP,
                relay_table,
                [(raw_cells[g], f) for f in widths(g)],
                [(packed[g], 2 + u, f) for f in widths(g)],
            )

            @pl.when(u != 2)
            def _():
                relay_copy(g, u).start()

            @pl.when(u == 2)
            def _():
                relay_own[g].start()

            return carry

        lax.fori_loop(0, 4, fill_relay, 0)

    own_tips.wait()
    for copy in tip_copies:
        copy.wait()

    for v in range(TIPS):
        value = tips_in[pl.ds(v, CHUNKS, stride=TIPS), :]
        ping[v, 0:CHUNKS, :] = value
        ping[v, CHUNKS : 2 * CHUNKS, :] = value

    source, dest = ping, pong
    step = 1
    while step < azims:

        def level(part, carry, source=source, dest=dest, shift=step * per):
            row = pl.multiple_of(part * 8, 8)
            left = [source[COLS * i : COLS * (i + 1), pl.ds(row, 8), :] for i in range(4)]
            right = [source[COLS * i : COLS * (i + 1), pl.ds(row + shift, 8), :] for i in range(4)]
            for i, value in enumerate(merge(left, right)):
                dest[COLS * i : COLS * (i + 1), pl.ds(row, 8), :] = value
                dest[COLS * i : COLS * (i + 1), pl.ds(row + CHUNKS, 8), :] = value
            return carry

        lax.fori_loop(0, CHUNKS // 8, level, 0)
        source, dest = dest, source
        step *= 2

    def last(part, carry):
        row = pl.multiple_of(part * 8, 8)
        block = [source[COLS * i : COLS * (i + 1), pl.ds(row, 8), :] for i in range(4)]
        values = close(block)
        for i in range(2):
            firsts[FIELDS * i : FIELDS * (i + 1), pl.ds(row, 8), :] = values[i]
            firsts[FIELDS * i : FIELDS * (i + 1), pl.ds(row + CHUNKS, 8), :] = values[i]
            for f in range(FIELDS):
                answers[pl.ds(part * 8 * BACK + i * FIELDS + f, 8, stride=BACK), :] = values[2 + i][f]
        return carry

    lax.fori_loop(0, CHUNKS // 8, last, 0)
    for v in range(2 * FIELDS):
        answers[pl.ds(2 * FIELDS + v, CHUNKS, stride=BACK), :] = firsts[v, per : per + CHUNKS, :]

    back_copies = [
        to_azim(answers, borders, back_rows, back_send, back_recv, o) for o in range(1, azims)
    ]
    for copy in back_copies:
        copy.start()
    own_back = own_azim(answers, borders, back_rows, 1)
    own_back.start()
    own_back.wait()
    for copy in back_copies:
        copy.wait()

    def compose(part, carry):
        at = pl.ds(pl.multiple_of(part * 8, 8), 8)

        def border(i, f):
            return borders[pl.ds(part * 8 * BACK + i * FIELDS + f, 8, stride=BACK), :]

        for f in range(FIELDS):
            outside = [border(i, f) for i in range(4)]
            for r in range(ROWS):
                value = solved[r, f, at, :]
                for i in range(4):
                    value = value - solved[r, FIELDS + i, at, :] * outside[i]
                result[f, r // 8, pl.ds(part * 64 + r % 8, 8, stride=8), :] = value
        return carry

    lax.fori_loop(0, CHUNKS // 8, compose, 0)

    def move(c, carry):
        at = pl.ds(pl.multiple_of(c * LANES, LANES), LANES)
        row = pl.multiple_of(c * 8, 8)
        for f in range(FIELDS):
            update[f, 0:8, at] = result[f, 0, pl.ds(row, 8), :] - state[f, 0:8, at]
            update[f, 8:12, at] = result[f, 1, pl.ds(row, 4), :] - state[f, 8:12, at]
        return carry

    lax.fori_loop(0, CHUNKS, move, 0, unroll=4)

    for copy in [own_land] + own_tiles + relay_own + near_land + far_land:
        copy.wait()
    for g in groups:
        mate_copy(g).wait()
        for flip in range(2):
            direct_copy(g, flip).wait()
        for u in (3, 0, 1):
            relay_copy(g, u).wait()


def finish_kernel(landing, arrived0, arrived1, update, state, fringe, out_hbm, out, rows, cells, total, places, counts, sems):
    planes = landing.shape[0]
    fetch = pltpu.make_async_copy(landing, places, sems.at[FIELDS])
    fetch.start()
    for r in range(ROWS):
        counts[r] = 0.0
    total[...] = jnp.zeros(total.shape, jnp.float32)
    fetch.wait()

    def add(slot, carry):
        d = slot // CAP
        k = slot - d * CAP
        row = places[d, 0, k]

        @pl.when(row >= 0)
        def _():
            for (low, high), source in zip(GROUPS, (arrived0, arrived1)):
                total[row, low:high] = total[row, low:high] + source[d, k]
            counts[row] = counts[row] + 1.0

        return carry

    lax.fori_loop(0, planes * CAP, add, 0)

    for b in range(2):
        line = lax.broadcasted_iota(jnp.int32, (8, LANES), 0) + 8 * b
        number = jnp.zeros((8, LANES), jnp.float32)
        for r in range(8 * b, min(8 * b + 8, ROWS)):
            number = jnp.where(line == r, counts[r], number)
        rows[2 * b] = number
        rows[2 * b + 1] = 1.0 / (number + 1.0)

    copies = []
    for f in range(FIELDS):
        for r in range(ROWS):
            cells[r // 8, pl.ds(r % 8, CHUNKS, stride=8), :] = total[r, f]

        def move(c, carry, f=f):
            at = pl.ds(pl.multiple_of(c * LANES, LANES), LANES)
            row = pl.multiple_of(c * 8, 8)
            for b, (low, high) in enumerate(((0, 8), (8, ROWS))):
                size = high - low
                q = state[f, low:high, at]
                relaxed = (cells[b, pl.ds(row, size), :] - rows[2 * b, 0:size, :] * q) * rows[
                    2 * b + 1, 0:size, :
                ]
                out[f, low:high, at] = jnp.where(
                    fringe[low:high, at] == 1, relaxed, update[f, low:high, at]
                )
            return carry

        lax.fori_loop(0, CHUNKS, move, 0, unroll=4)
        copy = pltpu.make_async_copy(out.at[f], out_hbm.at[f], sems.at[f])
        copy.start()
        copies.append(copy)
    for copy in copies:
        copy.wait()


def f32(*shape):
    return jax.ShapeDtypeStruct(shape, jnp.float32)


def local(
    state,
    speed,
    sigma,
    dissipation,
    fringe,
    destination,
    donor,
    receptor,
    offset_y,
    offset_x,
    fraction_y,
    fraction_x,
):
    azims = lax.axis_size("azim")
    planes = lax.axis_size("plane")
    vmem = pl.BlockSpec(memory_space=pltpu.VMEM)
    hbm = pl.BlockSpec(memory_space=pltpu.HBM)
    number = pltpu.VMEM
    wide0, wide1 = (high - low for low, high in GROUPS)
    arrived0, arrived1, landing_in, update = pl.pallas_call(
        functools.partial(exchange_kernel, azims, planes),
        out_shape=(
            f32(planes, CAP, wide0, CHUNKS, LANES),
            f32(planes, CAP, wide1, CHUNKS, LANES),
            jax.ShapeDtypeStruct((planes, 1, LANES), jnp.int32),
            f32(FIELDS, ROWS, CELLS),
        ),
        in_specs=[hbm] * 11,
        out_specs=(vmem,) * 4,
        scratch_shapes=[pltpu.SMEM((SLOTS,), jnp.int32)] * 5
        + [pltpu.SMEM((SLOTS,), jnp.float32)] * 2
        + [
            pltpu.SMEM((14 * CAP,), jnp.int32),
            pltpu.SMEM((2, 8, LANES), jnp.int32),
            pltpu.SMEM((2, 8, LANES), jnp.float32),
            number((FIELDS, ROWS, CELLS), jnp.float32),
            number((3, ROWS, CELLS), jnp.float32),
            number((FIELDS, 2, CHUNKS * 8, LANES), jnp.float32),
            number((FIELDS, 2 * SPREAD, LANES), jnp.float32),
            number((wide0, 2 * SPREAD, LANES), jnp.float32),
            number((wide1, 2 * SPREAD, LANES), jnp.float32),
            number((3, 2, CHUNKS * 8, LANES), jnp.float32),
            number((PLACES, CAP, wide0, CHUNKS, LANES), jnp.float32),
            number((PLACES, CAP, wide1, CHUNKS, LANES), jnp.float32),
            number((8, 1, LANES), jnp.int32),
            number((8, LANES), jnp.int32),
            number((8, LANES), jnp.float32),
            number((2, 8, LANES), jnp.int32),
            number((2, 8, LANES), jnp.float32),
            number((ROWS, COLS, CHUNKS, LANES), jnp.float32),
            number((CHUNKS * TIPS, LANES), jnp.float32),
            number((CHUNKS * TIPS, LANES), jnp.float32),
            number((TIPS, 2 * CHUNKS, LANES), jnp.float32),
            number((TIPS, 2 * CHUNKS, LANES), jnp.float32),
            number((2 * FIELDS, 2 * CHUNKS, LANES), jnp.float32),
            number((CHUNKS * BACK, LANES), jnp.float32),
            number((CHUNKS * BACK, LANES), jnp.float32),
            pltpu.SemaphoreType.DMA((7,)),
            pltpu.SemaphoreType.DMA((FIELDS + 3,)),
            pltpu.SemaphoreType.DMA((2,)),
            pltpu.SemaphoreType.DMA((2,)),
            pltpu.SemaphoreType.DMA((4,)),
            pltpu.SemaphoreType.DMA((4,)),
            pltpu.SemaphoreType.DMA((4,)),
            pltpu.SemaphoreType.DMA((2 * PLACES,)),
            pltpu.SemaphoreType.DMA((2 * PLACES,)),
            pltpu.SemaphoreType.DMA((8,)),
            pltpu.SemaphoreType.DMA((8,)),
            pltpu.SemaphoreType.DMA((azims,)),
            pltpu.SemaphoreType.DMA((azims,)),
            pltpu.SemaphoreType.DMA((azims,)),
            pltpu.SemaphoreType.DMA((azims,)),
            pltpu.SemaphoreType.DMA((8,)),
            pltpu.SemaphoreType.REGULAR,
            pltpu.SemaphoreType.REGULAR,
            pltpu.SemaphoreType.REGULAR,
        ],
        compiler_params=pltpu.CompilerParams(
            collective_id=0, has_side_effects=True, vmem_limit_bytes=40 * 2**20
        ),
        name="exchange",
    )(
        *(
            pltpu.with_memory_space_constraint(value, pltpu.HBM)
            for value in (
                destination.reshape(SLOTS),
                donor,
                receptor,
                offset_y,
                offset_x,
                fraction_y,
                fraction_x,
                state,
                speed,
                sigma,
                dissipation,
            )
        )
    )
    return pl.pallas_call(
        finish_kernel,
        out_shape=f32(FIELDS, ROWS, CELLS),
        in_specs=[vmem] * 6,
        out_specs=hbm,
        scratch_shapes=[
            number((FIELDS, ROWS, CELLS), jnp.float32),
            number((4, 8, LANES), jnp.float32),
            number((2, CHUNKS * 8, LANES), jnp.float32),
            number((ROWS, FIELDS, CHUNKS, LANES), jnp.float32),
            pltpu.SMEM((planes, 1, LANES), jnp.int32),
            pltpu.SMEM((ROWS,), jnp.float32),
            pltpu.SemaphoreType.DMA((FIELDS + 1,)),
        ],
        compiler_params=pltpu.CompilerParams(vmem_limit_bytes=32 * 2**20),
        name="finish",
    )(landing_in, arrived0, arrived1, update, state, fringe)


def solution(mesh):
    in_specs = (
        P(None, "azim", "plane"),
        P("azim", "plane"),
        P("azim", "plane"),
        P("azim", "plane"),
        P("azim", "plane"),
        P(("azim", "plane"), None),
        P(("azim", "plane")),
        P(("azim", "plane")),
        P(("azim", "plane")),
        P(("azim", "plane")),
        P(("azim", "plane")),
        P(("azim", "plane")),
    )
    out_specs = P(None, "azim", "plane")
    return jax.shard_map(local, mesh=mesh, in_specs=in_specs, out_specs=out_specs, check_vma=False)
```

```python
import functools

import jax
import jax.numpy as jnp
from jax import lax
from jax.experimental import pallas as pl
from jax.experimental.pallas import tpu as pltpu
from jax.sharding import PartitionSpec as P

TILE = 64
CAP = 4
FIELDS = 5
ROWS = 12
CELLS = TILE * TILE
LANES = 128
CHUNKS = CELLS // LANES
SLOTS = 16
COLS = FIELDS + 4
TIPS = 4 * COLS
BACK = 4 * FIELDS
MESH = pl.DeviceIdType.MESH
GROUPS = ((0, 3), (3, FIELDS))
PLACES = 8
SPREAD = CHUNKS * ROWS
TIP_ROW = {0: 0, 1: 1, ROWS - 2: 2, ROWS - 1: 3}


def spread(source, dest):
    def move(c, carry):
        lane = pl.multiple_of(c * LANES, LANES)
        row = pl.multiple_of(c * 8, 8)
        for f in range(source.shape[0]):
            dest[f, 0, pl.ds(row, 8), :] = source[f, 0:8, pl.ds(lane, LANES)]
            dest[f, 1, pl.ds(row, 4), :] = source[f, 8:12, pl.ds(lane, LANES)]
        return carry

    lax.fori_loop(0, CHUNKS, move, 0, unroll=4)


def spread_twice(source, dest):
    def move(j, carry):
        lane = pl.multiple_of(j * 2 * LANES, 2 * LANES)
        row = pl.multiple_of(j * 2 * ROWS, 8)
        value = jnp.concatenate(
            [source[:, pl.ds(lane, LANES)], source[:, pl.ds(lane + LANES, LANES)]], axis=0
        )
        dest[pl.ds(row, 2 * ROWS), :] = value
        dest[pl.ds(row + SPREAD, 2 * ROWS), :] = value
        return carry

    lax.fori_loop(0, CHUNKS // 2, move, 0, unroll=4)


def eliminate(cells, coefs, solved, tips, part):
    base = part * 64
    at = pl.ds(pl.multiple_of(part * 8, 8), 8)

    def load(ref, lead, r):
        return ref[lead, r // 8, pl.ds(base + r % 8, 8, stride=8), :]

    def load_cells(k, r):
        return cells[k, pl.ds(part * 8 * ROWS + r, 8, stride=ROWS), :]

    upper1 = []
    upper2 = []
    fields1 = fields2 = None
    for r in range(ROWS):
        c = load(coefs, 0, r)
        s = load(coefs, 1, r)
        d = load(coefs, 2, r)
        half = 0.5 * c
        common = -s - 4.0 * d
        a1 = common - half
        e1 = common + half
        centre = 1.0 + (2.0 * s + 10.0 * d)
        weight = 1.0 + 4.0 * d
        if r == 0:
            pivot, u1_top = centre, e1
        elif r == 1:
            pivot = centre - a1 * upper1[0]
            u1_top = e1 - a1 * upper2[0]
        else:
            a1 = a1 - d * upper1[r - 2]
            pivot = centre - d * upper2[r - 2] - a1 * upper1[r - 1]
            u1_top = e1 - a1 * upper2[r - 1]
        inverse = 1.0 / pivot
        upper1.append(u1_top * inverse)
        upper2.append(d * inverse)
        now = []
        for k in range(FIELDS + 2):
            if k < FIELDS:
                value = weight * load_cells(k, r)
            elif r == 0:
                now.append((d if k == FIELDS else a1) * inverse)
                continue
            elif r == 1 and k == FIELDS + 1:
                value = d
            else:
                value = None
            if r >= 1:
                term = a1 * fields1[k]
                value = -term if value is None else value - term
            if r >= 2:
                value = value - d * fields2[k]
            now.append(value * inverse)
        for k in range(FIELDS + 2):
            solved[r, k, at, :] = now[k]
        fields2, fields1 = fields1, now

    later1 = later2 = None
    for r in range(ROWS - 1, -1, -1):
        now = []
        for k in range(COLS):
            if k < FIELDS + 2:
                value = solved[r, k, at, :]
            elif r == ROWS - 1:
                value = upper1[r] if k == FIELDS + 2 else upper2[r]
            elif r == ROWS - 2 and k == FIELDS + 2:
                value = upper2[r]
            else:
                value = None
            if r < ROWS - 1:
                term = upper1[r] * later1[k]
                value = -term if value is None else value - term
            if r < ROWS - 2:
                value = value - upper2[r] * later2[k]
            now.append(value)
        for k in range(COLS):
            solved[r, k, at, :] = now[k]
        if r in TIP_ROW:
            for k in range(COLS):
                tips[pl.ds(part * 8 * TIPS + TIP_ROW[r] * COLS + k, 8, stride=TIPS), :] = now[k]
        later2, later1 = later1, now


def merge(left, right):
    def pair(matrix, columns):
        return [matrix[i][0] * columns[0] + matrix[i][1] * columns[1] for i in range(2)]

    gs = slice(0, FIELDS)
    ws = slice(FIELDS, FIELDS + 2)
    vs = slice(FIELDS + 2, FIELDS + 4)
    left_v = [[left[i][FIELDS + 2 + m] for m in range(2)] for i in range(4)]
    right_w = [[right[i][FIELDS + m] for m in range(2)] for i in range(4)]
    nothing = jnp.zeros((2,) + left[0].shape[1:], jnp.float32)
    product = [
        [sum(right_w[i][m] * left_v[2 + m][j] for m in range(2)) for j in range(2)]
        for i in range(2)
    ]
    m00, m01 = 1.0 - product[0][0], -product[0][1]
    m10, m11 = -product[1][0], 1.0 - product[1][1]
    scale = 1.0 / (m00 * m11 - m01 * m10)
    inverse = [[m11 * scale, -m01 * scale], [-m10 * scale, m00 * scale]]
    known = [jnp.concatenate([left[2 + i][gs], left[2 + i][ws]], axis=0) for i in range(2)]
    through = pair(right_w[:2], known)
    raw = [
        jnp.concatenate(
            [right[i][gs] - through[i][gs], -through[i][FIELDS:], right[i][vs]], axis=0
        )
        for i in range(2)
    ]
    inner_a = pair(inverse, raw)
    from_a = pair(left_v[2:], inner_a)
    inner_b = [
        jnp.concatenate([left[2 + i][gs], left[2 + i][ws], nothing], axis=0) - from_a[i]
        for i in range(2)
    ]
    from_a = pair(left_v[:2], inner_a)
    outer_a = [
        jnp.concatenate([left[i][gs], left[i][ws], nothing], axis=0) - from_a[i] for i in range(2)
    ]
    from_b = pair(right_w[2:], inner_b)
    outer_b = [
        jnp.concatenate([right[2 + i][gs], nothing, right[2 + i][vs]], axis=0) - from_b[i]
        for i in range(2)
    ]
    return outer_a + outer_b


def close(block):
    matrix = []
    for i in range(4):
        line = [block[i][FIELDS + 2], block[i][FIELDS + 3], block[i][FIELDS], block[i][FIELDS + 1]]
        line[i] = 1.0 + line[i]
        matrix.append(line)
    values = [block[i][0:FIELDS] for i in range(4)]
    for p in range(4):
        scale = 1.0 / matrix[p][p]
        for c in range(p + 1, 4):
            matrix[p][c] = matrix[p][c] * scale
        values[p] = values[p] * scale
        for r in range(p + 1, 4):
            for c in range(p + 1, 4):
                matrix[r][c] = matrix[r][c] - matrix[r][p] * matrix[p][c]
            values[r] = values[r] - matrix[r][p] * values[p]
    for r in range(2, -1, -1):
        for c in range(r + 1, 4):
            values[r] = values[r] - matrix[r][c] * values[c]
    return values


def exchange_kernel(
    azims,
    planes,
    destination_hbm,
    donor_hbm,
    receptor_hbm,
    offset_y_hbm,
    offset_x_hbm,
    fraction_y_hbm,
    fraction_x_hbm,
    state_hbm,
    speed_hbm,
    sigma_hbm,
    dissipation_hbm,
    arrived0,
    arrived1,
    landing_in,
    update,
    destination,
    donor,
    receptor,
    offset_y,
    offset_x,
    fraction_y,
    fraction_x,
    entries,
    integers,
    reals,
    state,
    raw_coefs,
    result,
    cells,
    cells0,
    cells1,
    coefs,
    packed0,
    packed1,
    landing,
    integers_out,
    reals_out,
    integers_in,
    reals_in,
    solved,
    tips,
    tips_in,
    ping,
    pong,
    firsts,
    answers,
    borders,
    small_sem,
    large_sem,
    raw_send,
    raw_recv,
    table_send,
    table_recv,
    table_sem,
    tile_send,
    tile_recv,
    land_send,
    land_recv,
    tips_send,
    tips_recv,
    back_send,
    back_recv,
    own_sem,
    mated,
    ready,
    go,
):
    a = lax.axis_index("azim")
    p = lax.axis_index("plane")
    per = CHUNKS // azims
    tip_rows = per * TIPS
    back_rows = per * BACK
    chips = planes // 2
    core = lax.rem(p, 2)
    groups = (0, 1)
    arrived = (arrived0, arrived1)
    packed = (packed0, packed1)
    raw_cells = (cells0, cells1)

    small = [
        pltpu.make_async_copy(source, dest, small_sem.at[i])
        for i, (source, dest) in enumerate(
            (
                (destination_hbm, destination),
                (donor_hbm, donor),
                (receptor_hbm, receptor),
                (offset_y_hbm, offset_y),
                (offset_x_hbm, offset_x),
                (fraction_y_hbm, fraction_y),
                (fraction_x_hbm, fraction_x),
            )
        )
    ]
    large = [
        pltpu.make_async_copy(source, dest, large_sem.at[i])
        for i, (source, dest) in enumerate(
            [(state_hbm.at[f], state.at[f]) for f in range(FIELDS)]
            + [
                (speed_hbm, raw_coefs.at[0]),
                (sigma_hbm, raw_coefs.at[1]),
                (dissipation_hbm, raw_coefs.at[2]),
            ]
        )
    ]
    for copy in small:
        copy.start()
    for copy in large:
        copy.start()

    barrier = pltpu.get_barrier_semaphore()
    near = [(0, 1), (1, 0), (1, 1), (chips - 1, 0), (chips - 1, 1)]

    def plane_at(ahead, flip):
        return lax.rem(p // 2 + ahead, chips) * 2 + lax.rem(p + flip, 2)

    def remote(source, dest, send, recv, there):
        return pltpu.make_async_remote_copy(
            src_ref=source,
            dst_ref=dest,
            send_sem=send,
            recv_sem=recv,
            device_id=(a, there),
            device_id_type=MESH,
        )

    onward = (1 + core * (chips - 2), chips - 1 - core * (chips - 2))
    behind = (onward[1], onward[0])

    for ahead, flip in near:

        @pl.when(lax.rem(core + flip, 2) == 1)
        def _():
            pl.semaphore_signal(
                barrier, inc=1, device_id=(a, plane_at(ahead, flip)), device_id_type=MESH
            )

    for o in range(1, azims):
        pl.semaphore_signal(
            barrier, inc=1, device_id=(lax.rem(a + o, azims), p - core), device_id_type=MESH
        )

    @pl.when(core == 1)
    def _():
        pl.semaphore_signal(barrier, inc=1, device_id=(a, plane_at(0, 1)), device_id_type=MESH)

    def to_azim(source, dest, rows, send, recv, o):
        there = lax.rem(a + o, azims)
        return pltpu.make_async_remote_copy(
            src_ref=source.at[pl.ds(pl.multiple_of(there * rows, 8), rows), :],
            dst_ref=dest.at[pl.ds(pl.multiple_of(a * rows, 8), rows), :],
            send_sem=send.at[o],
            recv_sem=recv.at[o],
            device_id=(there, p),
            device_id_type=MESH,
        )

    def own_azim(source, dest, rows, index):
        at = pl.ds(pl.multiple_of(a * rows, 8), rows)
        return pltpu.make_async_copy(source.at[at, :], dest.at[at, :], own_sem.at[index])

    def raw_copy(g):
        low, high = GROUPS[g]
        return remote(
            cells.at[low:high, 0:SPREAD, :],
            raw_cells[g].at[:, 0:SPREAD, :],
            raw_send.at[g],
            raw_recv.at[g],
            plane_at(onward[g], 0),
        )

    def table_copies(g):
        there = plane_at(onward[g], 0)
        return (
            remote(integers_out, integers_in.at[g], table_send.at[2 * g], table_recv.at[2 * g], there),
            remote(
                reals_out, reals_in.at[g], table_send.at[2 * g + 1], table_recv.at[2 * g + 1], there
            ),
        )

    def tile_copy(g, place, owner, ahead, flip):
        index = g * PLACES + place
        return remote(
            packed[g].at[place],
            arrived[g].at[owner],
            tile_send.at[index],
            tile_recv.at[index],
            plane_at(ahead, flip),
        )

    def land_copy(index, owner, ahead, flip):
        return remote(
            landing.at[index],
            landing_in.at[owner],
            land_send.at[index],
            land_recv.at[index],
            plane_at(ahead, flip),
        )

    def direct_copy(g, flip):
        return tile_copy(g, flip, p, behind[g], flip)

    def relay_copy(g, u):
        return tile_copy(g, 2 + u, plane_at(behind[g], 0), (1 - u // 2) * onward[g], u - 2 * (u // 2))

    def mate_copy(g):
        return tile_copy(g, 6, p, 0, 1)

    spot = lax.broadcasted_iota(jnp.int32, (1, LANES), 1)
    for copy in small:
        copy.wait()
    for line, source in enumerate((destination, donor, receptor, offset_y, offset_x)):
        value = jnp.zeros((1, LANES), jnp.int32)
        for e in range(SLOTS):
            value = jnp.where(spot == e, source[e], value)
        integers_out[line : line + 1, :] = value
    for line, source in enumerate((fraction_y, fraction_x)):
        value = jnp.zeros((1, LANES), jnp.float32)
        for e in range(SLOTS):
            value = jnp.where(spot == e, source[e], value)
        reals_out[line : line + 1, :] = value

    for f in range(FIELDS):
        large[f].wait()
        spread_twice(state.at[f], cells.at[f])

    @pl.when(core == 1)
    def _():
        pl.semaphore_wait(barrier, len(near))
        pl.semaphore_signal(mated, inc=1, device_id=(a, plane_at(0, 1)), device_id_type=MESH)
        for ahead in (1, chips - 1):
            pl.semaphore_signal(ready, inc=1, device_id=(a, plane_at(ahead, 1)), device_id_type=MESH)

    @pl.when(core == 0)
    def _():
        pl.semaphore_wait(mated, 1)
        pl.semaphore_wait(ready, 2)

    for g in groups:
        for copy in table_copies(g):
            copy.start()
    for g in groups:
        raw_copy(g).start()
    for copy in large[FIELDS:]:
        copy.wait()
    spread(raw_coefs, coefs)

    def one_part(part, carry):
        eliminate(cells, coefs, solved, tips, part)
        return carry

    lax.fori_loop(0, CHUNKS // 8, one_part, 0)

    def search(named, target, base):
        seen = jnp.int32(0)
        found = [jnp.int32(-1)] * CAP
        for e in range(SLOTS):
            match = named(e) == target
            for k in range(CAP):
                found[k] = jnp.where(match & (seen == k), e, found[k])
            seen = seen + jnp.where(match, 1, 0)
        for k in range(CAP):
            entries[base + k] = found[k]

    lane = lax.broadcasted_iota(jnp.int32, (CHUNKS, LANES), 1)
    high_half = lane >= TILE
    wide = lax.broadcasted_iota(jnp.int32, (LANES, 2 * LANES), 1)
    second = wide // LANES
    wide_lane = wide & (LANES - 1)
    from_lane = lax.broadcasted_iota(jnp.int32, (LANES, 2 * LANES), 0)

    def places_of(base, receptor_of):
        places = jnp.full((1, LANES), -1, jnp.int32)
        for k in range(CAP):
            entry = entries[base + k]
            place = jnp.where(entry >= 0, receptor_of(jnp.maximum(entry, 0)), -1)
            places = jnp.where(spot == k, place, places)
        return places

    def fill(base, table, blocks, dests):
        donor_of, oy_of, ox_of, fy_of, fx_of = table
        for k in range(CAP):
            e = jnp.maximum(entries[base + k], 0)
            row = donor_of(e)
            ox = ox_of(e)
            oy = oy_of(e)
            fx = fx_of(e)
            fy = fy_of(e)
            start = row + ROWS * (oy >> 1)
            odd = (oy & 1) == 1
            even_first = jnp.where(odd, 0.0, 1.0 - fy)
            even_second = jnp.where(odd, fy, 0.0)
            odd_weight = jnp.where(odd, 1.0 - fy, fy)
            pick = (wide_lane & TILE) + ((wide_lane + ox + second) & (TILE - 1))
            chosen = jnp.where(from_lane == pick, 1.0, 0.0).astype(jnp.bfloat16)
            values = []
            for source, f in blocks:
                here = source[f, pl.ds(start, CHUNKS, stride=ROWS), :]
                after = source[f, pl.ds(start + ROWS, CHUNKS, stride=ROWS), :]
                between = pltpu.roll(jnp.where(high_half, here, after), TILE, 1)
                values.append(even_first * here + even_second * after + odd_weight * between)
            value = jnp.concatenate(values, axis=0)
            high = value.astype(jnp.bfloat16)
            rest = value - high.astype(jnp.float32)
            middle = rest.astype(jnp.bfloat16)
            low = (rest - middle.astype(jnp.float32)).astype(jnp.bfloat16)
            moved = jnp.dot(
                jnp.concatenate([high, middle, low], axis=1),
                jnp.concatenate([chosen, chosen, chosen], axis=0),
                preferred_element_type=jnp.float32,
            )
            mixed = (1.0 - fx) * moved[:, :LANES] + fx * moved[:, LANES:]
            for n, (dest, place, f) in enumerate(dests):
                dest[place, k, f] = mixed[n * CHUNKS : (n + 1) * CHUNKS]

    own_table = tuple(
        functools.partial(lambda ref, e: ref[e], ref)
        for ref in (donor, offset_y, offset_x, fraction_y, fraction_x)
    )
    for g in groups:

        def find(flip, carry, g=g):
            search(lambda e: destination[e], plane_at(behind[g], flip), (2 * g + flip) * CAP)
            return carry

        lax.fori_loop(0, 2, find, 0)

    def find_near(flip, carry):
        search(lambda e: destination[e], plane_at(0, flip), (4 + flip) * CAP)
        return carry

    lax.fori_loop(0, 2, find_near, 0)
    for index in range(4):
        landing[index] = places_of(index * CAP, lambda e: receptor[e])
    landing[4] = places_of(5 * CAP, lambda e: receptor[e])
    landing[5] = places_of(4 * CAP, lambda e: receptor[e])
    near_land = [land_copy(2 * g + flip, p, behind[g], flip) for g in groups for flip in range(2)]
    near_land.append(land_copy(4, p, 0, 1))
    for copy in near_land:
        copy.start()
    own_land = pltpu.make_async_copy(landing.at[5], landing_in.at[p], own_sem.at[3])
    own_land.start()

    def widths(g):
        return range(GROUPS[g][1] - GROUPS[g][0])

    for g in groups:

        def fill_direct(flip, carry, g=g):
            fill(
                (2 * g + flip) * CAP,
                own_table,
                [(cells, GROUPS[g][0] + f) for f in widths(g)],
                [(packed[g], flip, f) for f in widths(g)],
            )
            return carry

        lax.fori_loop(0, 2, fill_direct, 0)

    @pl.when(core == 0)
    def _():
        pl.semaphore_wait(barrier, 2 * azims - 1)
        pl.semaphore_signal(go, inc=1, device_id=(a, plane_at(0, 1)), device_id_type=MESH)

    @pl.when(core == 1)
    def _():
        pl.semaphore_wait(go, 1)

    tip_copies = [to_azim(tips, tips_in, tip_rows, tips_send, tips_recv, o) for o in range(1, azims)]
    for copy in tip_copies:
        copy.start()
    own_tips = own_azim(tips, tips_in, tip_rows, 0)
    own_tips.start()

    def fill_near(flip, carry):
        fill(
            (4 + flip) * CAP,
            own_table,
            [(cells, f) for f in range(FIELDS)],
            [(packed[g], 7 - flip, f) for g in groups for f in widths(g)],
        )
        return carry

    lax.fori_loop(0, 2, fill_near, 0)
    own_tiles = [
        pltpu.make_async_copy(packed[g].at[7], arrived[g].at[p], own_sem.at[4 + g]) for g in groups
    ]
    for g in groups:
        mate_copy(g).start()
        own_tiles[g].start()

    for g in groups:
        raw_copy(g).wait_send()
    for flip in range(2):
        for g in groups:
            direct_copy(g, flip).start()

    fetches = []
    for g in groups:
        for copy in table_copies(g):
            copy.wait()
        fetches.append(pltpu.make_async_copy(integers_in.at[g], integers.at[g], table_sem.at[2 * g]))
        fetches.append(pltpu.make_async_copy(reals_in.at[g], reals.at[g], table_sem.at[2 * g + 1]))
    for copy in fetches:
        copy.start()
    for copy in fetches:
        copy.wait()
    for g in groups:

        def find_relay(u, carry, g=g):
            target = plane_at((1 - u // 2) * onward[g], u - 2 * (u // 2))
            search(lambda e: integers[g, 0, e], target, (6 + 4 * g + u) * CAP)
            return carry

        lax.fori_loop(0, 4, find_relay, 0)
    far_land = []
    for u in range(2):
        landing[6 + u] = places_of((6 + u) * CAP, lambda e: integers[0, 2, e])
        far_land.append(land_copy(6 + u, plane_at(behind[0], 0), onward[0], u))
        far_land[-1].start()

    relay_own = [
        pltpu.make_async_copy(
            packed[g].at[4], arrived[g].at[plane_at(behind[g], 0)], own_sem.at[6 + g]
        )
        for g in groups
    ]
    def fill_relay(g, u):
        fill(
            (6 + 4 * g + u) * CAP,
            (
                lambda e: integers[g, 1, e],
                lambda e: integers[g, 3, e],
                lambda e: integers[g, 4, e],
                lambda e: reals[g, 0, e],
                lambda e: reals[g, 1, e],
            ),
            [(raw_cells[g], f) for f in widths(g)],
            [(packed[g], 2 + u, f) for f in widths(g)],
        )

    for g in groups:
        raw_copy(g).wait_recv()
        for f in widths(g):
            raw_cells[g][f, SPREAD:, :] = raw_cells[g][f, 0:SPREAD, :]

        def fill_onward(u, carry, g=g):
            fill_relay(g, u)
            relay_copy(g, u).start()
            return carry

        lax.fori_loop(0, 2, fill_onward, 0)

    own_tips.wait()
    for copy in tip_copies:
        copy.wait()

    for v in range(TIPS):
        value = tips_in[pl.ds(v, CHUNKS, stride=TIPS), :]
        ping[v, 0:CHUNKS, :] = value
        ping[v, CHUNKS : 2 * CHUNKS, :] = value

    source, dest = ping, pong
    step = 1
    while step < azims:

        def level(part, carry, source=source, dest=dest, shift=step * per):
            row = pl.multiple_of(part * 8, 8)
            left = [source[COLS * i : COLS * (i + 1), pl.ds(row, 8), :] for i in range(4)]
            right = [source[COLS * i : COLS * (i + 1), pl.ds(row + shift, 8), :] for i in range(4)]
            for i, value in enumerate(merge(left, right)):
                dest[COLS * i : COLS * (i + 1), pl.ds(row, 8), :] = value
                dest[COLS * i : COLS * (i + 1), pl.ds(row + CHUNKS, 8), :] = value
            return carry

        lax.fori_loop(0, CHUNKS // 8, level, 0)
        source, dest = dest, source
        step *= 2

    def last(part, carry):
        row = pl.multiple_of(part * 8, 8)
        block = [source[COLS * i : COLS * (i + 1), pl.ds(row, 8), :] for i in range(4)]
        values = close(block)
        for i in range(2):
            firsts[FIELDS * i : FIELDS * (i + 1), pl.ds(row, 8), :] = values[i]
            firsts[FIELDS * i : FIELDS * (i + 1), pl.ds(row + CHUNKS, 8), :] = values[i]
            for f in range(FIELDS):
                answers[pl.ds(part * 8 * BACK + i * FIELDS + f, 8, stride=BACK), :] = values[2 + i][f]
        return carry

    lax.fori_loop(0, CHUNKS // 8, last, 0)
    for v in range(2 * FIELDS):
        answers[pl.ds(2 * FIELDS + v, CHUNKS, stride=BACK), :] = firsts[v, per : per + CHUNKS, :]

    back_copies = [
        to_azim(answers, borders, back_rows, back_send, back_recv, o) for o in range(1, azims)
    ]
    for copy in back_copies:
        copy.start()
    own_back = own_azim(answers, borders, back_rows, 1)
    own_back.start()
    for g in groups:

        def fill_chip(u, carry, g=g):
            fill_relay(g, u)
            return carry

        lax.fori_loop(2, 4, fill_chip, 0)
        relay_own[g].start()
        relay_copy(g, 3).start()

    own_back.wait()
    for copy in back_copies:
        copy.wait()

    def compose(part, carry):
        at = pl.ds(pl.multiple_of(part * 8, 8), 8)

        def border(i, f):
            return borders[pl.ds(part * 8 * BACK + i * FIELDS + f, 8, stride=BACK), :]

        for f in range(FIELDS):
            outside = [border(i, f) for i in range(4)]
            for r in range(ROWS):
                value = solved[r, f, at, :]
                for i in range(4):
                    value = value - solved[r, FIELDS + i, at, :] * outside[i]
                result[f, r // 8, pl.ds(part * 64 + r % 8, 8, stride=8), :] = value
        return carry

    lax.fori_loop(0, CHUNKS // 8, compose, 0)

    def move(c, carry):
        at = pl.ds(pl.multiple_of(c * LANES, LANES), LANES)
        row = pl.multiple_of(c * 8, 8)
        for f in range(FIELDS):
            update[f, 0:8, at] = result[f, 0, pl.ds(row, 8), :] - state[f, 0:8, at]
            update[f, 8:12, at] = result[f, 1, pl.ds(row, 4), :] - state[f, 8:12, at]
        return carry

    lax.fori_loop(0, CHUNKS, move, 0, unroll=4)

    for copy in [own_land] + own_tiles + relay_own + near_land + far_land:
        copy.wait()
    for g in groups:
        mate_copy(g).wait()
        for flip in range(2):
            direct_copy(g, flip).wait()
        for u in (3, 0, 1):
            relay_copy(g, u).wait()


def finish_kernel(landing, arrived0, arrived1, update, state, fringe, out_hbm, out, rows, cells, total, places, counts, sems):
    planes = landing.shape[0]
    fetch = pltpu.make_async_copy(landing, places, sems.at[FIELDS])
    fetch.start()
    for r in range(ROWS + 1):
        counts[r] = 0.0
    total[...] = jnp.zeros(total.shape, jnp.float32)
    fetch.wait()

    def add(slot, carry):
        d = slot // CAP
        k = slot - d * CAP
        row = places[d, 0, k]

        row = jnp.where(row >= 0, row, ROWS)
        for (low, high), source in zip(GROUPS, (arrived0, arrived1)):
            total[row, low:high] = total[row, low:high] + source[d, k]
        counts[row] = counts[row] + 1.0
        return carry

    lax.fori_loop(0, planes * CAP, add, 0, unroll=4)

    for b in range(2):
        line = lax.broadcasted_iota(jnp.int32, (8, LANES), 0) + 8 * b
        number = jnp.zeros((8, LANES), jnp.float32)
        for r in range(8 * b, min(8 * b + 8, ROWS)):
            number = jnp.where(line == r, counts[r], number)
        rows[2 * b] = number
        rows[2 * b + 1] = 1.0 / (number + 1.0)

    copies = []
    for f in range(FIELDS):
        for r in range(ROWS):
            cells[r // 8, pl.ds(r % 8, CHUNKS, stride=8), :] = total[r, f]

        def move(c, carry, f=f):
            at = pl.ds(pl.multiple_of(c * LANES, LANES), LANES)
            row = pl.multiple_of(c * 8, 8)
            for b, (low, high) in enumerate(((0, 8), (8, ROWS))):
                size = high - low
                q = state[f, low:high, at]
                relaxed = (cells[b, pl.ds(row, size), :] - rows[2 * b, 0:size, :] * q) * rows[
                    2 * b + 1, 0:size, :
                ]
                out[f, low:high, at] = jnp.where(
                    fringe[low:high, at] == 1, relaxed, update[f, low:high, at]
                )
            return carry

        lax.fori_loop(0, CHUNKS, move, 0, unroll=4)
        copy = pltpu.make_async_copy(out.at[f], out_hbm.at[f], sems.at[f])
        copy.start()
        copies.append(copy)
    for copy in copies:
        copy.wait()


def f32(*shape):
    return jax.ShapeDtypeStruct(shape, jnp.float32)


def local(
    state,
    speed,
    sigma,
    dissipation,
    fringe,
    destination,
    donor,
    receptor,
    offset_y,
    offset_x,
    fraction_y,
    fraction_x,
):
    azims = lax.axis_size("azim")
    planes = lax.axis_size("plane")
    vmem = pl.BlockSpec(memory_space=pltpu.VMEM)
    hbm = pl.BlockSpec(memory_space=pltpu.HBM)
    number = pltpu.VMEM
    wide0, wide1 = (high - low for low, high in GROUPS)
    arrived0, arrived1, landing_in, update = pl.pallas_call(
        functools.partial(exchange_kernel, azims, planes),
        out_shape=(
            f32(planes, CAP, wide0, CHUNKS, LANES),
            f32(planes, CAP, wide1, CHUNKS, LANES),
            jax.ShapeDtypeStruct((planes, 1, LANES), jnp.int32),
            f32(FIELDS, ROWS, CELLS),
        ),
        in_specs=[hbm] * 11,
        out_specs=(vmem,) * 4,
        scratch_shapes=[pltpu.SMEM((SLOTS,), jnp.int32)] * 5
        + [pltpu.SMEM((SLOTS,), jnp.float32)] * 2
        + [
            pltpu.SMEM((14 * CAP,), jnp.int32),
            pltpu.SMEM((2, 8, LANES), jnp.int32),
            pltpu.SMEM((2, 8, LANES), jnp.float32),
            number((FIELDS, ROWS, CELLS), jnp.float32),
            number((3, ROWS, CELLS), jnp.float32),
            number((FIELDS, 2, CHUNKS * 8, LANES), jnp.float32),
            number((FIELDS, 2 * SPREAD, LANES), jnp.float32),
            number((wide0, 2 * SPREAD, LANES), jnp.float32),
            number((wide1, 2 * SPREAD, LANES), jnp.float32),
            number((3, 2, CHUNKS * 8, LANES), jnp.float32),
            number((PLACES, CAP, wide0, CHUNKS, LANES), jnp.float32),
            number((PLACES, CAP, wide1, CHUNKS, LANES), jnp.float32),
            number((8, 1, LANES), jnp.int32),
            number((8, LANES), jnp.int32),
            number((8, LANES), jnp.float32),
            number((2, 8, LANES), jnp.int32),
            number((2, 8, LANES), jnp.float32),
            number((ROWS, COLS, CHUNKS, LANES), jnp.float32),
            number((CHUNKS * TIPS, LANES), jnp.float32),
            number((CHUNKS * TIPS, LANES), jnp.float32),
            number((TIPS, 2 * CHUNKS, LANES), jnp.float32),
            number((TIPS, 2 * CHUNKS, LANES), jnp.float32),
            number((2 * FIELDS, 2 * CHUNKS, LANES), jnp.float32),
            number((CHUNKS * BACK, LANES), jnp.float32),
            number((CHUNKS * BACK, LANES), jnp.float32),
            pltpu.SemaphoreType.DMA((7,)),
            pltpu.SemaphoreType.DMA((FIELDS + 3,)),
            pltpu.SemaphoreType.DMA((2,)),
            pltpu.SemaphoreType.DMA((2,)),
            pltpu.SemaphoreType.DMA((4,)),
            pltpu.SemaphoreType.DMA((4,)),
            pltpu.SemaphoreType.DMA((4,)),
            pltpu.SemaphoreType.DMA((2 * PLACES,)),
            pltpu.SemaphoreType.DMA((2 * PLACES,)),
            pltpu.SemaphoreType.DMA((8,)),
            pltpu.SemaphoreType.DMA((8,)),
            pltpu.SemaphoreType.DMA((azims,)),
            pltpu.SemaphoreType.DMA((azims,)),
            pltpu.SemaphoreType.DMA((azims,)),
            pltpu.SemaphoreType.DMA((azims,)),
            pltpu.SemaphoreType.DMA((8,)),
            pltpu.SemaphoreType.REGULAR,
            pltpu.SemaphoreType.REGULAR,
            pltpu.SemaphoreType.REGULAR,
        ],
        compiler_params=pltpu.CompilerParams(
            collective_id=0, has_side_effects=True, vmem_limit_bytes=40 * 2**20
        ),
        name="exchange",
    )(
        *(
            pltpu.with_memory_space_constraint(value, pltpu.HBM)
            for value in (
                destination.reshape(SLOTS),
                donor,
                receptor,
                offset_y,
                offset_x,
                fraction_y,
                fraction_x,
                state,
                speed,
                sigma,
                dissipation,
            )
        )
    )
    return pl.pallas_call(
        finish_kernel,
        out_shape=f32(FIELDS, ROWS, CELLS),
        in_specs=[vmem] * 6,
        out_specs=hbm,
        scratch_shapes=[
            number((FIELDS, ROWS, CELLS), jnp.float32),
            number((4, 8, LANES), jnp.float32),
            number((2, CHUNKS * 8, LANES), jnp.float32),
            number((ROWS + 1, FIELDS, CHUNKS, LANES), jnp.float32),
            pltpu.SMEM((planes, 1, LANES), jnp.int32),
            pltpu.SMEM((ROWS + 1,), jnp.float32),
            pltpu.SemaphoreType.DMA((FIELDS + 1,)),
        ],
        compiler_params=pltpu.CompilerParams(vmem_limit_bytes=32 * 2**20),
        name="finish",
    )(landing_in, arrived0, arrived1, update, state, fringe)


def solution(mesh):
    in_specs = (
        P(None, "azim", "plane"),
        P("azim", "plane"),
        P("azim", "plane"),
        P("azim", "plane"),
        P("azim", "plane"),
        P(("azim", "plane"), None),
        P(("azim", "plane")),
        P(("azim", "plane")),
        P(("azim", "plane")),
        P(("azim", "plane")),
        P(("azim", "plane")),
        P(("azim", "plane")),
    )
    out_specs = P(None, "azim", "plane")
    return jax.shard_map(local, mesh=mesh, in_specs=in_specs, out_specs=out_specs, check_vma=False)
```

```python
import functools

import jax
import jax.numpy as jnp
from jax import lax
from jax.experimental import pallas as pl
from jax.experimental.pallas import tpu as pltpu
from jax.sharding import PartitionSpec as P

TILE = 64
CAP = 4
FIELDS = 5
ROWS = 12
CELLS = TILE * TILE
LANES = 128
CHUNKS = CELLS // LANES
SLOTS = 16
COLS = FIELDS + 4
TIPS = 4 * COLS
BACK = 4 * FIELDS
MESH = pl.DeviceIdType.MESH
GROUPS = ((0, 3), (3, FIELDS))
PLACES = 8
ORDER = (0, 3, 1, 4, 2)
SPREAD = CHUNKS * ROWS
TIP_ROW = {0: 0, 1: 1, ROWS - 2: 2, ROWS - 1: 3}


def spread(source, dest):
    def move(c, carry):
        lane = pl.multiple_of(c * LANES, LANES)
        row = pl.multiple_of(c * 8, 8)
        for f in range(source.shape[0]):
            dest[f, 0, pl.ds(row, 8), :] = source[f, 0:8, pl.ds(lane, LANES)]
            dest[f, 1, pl.ds(row, 4), :] = source[f, 8:12, pl.ds(lane, LANES)]
        return carry

    lax.fori_loop(0, CHUNKS, move, 0, unroll=4)


def spread_twice(source, dest):
    def move(j, carry):
        lane = pl.multiple_of(j * 2 * LANES, 2 * LANES)
        row = pl.multiple_of(j * 2 * ROWS, 8)
        value = jnp.concatenate(
            [source[:, pl.ds(lane, LANES)], source[:, pl.ds(lane + LANES, LANES)]], axis=0
        )
        dest[pl.ds(row, 2 * ROWS), :] = value
        dest[pl.ds(row + SPREAD, 2 * ROWS), :] = value
        return carry

    lax.fori_loop(0, CHUNKS // 2, move, 0, unroll=4)


def eliminate(cells, coefs, solved, tips, part):
    base = part * 64
    at = pl.ds(pl.multiple_of(part * 8, 8), 8)

    def load(ref, lead, r):
        return ref[lead, r // 8, pl.ds(base + r % 8, 8, stride=8), :]

    def load_cells(k, r):
        return cells[k, pl.ds(part * 8 * ROWS + r, 8, stride=ROWS), :]

    upper1 = []
    upper2 = []
    fields1 = fields2 = None
    for r in range(ROWS):
        c = load(coefs, 0, r)
        s = load(coefs, 1, r)
        d = load(coefs, 2, r)
        half = 0.5 * c
        common = -s - 4.0 * d
        a1 = common - half
        e1 = common + half
        centre = 1.0 + (2.0 * s + 10.0 * d)
        weight = 1.0 + 4.0 * d
        if r == 0:
            pivot, u1_top = centre, e1
        elif r == 1:
            pivot = centre - a1 * upper1[0]
            u1_top = e1 - a1 * upper2[0]
        else:
            a1 = a1 - d * upper1[r - 2]
            pivot = centre - d * upper2[r - 2] - a1 * upper1[r - 1]
            u1_top = e1 - a1 * upper2[r - 1]
        inverse = 1.0 / pivot
        upper1.append(u1_top * inverse)
        upper2.append(d * inverse)
        now = []
        for k in range(FIELDS + 2):
            if k < FIELDS:
                value = weight * load_cells(k, r)
            elif r == 0:
                now.append((d if k == FIELDS else a1) * inverse)
                continue
            elif r == 1 and k == FIELDS + 1:
                value = d
            else:
                value = None
            if r >= 1:
                term = a1 * fields1[k]
                value = -term if value is None else value - term
            if r >= 2:
                value = value - d * fields2[k]
            now.append(value * inverse)
        for k in range(FIELDS + 2):
            solved[r, k, at, :] = now[k]
        fields2, fields1 = fields1, now

    later1 = later2 = None
    for r in range(ROWS - 1, -1, -1):
        now = []
        for k in range(COLS):
            if k < FIELDS + 2:
                value = solved[r, k, at, :]
            elif r == ROWS - 1:
                value = upper1[r] if k == FIELDS + 2 else upper2[r]
            elif r == ROWS - 2 and k == FIELDS + 2:
                value = upper2[r]
            else:
                value = None
            if r < ROWS - 1:
                term = upper1[r] * later1[k]
                value = -term if value is None else value - term
            if r < ROWS - 2:
                value = value - upper2[r] * later2[k]
            now.append(value)
        for k in range(COLS):
            solved[r, k, at, :] = now[k]
        if r in TIP_ROW:
            for k in range(COLS):
                tips[pl.ds(part * 8 * TIPS + TIP_ROW[r] * COLS + k, 8, stride=TIPS), :] = now[k]
        later2, later1 = later1, now


def merge(left, right):
    def pair(matrix, columns):
        return [matrix[i][0] * columns[0] + matrix[i][1] * columns[1] for i in range(2)]

    gs = slice(0, FIELDS)
    ws = slice(FIELDS, FIELDS + 2)
    vs = slice(FIELDS + 2, FIELDS + 4)
    left_v = [[left[i][FIELDS + 2 + m] for m in range(2)] for i in range(4)]
    right_w = [[right[i][FIELDS + m] for m in range(2)] for i in range(4)]
    nothing = jnp.zeros((2,) + left[0].shape[1:], jnp.float32)
    product = [
        [sum(right_w[i][m] * left_v[2 + m][j] for m in range(2)) for j in range(2)]
        for i in range(2)
    ]
    m00, m01 = 1.0 - product[0][0], -product[0][1]
    m10, m11 = -product[1][0], 1.0 - product[1][1]
    scale = 1.0 / (m00 * m11 - m01 * m10)
    inverse = [[m11 * scale, -m01 * scale], [-m10 * scale, m00 * scale]]
    known = [jnp.concatenate([left[2 + i][gs], left[2 + i][ws]], axis=0) for i in range(2)]
    through = pair(right_w[:2], known)
    raw = [
        jnp.concatenate(
            [right[i][gs] - through[i][gs], -through[i][FIELDS:], right[i][vs]], axis=0
        )
        for i in range(2)
    ]
    inner_a = pair(inverse, raw)
    from_a = pair(left_v[2:], inner_a)
    inner_b = [
        jnp.concatenate([left[2 + i][gs], left[2 + i][ws], nothing], axis=0) - from_a[i]
        for i in range(2)
    ]
    from_a = pair(left_v[:2], inner_a)
    outer_a = [
        jnp.concatenate([left[i][gs], left[i][ws], nothing], axis=0) - from_a[i] for i in range(2)
    ]
    from_b = pair(right_w[2:], inner_b)
    outer_b = [
        jnp.concatenate([right[2 + i][gs], nothing, right[2 + i][vs]], axis=0) - from_b[i]
        for i in range(2)
    ]
    return outer_a + outer_b


def close(block):
    matrix = []
    for i in range(4):
        line = [block[i][FIELDS + 2], block[i][FIELDS + 3], block[i][FIELDS], block[i][FIELDS + 1]]
        line[i] = 1.0 + line[i]
        matrix.append(line)
    values = [block[i][0:FIELDS] for i in range(4)]
    for p in range(4):
        scale = 1.0 / matrix[p][p]
        for c in range(p + 1, 4):
            matrix[p][c] = matrix[p][c] * scale
        values[p] = values[p] * scale
        for r in range(p + 1, 4):
            for c in range(p + 1, 4):
                matrix[r][c] = matrix[r][c] - matrix[r][p] * matrix[p][c]
            values[r] = values[r] - matrix[r][p] * values[p]
    for r in range(2, -1, -1):
        for c in range(r + 1, 4):
            values[r] = values[r] - matrix[r][c] * values[c]
    return values


def exchange_kernel(
    azims,
    planes,
    destination_hbm,
    donor_hbm,
    receptor_hbm,
    offset_y_hbm,
    offset_x_hbm,
    fraction_y_hbm,
    fraction_x_hbm,
    state_hbm,
    speed_hbm,
    sigma_hbm,
    dissipation_hbm,
    arrived0,
    arrived1,
    landing_in,
    update,
    destination,
    donor,
    receptor,
    offset_y,
    offset_x,
    fraction_y,
    fraction_x,
    entries,
    integers,
    reals,
    state,
    raw_coefs,
    result,
    cells,
    cells0,
    cells1,
    coefs,
    packed0,
    packed1,
    landing,
    integers_out,
    reals_out,
    integers_in,
    reals_in,
    solved,
    tips,
    tips_in,
    ping,
    pong,
    firsts,
    answers,
    borders,
    small_sem,
    large_sem,
    raw_send,
    raw_recv,
    table_send,
    table_recv,
    table_sem,
    tile_send,
    tile_recv,
    land_send,
    land_recv,
    tips_send,
    tips_recv,
    back_send,
    back_recv,
    own_sem,
    mated,
    ready,
    go,
):
    a = lax.axis_index("azim")
    p = lax.axis_index("plane")
    per = CHUNKS // azims
    tip_rows = per * TIPS
    back_rows = per * BACK
    chips = planes // 2
    core = lax.rem(p, 2)
    groups = (0, 1)
    arrived = (arrived0, arrived1)
    packed = (packed0, packed1)
    raw_cells = (cells0, cells1)

    small = [
        pltpu.make_async_copy(source, dest, small_sem.at[i])
        for i, (source, dest) in enumerate(
            (
                (destination_hbm, destination),
                (donor_hbm, donor),
                (receptor_hbm, receptor),
                (offset_y_hbm, offset_y),
                (offset_x_hbm, offset_x),
                (fraction_y_hbm, fraction_y),
                (fraction_x_hbm, fraction_x),
            )
        )
    ]
    large = [
        pltpu.make_async_copy(source, dest, large_sem.at[i])
        for i, (source, dest) in enumerate(
            [(state_hbm.at[f], state.at[f]) for f in range(FIELDS)]
            + [
                (speed_hbm, raw_coefs.at[0]),
                (sigma_hbm, raw_coefs.at[1]),
                (dissipation_hbm, raw_coefs.at[2]),
            ]
        )
    ]
    for copy in small:
        copy.start()
    for copy in large:
        copy.start()

    barrier = pltpu.get_barrier_semaphore()
    near = [(0, 1), (1, 0), (1, 1), (chips - 1, 0), (chips - 1, 1)]

    def plane_at(ahead, flip):
        return lax.rem(p // 2 + ahead, chips) * 2 + lax.rem(p + flip, 2)

    def remote(source, dest, send, recv, there):
        return pltpu.make_async_remote_copy(
            src_ref=source,
            dst_ref=dest,
            send_sem=send,
            recv_sem=recv,
            device_id=(a, there),
            device_id_type=MESH,
        )

    onward = (1 + core * (chips - 2), chips - 1 - core * (chips - 2))
    behind = (onward[1], onward[0])

    for ahead, flip in near:

        @pl.when(lax.rem(core + flip, 2) == 1)
        def _():
            pl.semaphore_signal(
                barrier, inc=1, device_id=(a, plane_at(ahead, flip)), device_id_type=MESH
            )

    for o in range(1, azims):
        pl.semaphore_signal(
            barrier, inc=1, device_id=(lax.rem(a + o, azims), p - core), device_id_type=MESH
        )

    @pl.when(core == 1)
    def _():
        pl.semaphore_signal(barrier, inc=1, device_id=(a, plane_at(0, 1)), device_id_type=MESH)

    def to_azim(source, dest, rows, send, recv, o):
        there = lax.rem(a + o, azims)
        return pltpu.make_async_remote_copy(
            src_ref=source.at[pl.ds(pl.multiple_of(there * rows, 8), rows), :],
            dst_ref=dest.at[pl.ds(pl.multiple_of(a * rows, 8), rows), :],
            send_sem=send.at[o],
            recv_sem=recv.at[o],
            device_id=(there, p),
            device_id_type=MESH,
        )

    def own_azim(source, dest, rows, index):
        at = pl.ds(pl.multiple_of(a * rows, 8), rows)
        return pltpu.make_async_copy(source.at[at, :], dest.at[at, :], own_sem.at[index])

    def raw_copy(f):
        g = 0 if f < GROUPS[0][1] else 1
        return remote(
            cells.at[f, 0:SPREAD, :],
            raw_cells[g].at[f - GROUPS[g][0], 0:SPREAD, :],
            raw_send.at[f],
            raw_recv.at[f],
            plane_at(onward[g], 0),
        )

    def table_copies(g):
        there = plane_at(onward[g], 0)
        return (
            remote(integers_out, integers_in.at[g], table_send.at[2 * g], table_recv.at[2 * g], there),
            remote(
                reals_out, reals_in.at[g], table_send.at[2 * g + 1], table_recv.at[2 * g + 1], there
            ),
        )

    def tile_copy(g, place, owner, ahead, flip):
        index = g * PLACES + place
        return remote(
            packed[g].at[place],
            arrived[g].at[owner],
            tile_send.at[index],
            tile_recv.at[index],
            plane_at(ahead, flip),
        )

    def land_copy(index, owner, ahead, flip):
        return remote(
            landing.at[index],
            landing_in.at[owner],
            land_send.at[index],
            land_recv.at[index],
            plane_at(ahead, flip),
        )

    def direct_copy(g, flip):
        return tile_copy(g, flip, p, behind[g], flip)

    def relay_copy(g, u):
        return tile_copy(g, 2 + u, plane_at(behind[g], 0), (1 - u // 2) * onward[g], u - 2 * (u // 2))

    def mate_copy(g):
        return tile_copy(g, 6, p, 0, 1)

    spot = lax.broadcasted_iota(jnp.int32, (1, LANES), 1)
    for copy in small:
        copy.wait()
    for line, source in enumerate((destination, donor, receptor, offset_y, offset_x)):
        value = jnp.zeros((1, LANES), jnp.int32)
        for e in range(SLOTS):
            value = jnp.where(spot == e, source[e], value)
        integers_out[line : line + 1, :] = value
    for line, source in enumerate((fraction_y, fraction_x)):
        value = jnp.zeros((1, LANES), jnp.float32)
        for e in range(SLOTS):
            value = jnp.where(spot == e, source[e], value)
        reals_out[line : line + 1, :] = value

    def send_tables():
        for g in groups:
            for copy in table_copies(g):
                copy.start()

    @pl.when(core == 1)
    def _():
        pl.semaphore_wait(barrier, len(near))
        pl.semaphore_signal(mated, inc=1, device_id=(a, plane_at(0, 1)), device_id_type=MESH)
        for ahead in (1, chips - 1):
            pl.semaphore_signal(ready, inc=1, device_id=(a, plane_at(ahead, 1)), device_id_type=MESH)
        send_tables()

    for f in ORDER:
        large[f].wait()
        spread_twice(state.at[f], cells.at[f])

        @pl.when(core == 1)
        def _():
            raw_copy(f).start()

    @pl.when(core == 0)
    def _():
        pl.semaphore_wait(mated, 1)
        pl.semaphore_wait(ready, 2)
        send_tables()
        for f in ORDER:
            raw_copy(f).start()

    for copy in large[FIELDS:]:
        copy.wait()
    spread(raw_coefs, coefs)

    def one_part(part, carry):
        eliminate(cells, coefs, solved, tips, part)
        return carry

    lax.fori_loop(0, CHUNKS // 8, one_part, 0)

    def search(named, target, base):
        seen = jnp.int32(0)
        found = [jnp.int32(-1)] * CAP
        for e in range(SLOTS):
            match = named(e) == target
            for k in range(CAP):
                found[k] = jnp.where(match & (seen == k), e, found[k])
            seen = seen + jnp.where(match, 1, 0)
        for k in range(CAP):
            entries[base + k] = found[k]

    lane = lax.broadcasted_iota(jnp.int32, (CHUNKS, LANES), 1)
    high_half = lane >= TILE
    wide = lax.broadcasted_iota(jnp.int32, (LANES, 2 * LANES), 1)
    second = wide // LANES
    wide_lane = wide & (LANES - 1)
    from_lane = lax.broadcasted_iota(jnp.int32, (LANES, 2 * LANES), 0)

    def places_of(base, receptor_of):
        places = jnp.full((1, LANES), -1, jnp.int32)
        for k in range(CAP):
            entry = entries[base + k]
            place = jnp.where(entry >= 0, receptor_of(jnp.maximum(entry, 0)), -1)
            places = jnp.where(spot == k, place, places)
        return places

    def fill(base, table, blocks, dests):
        donor_of, oy_of, ox_of, fy_of, fx_of = table
        for k in range(CAP):
            e = jnp.maximum(entries[base + k], 0)
            row = donor_of(e)
            ox = ox_of(e)
            oy = oy_of(e)
            fx = fx_of(e)
            fy = fy_of(e)
            start = row + ROWS * (oy >> 1)
            odd = (oy & 1) == 1
            even_first = jnp.where(odd, 0.0, 1.0 - fy)
            even_second = jnp.where(odd, fy, 0.0)
            odd_weight = jnp.where(odd, 1.0 - fy, fy)
            pick = (wide_lane & TILE) + ((wide_lane + ox + second) & (TILE - 1))
            chosen = jnp.where(from_lane == pick, 1.0, 0.0).astype(jnp.bfloat16)
            values = []
            for source, f in blocks:
                here = source[f, pl.ds(start, CHUNKS, stride=ROWS), :]
                after = source[f, pl.ds(start + ROWS, CHUNKS, stride=ROWS), :]
                between = pltpu.roll(jnp.where(high_half, here, after), TILE, 1)
                values.append(even_first * here + even_second * after + odd_weight * between)
            value = jnp.concatenate(values, axis=0)
            high = value.astype(jnp.bfloat16)
            rest = value - high.astype(jnp.float32)
            middle = rest.astype(jnp.bfloat16)
            low = (rest - middle.astype(jnp.float32)).astype(jnp.bfloat16)
            moved = jnp.dot(
                jnp.concatenate([high, middle, low], axis=1),
                jnp.concatenate([chosen, chosen, chosen], axis=0),
                preferred_element_type=jnp.float32,
            )
            mixed = (1.0 - fx) * moved[:, :LANES] + fx * moved[:, LANES:]
            for n, (dest, place, f) in enumerate(dests):
                dest[place, k, f] = mixed[n * CHUNKS : (n + 1) * CHUNKS]

    own_table = tuple(
        functools.partial(lambda ref, e: ref[e], ref)
        for ref in (donor, offset_y, offset_x, fraction_y, fraction_x)
    )
    for g in groups:

        def find(flip, carry, g=g):
            search(lambda e: destination[e], plane_at(behind[g], flip), (2 * g + flip) * CAP)
            return carry

        lax.fori_loop(0, 2, find, 0)

    def find_near(flip, carry):
        search(lambda e: destination[e], plane_at(0, flip), (4 + flip) * CAP)
        return carry

    lax.fori_loop(0, 2, find_near, 0)
    for index in range(4):
        landing[index] = places_of(index * CAP, lambda e: receptor[e])
    landing[4] = places_of(5 * CAP, lambda e: receptor[e])
    landing[5] = places_of(4 * CAP, lambda e: receptor[e])
    near_land = [land_copy(2 * g + flip, p, behind[g], flip) for g in groups for flip in range(2)]
    near_land.append(land_copy(4, p, 0, 1))
    for copy in near_land:
        copy.start()
    own_land = pltpu.make_async_copy(landing.at[5], landing_in.at[p], own_sem.at[3])
    own_land.start()

    def widths(g):
        return range(GROUPS[g][1] - GROUPS[g][0])

    for g in groups:

        def fill_direct(flip, carry, g=g):
            fill(
                (2 * g + flip) * CAP,
                own_table,
                [(cells, GROUPS[g][0] + f) for f in widths(g)],
                [(packed[g], flip, f) for f in widths(g)],
            )
            return carry

        lax.fori_loop(0, 2, fill_direct, 0)

    @pl.when(core == 0)
    def _():
        pl.semaphore_wait(barrier, 2 * azims - 1)
        pl.semaphore_signal(go, inc=1, device_id=(a, plane_at(0, 1)), device_id_type=MESH)

    @pl.when(core == 1)
    def _():
        pl.semaphore_wait(go, 1)

    tip_copies = [to_azim(tips, tips_in, tip_rows, tips_send, tips_recv, o) for o in range(1, azims)]
    for copy in tip_copies:
        copy.start()
    own_tips = own_azim(tips, tips_in, tip_rows, 0)
    own_tips.start()

    def fill_near(flip, carry):
        fill(
            (4 + flip) * CAP,
            own_table,
            [(cells, f) for f in range(FIELDS)],
            [(packed[g], 7 - flip, f) for g in groups for f in widths(g)],
        )
        return carry

    lax.fori_loop(0, 2, fill_near, 0)
    own_tiles = [
        pltpu.make_async_copy(packed[g].at[7], arrived[g].at[p], own_sem.at[4 + g]) for g in groups
    ]
    for g in groups:
        mate_copy(g).start()
        own_tiles[g].start()

    for f in ORDER:
        raw_copy(f).wait_send()
    for flip in range(2):
        for g in groups:
            direct_copy(g, flip).start()

    fetches = []
    for g in groups:
        for copy in table_copies(g):
            copy.wait()
        fetches.append(pltpu.make_async_copy(integers_in.at[g], integers.at[g], table_sem.at[2 * g]))
        fetches.append(pltpu.make_async_copy(reals_in.at[g], reals.at[g], table_sem.at[2 * g + 1]))
    for copy in fetches:
        copy.start()
    for copy in fetches:
        copy.wait()
    for g in groups:

        def find_relay(u, carry, g=g):
            target = plane_at((1 - u // 2) * onward[g], u - 2 * (u // 2))
            search(lambda e: integers[g, 0, e], target, (6 + 4 * g + u) * CAP)
            return carry

        lax.fori_loop(0, 4, find_relay, 0)
    far_land = []
    for u in range(2):
        landing[6 + u] = places_of((6 + u) * CAP, lambda e: integers[0, 2, e])
        far_land.append(land_copy(6 + u, plane_at(behind[0], 0), onward[0], u))
        far_land[-1].start()

    relay_own = [
        pltpu.make_async_copy(
            packed[g].at[4], arrived[g].at[plane_at(behind[g], 0)], own_sem.at[6 + g]
        )
        for g in groups
    ]
    def fill_relay(g, u):
        fill(
            (6 + 4 * g + u) * CAP,
            (
                lambda e: integers[g, 1, e],
                lambda e: integers[g, 3, e],
                lambda e: integers[g, 4, e],
                lambda e: reals[g, 0, e],
                lambda e: reals[g, 1, e],
            ),
            [(raw_cells[g], f) for f in widths(g)],
            [(packed[g], 2 + u, f) for f in widths(g)],
        )

    for g in groups:
        for f in widths(g):
            raw_copy(GROUPS[g][0] + f).wait_recv()
            raw_cells[g][f, SPREAD:, :] = raw_cells[g][f, 0:SPREAD, :]

        def fill_onward(u, carry, g=g):
            fill_relay(g, u)
            relay_copy(g, u).start()
            return carry

        lax.fori_loop(0, 2, fill_onward, 0)

    own_tips.wait()
    for copy in tip_copies:
        copy.wait()

    for v in range(TIPS):
        value = tips_in[pl.ds(v, CHUNKS, stride=TIPS), :]
        ping[v, 0:CHUNKS, :] = value
        ping[v, CHUNKS : 2 * CHUNKS, :] = value

    source, dest = ping, pong
    step = 1
    while step < azims:

        def level(part, carry, source=source, dest=dest, shift=step * per):
            row = pl.multiple_of(part * 8, 8)
            left = [source[COLS * i : COLS * (i + 1), pl.ds(row, 8), :] for i in range(4)]
            right = [source[COLS * i : COLS * (i + 1), pl.ds(row + shift, 8), :] for i in range(4)]
            for i, value in enumerate(merge(left, right)):
                dest[COLS * i : COLS * (i + 1), pl.ds(row, 8), :] = value
                dest[COLS * i : COLS * (i + 1), pl.ds(row + CHUNKS, 8), :] = value
            return carry

        lax.fori_loop(0, CHUNKS // 8, level, 0)
        source, dest = dest, source
        step *= 2

    def last(part, carry):
        row = pl.multiple_of(part * 8, 8)
        block = [source[COLS * i : COLS * (i + 1), pl.ds(row, 8), :] for i in range(4)]
        values = close(block)
        for i in range(2):
            firsts[FIELDS * i : FIELDS * (i + 1), pl.ds(row, 8), :] = values[i]
            firsts[FIELDS * i : FIELDS * (i + 1), pl.ds(row + CHUNKS, 8), :] = values[i]
            for f in range(FIELDS):
                answers[pl.ds(part * 8 * BACK + i * FIELDS + f, 8, stride=BACK), :] = values[2 + i][f]
        return carry

    lax.fori_loop(0, CHUNKS // 8, last, 0)
    for v in range(2 * FIELDS):
        answers[pl.ds(2 * FIELDS + v, CHUNKS, stride=BACK), :] = firsts[v, per : per + CHUNKS, :]

    back_copies = [
        to_azim(answers, borders, back_rows, back_send, back_recv, o) for o in range(1, azims)
    ]
    for copy in back_copies:
        copy.start()
    own_back = own_azim(answers, borders, back_rows, 1)
    own_back.start()
    for g in groups:

        def fill_chip(u, carry, g=g):
            fill_relay(g, u)
            return carry

        lax.fori_loop(2, 4, fill_chip, 0)
        relay_own[g].start()
        relay_copy(g, 3).start()

    own_back.wait()
    for copy in back_copies:
        copy.wait()

    def compose(part, carry):
        at = pl.ds(pl.multiple_of(part * 8, 8), 8)

        def border(i, f):
            return borders[pl.ds(part * 8 * BACK + i * FIELDS + f, 8, stride=BACK), :]

        for f in range(FIELDS):
            outside = [border(i, f) for i in range(4)]
            for r in range(ROWS):
                value = solved[r, f, at, :]
                for i in range(4):
                    value = value - solved[r, FIELDS + i, at, :] * outside[i]
                result[f, r // 8, pl.ds(part * 64 + r % 8, 8, stride=8), :] = value
        return carry

    lax.fori_loop(0, CHUNKS // 8, compose, 0)

    def move(c, carry):
        at = pl.ds(pl.multiple_of(c * LANES, LANES), LANES)
        row = pl.multiple_of(c * 8, 8)
        for f in range(FIELDS):
            update[f, 0:8, at] = result[f, 0, pl.ds(row, 8), :] - state[f, 0:8, at]
            update[f, 8:12, at] = result[f, 1, pl.ds(row, 4), :] - state[f, 8:12, at]
        return carry

    lax.fori_loop(0, CHUNKS, move, 0, unroll=4)

    for copy in [own_land] + own_tiles + relay_own + near_land + far_land:
        copy.wait()
    for g in groups:
        mate_copy(g).wait()
        for flip in range(2):
            direct_copy(g, flip).wait()
        for u in (3, 0, 1):
            relay_copy(g, u).wait()


def finish_kernel(landing, arrived0, arrived1, update, state, fringe, out_hbm, out, rows, cells, total, places, counts, sems):
    planes = landing.shape[0]
    fetch = pltpu.make_async_copy(landing, places, sems.at[FIELDS])
    fetch.start()
    for r in range(ROWS + 1):
        counts[r] = 0.0
    total[...] = jnp.zeros(total.shape, jnp.float32)
    fetch.wait()

    def add(slot, carry):
        d = slot // CAP
        k = slot - d * CAP
        row = places[d, 0, k]

        row = jnp.where(row >= 0, row, ROWS)
        for (low, high), source in zip(GROUPS, (arrived0, arrived1)):
            total[row, low:high] = total[row, low:high] + source[d, k]
        counts[row] = counts[row] + 1.0
        return carry

    lax.fori_loop(0, planes * CAP, add, 0, unroll=4)

    for b in range(2):
        line = lax.broadcasted_iota(jnp.int32, (8, LANES), 0) + 8 * b
        number = jnp.zeros((8, LANES), jnp.float32)
        for r in range(8 * b, min(8 * b + 8, ROWS)):
            number = jnp.where(line == r, counts[r], number)
        rows[2 * b] = number
        rows[2 * b + 1] = 1.0 / (number + 1.0)

    copies = []
    for f in range(FIELDS):
        for r in range(ROWS):
            cells[r // 8, pl.ds(r % 8, CHUNKS, stride=8), :] = total[r, f]

        def move(c, carry, f=f):
            at = pl.ds(pl.multiple_of(c * LANES, LANES), LANES)
            row = pl.multiple_of(c * 8, 8)
            for b, (low, high) in enumerate(((0, 8), (8, ROWS))):
                size = high - low
                q = state[f, low:high, at]
                relaxed = (cells[b, pl.ds(row, size), :] - rows[2 * b, 0:size, :] * q) * rows[
                    2 * b + 1, 0:size, :
                ]
                out[f, low:high, at] = jnp.where(
                    fringe[low:high, at] == 1, relaxed, update[f, low:high, at]
                )
            return carry

        lax.fori_loop(0, CHUNKS, move, 0, unroll=4)
        copy = pltpu.make_async_copy(out.at[f], out_hbm.at[f], sems.at[f])
        copy.start()
        copies.append(copy)
    for copy in copies:
        copy.wait()


def f32(*shape):
    return jax.ShapeDtypeStruct(shape, jnp.float32)


def local(
    state,
    speed,
    sigma,
    dissipation,
    fringe,
    destination,
    donor,
    receptor,
    offset_y,
    offset_x,
    fraction_y,
    fraction_x,
):
    azims = lax.axis_size("azim")
    planes = lax.axis_size("plane")
    vmem = pl.BlockSpec(memory_space=pltpu.VMEM)
    hbm = pl.BlockSpec(memory_space=pltpu.HBM)
    number = pltpu.VMEM
    wide0, wide1 = (high - low for low, high in GROUPS)
    arrived0, arrived1, landing_in, update = pl.pallas_call(
        functools.partial(exchange_kernel, azims, planes),
        out_shape=(
            f32(planes, CAP, wide0, CHUNKS, LANES),
            f32(planes, CAP, wide1, CHUNKS, LANES),
            jax.ShapeDtypeStruct((planes, 1, LANES), jnp.int32),
            f32(FIELDS, ROWS, CELLS),
        ),
        in_specs=[hbm] * 11,
        out_specs=(vmem,) * 4,
        scratch_shapes=[pltpu.SMEM((SLOTS,), jnp.int32)] * 5
        + [pltpu.SMEM((SLOTS,), jnp.float32)] * 2
        + [
            pltpu.SMEM((14 * CAP,), jnp.int32),
            pltpu.SMEM((2, 8, LANES), jnp.int32),
            pltpu.SMEM((2, 8, LANES), jnp.float32),
            number((FIELDS, ROWS, CELLS), jnp.float32),
            number((3, ROWS, CELLS), jnp.float32),
            number((FIELDS, 2, CHUNKS * 8, LANES), jnp.float32),
            number((FIELDS, 2 * SPREAD, LANES), jnp.float32),
            number((wide0, 2 * SPREAD, LANES), jnp.float32),
            number((wide1, 2 * SPREAD, LANES), jnp.float32),
            number((3, 2, CHUNKS * 8, LANES), jnp.float32),
            number((PLACES, CAP, wide0, CHUNKS, LANES), jnp.float32),
            number((PLACES, CAP, wide1, CHUNKS, LANES), jnp.float32),
            number((8, 1, LANES), jnp.int32),
            number((8, LANES), jnp.int32),
            number((8, LANES), jnp.float32),
            number((2, 8, LANES), jnp.int32),
            number((2, 8, LANES), jnp.float32),
            number((ROWS, COLS, CHUNKS, LANES), jnp.float32),
            number((CHUNKS * TIPS, LANES), jnp.float32),
            number((CHUNKS * TIPS, LANES), jnp.float32),
            number((TIPS, 2 * CHUNKS, LANES), jnp.float32),
            number((TIPS, 2 * CHUNKS, LANES), jnp.float32),
            number((2 * FIELDS, 2 * CHUNKS, LANES), jnp.float32),
            number((CHUNKS * BACK, LANES), jnp.float32),
            number((CHUNKS * BACK, LANES), jnp.float32),
            pltpu.SemaphoreType.DMA((7,)),
            pltpu.SemaphoreType.DMA((FIELDS + 3,)),
            pltpu.SemaphoreType.DMA((FIELDS,)),
            pltpu.SemaphoreType.DMA((FIELDS,)),
            pltpu.SemaphoreType.DMA((4,)),
            pltpu.SemaphoreType.DMA((4,)),
            pltpu.SemaphoreType.DMA((4,)),
            pltpu.SemaphoreType.DMA((2 * PLACES,)),
            pltpu.SemaphoreType.DMA((2 * PLACES,)),
            pltpu.SemaphoreType.DMA((8,)),
            pltpu.SemaphoreType.DMA((8,)),
            pltpu.SemaphoreType.DMA((azims,)),
            pltpu.SemaphoreType.DMA((azims,)),
            pltpu.SemaphoreType.DMA((azims,)),
            pltpu.SemaphoreType.DMA((azims,)),
            pltpu.SemaphoreType.DMA((8,)),
            pltpu.SemaphoreType.REGULAR,
            pltpu.SemaphoreType.REGULAR,
            pltpu.SemaphoreType.REGULAR,
        ],
        compiler_params=pltpu.CompilerParams(
            collective_id=0, has_side_effects=True, vmem_limit_bytes=40 * 2**20
        ),
        name="exchange",
    )(
        *(
            pltpu.with_memory_space_constraint(value, pltpu.HBM)
            for value in (
                destination.reshape(SLOTS),
                donor,
                receptor,
                offset_y,
                offset_x,
                fraction_y,
                fraction_x,
                state,
                speed,
                sigma,
                dissipation,
            )
        )
    )
    return pl.pallas_call(
        finish_kernel,
        out_shape=f32(FIELDS, ROWS, CELLS),
        in_specs=[vmem] * 6,
        out_specs=hbm,
        scratch_shapes=[
            number((FIELDS, ROWS, CELLS), jnp.float32),
            number((4, 8, LANES), jnp.float32),
            number((2, CHUNKS * 8, LANES), jnp.float32),
            number((ROWS + 1, FIELDS, CHUNKS, LANES), jnp.float32),
            pltpu.SMEM((planes, 1, LANES), jnp.int32),
            pltpu.SMEM((ROWS + 1,), jnp.float32),
            pltpu.SemaphoreType.DMA((FIELDS + 1,)),
        ],
        compiler_params=pltpu.CompilerParams(vmem_limit_bytes=32 * 2**20),
        name="finish",
    )(landing_in, arrived0, arrived1, update, state, fringe)


def solution(mesh):
    in_specs = (
        P(None, "azim", "plane"),
        P("azim", "plane"),
        P("azim", "plane"),
        P("azim", "plane"),
        P("azim", "plane"),
        P(("azim", "plane"), None),
        P(("azim", "plane")),
        P(("azim", "plane")),
        P(("azim", "plane")),
        P(("azim", "plane")),
        P(("azim", "plane")),
        P(("azim", "plane")),
    )
    out_specs = P(None, "azim", "plane")
    return jax.shard_map(local, mesh=mesh, in_specs=in_specs, out_specs=out_specs, check_vma=False)
```

```python
import functools

import jax
import jax.numpy as jnp
from jax import lax
from jax.experimental import pallas as pl
from jax.experimental.pallas import tpu as pltpu
from jax.sharding import PartitionSpec as P

TILE = 64
CAP = 4
FIELDS = 5
ROWS = 12
CELLS = TILE * TILE
LANES = 128
CHUNKS = CELLS // LANES
SLOTS = 16
COLS = FIELDS + 4
TIPS = 4 * COLS
BACK = 4 * FIELDS
MESH = pl.DeviceIdType.MESH
GROUPS = ((0, 3), (3, FIELDS))
PLACES = 8
ORDER = (0, 3, 1, 4, 2)
SPREAD = CHUNKS * ROWS
TIP_ROW = {0: 0, 1: 1, ROWS - 2: 2, ROWS - 1: 3}


def spread(source, dest):
    def move(c, carry):
        lane = pl.multiple_of(c * LANES, LANES)
        row = pl.multiple_of(c * 8, 8)
        for f in range(source.shape[0]):
            dest[f, 0, pl.ds(row, 8), :] = source[f, 0:8, pl.ds(lane, LANES)]
            dest[f, 1, pl.ds(row, 4), :] = source[f, 8:12, pl.ds(lane, LANES)]
        return carry

    lax.fori_loop(0, CHUNKS, move, 0, unroll=4)


def spread_twice(source, dest):
    def move(j, carry):
        lane = pl.multiple_of(j * 2 * LANES, 2 * LANES)
        row = pl.multiple_of(j * 2 * ROWS, 8)
        value = jnp.concatenate(
            [source[:, pl.ds(lane, LANES)], source[:, pl.ds(lane + LANES, LANES)]], axis=0
        )
        dest[pl.ds(row, 2 * ROWS), :] = value
        dest[pl.ds(row + SPREAD, 2 * ROWS), :] = value
        return carry

    lax.fori_loop(0, CHUNKS // 2, move, 0, unroll=4)


def eliminate(cells, coefs, solved, tips, part):
    base = part * 64
    at = pl.ds(pl.multiple_of(part * 8, 8), 8)

    def load(ref, lead, r):
        return ref[lead, r // 8, pl.ds(base + r % 8, 8, stride=8), :]

    def load_cells(k, r):
        return cells[k, pl.ds(part * 8 * ROWS + r, 8, stride=ROWS), :]

    upper1 = []
    upper2 = []
    fields1 = fields2 = None
    for r in range(ROWS):
        c = load(coefs, 0, r)
        s = load(coefs, 1, r)
        d = load(coefs, 2, r)
        half = 0.5 * c
        common = -s - 4.0 * d
        a1 = common - half
        e1 = common + half
        centre = 1.0 + (2.0 * s + 10.0 * d)
        weight = 1.0 + 4.0 * d
        if r == 0:
            pivot, u1_top = centre, e1
        elif r == 1:
            pivot = centre - a1 * upper1[0]
            u1_top = e1 - a1 * upper2[0]
        else:
            a1 = a1 - d * upper1[r - 2]
            pivot = centre - d * upper2[r - 2] - a1 * upper1[r - 1]
            u1_top = e1 - a1 * upper2[r - 1]
        inverse = 1.0 / pivot
        upper1.append(u1_top * inverse)
        upper2.append(d * inverse)
        now = []
        for k in range(FIELDS + 2):
            if k < FIELDS:
                value = weight * load_cells(k, r)
            elif r == 0:
                now.append((d if k == FIELDS else a1) * inverse)
                continue
            elif r == 1 and k == FIELDS + 1:
                value = d
            else:
                value = None
            if r >= 1:
                term = a1 * fields1[k]
                value = -term if value is None else value - term
            if r >= 2:
                value = value - d * fields2[k]
            now.append(value * inverse)
        for k in range(FIELDS + 2):
            solved[r, k, at, :] = now[k]
        fields2, fields1 = fields1, now

    later1 = later2 = None
    for r in range(ROWS - 1, -1, -1):
        now = []
        for k in range(COLS):
            if k < FIELDS + 2:
                value = solved[r, k, at, :]
            elif r == ROWS - 1:
                value = upper1[r] if k == FIELDS + 2 else upper2[r]
            elif r == ROWS - 2 and k == FIELDS + 2:
                value = upper2[r]
            else:
                value = None
            if r < ROWS - 1:
                term = upper1[r] * later1[k]
                value = -term if value is None else value - term
            if r < ROWS - 2:
                value = value - upper2[r] * later2[k]
            now.append(value)
        for k in range(COLS):
            solved[r, k, at, :] = now[k]
        if r in TIP_ROW:
            for k in range(COLS):
                tips[pl.ds(part * 8 * TIPS + TIP_ROW[r] * COLS + k, 8, stride=TIPS), :] = now[k]
        later2, later1 = later1, now


def merge(left, right):
    def pair(matrix, columns):
        return [matrix[i][0] * columns[0] + matrix[i][1] * columns[1] for i in range(2)]

    gs = slice(0, FIELDS)
    ws = slice(FIELDS, FIELDS + 2)
    vs = slice(FIELDS + 2, FIELDS + 4)
    left_v = [[left[i][FIELDS + 2 + m] for m in range(2)] for i in range(4)]
    right_w = [[right[i][FIELDS + m] for m in range(2)] for i in range(4)]
    nothing = jnp.zeros((2,) + left[0].shape[1:], jnp.float32)
    product = [
        [sum(right_w[i][m] * left_v[2 + m][j] for m in range(2)) for j in range(2)]
        for i in range(2)
    ]
    m00, m01 = 1.0 - product[0][0], -product[0][1]
    m10, m11 = -product[1][0], 1.0 - product[1][1]
    scale = 1.0 / (m00 * m11 - m01 * m10)
    inverse = [[m11 * scale, -m01 * scale], [-m10 * scale, m00 * scale]]
    known = [jnp.concatenate([left[2 + i][gs], left[2 + i][ws]], axis=0) for i in range(2)]
    through = pair(right_w[:2], known)
    raw = [
        jnp.concatenate(
            [right[i][gs] - through[i][gs], -through[i][FIELDS:], right[i][vs]], axis=0
        )
        for i in range(2)
    ]
    inner_a = pair(inverse, raw)
    from_a = pair(left_v[2:], inner_a)
    inner_b = [
        jnp.concatenate([left[2 + i][gs], left[2 + i][ws], nothing], axis=0) - from_a[i]
        for i in range(2)
    ]
    from_a = pair(left_v[:2], inner_a)
    outer_a = [
        jnp.concatenate([left[i][gs], left[i][ws], nothing], axis=0) - from_a[i] for i in range(2)
    ]
    from_b = pair(right_w[2:], inner_b)
    outer_b = [
        jnp.concatenate([right[2 + i][gs], nothing, right[2 + i][vs]], axis=0) - from_b[i]
        for i in range(2)
    ]
    return outer_a + outer_b


def close(block):
    matrix = []
    for i in range(4):
        line = [block[i][FIELDS + 2], block[i][FIELDS + 3], block[i][FIELDS], block[i][FIELDS + 1]]
        line[i] = 1.0 + line[i]
        matrix.append(line)
    values = [block[i][0:FIELDS] for i in range(4)]
    for p in range(4):
        scale = 1.0 / matrix[p][p]
        for c in range(p + 1, 4):
            matrix[p][c] = matrix[p][c] * scale
        values[p] = values[p] * scale
        for r in range(p + 1, 4):
            for c in range(p + 1, 4):
                matrix[r][c] = matrix[r][c] - matrix[r][p] * matrix[p][c]
            values[r] = values[r] - matrix[r][p] * values[p]
    for r in range(2, -1, -1):
        for c in range(r + 1, 4):
            values[r] = values[r] - matrix[r][c] * values[c]
    return values


def exchange_kernel(
    azims,
    planes,
    destination_hbm,
    donor_hbm,
    receptor_hbm,
    offset_y_hbm,
    offset_x_hbm,
    fraction_y_hbm,
    fraction_x_hbm,
    state_hbm,
    speed_hbm,
    sigma_hbm,
    dissipation_hbm,
    arrived0,
    arrived1,
    landing_in,
    update,
    destination,
    donor,
    receptor,
    offset_y,
    offset_x,
    fraction_y,
    fraction_x,
    entries,
    integers,
    reals,
    state,
    raw_coefs,
    result,
    cells,
    cells0,
    cells1,
    coefs,
    packed0,
    packed1,
    landing,
    integers_out,
    reals_out,
    integers_in,
    reals_in,
    solved,
    tips,
    tips_in,
    ping,
    pong,
    firsts,
    answers,
    borders,
    small_sem,
    large_sem,
    raw_send,
    raw_recv,
    table_send,
    table_recv,
    table_sem,
    tile_send,
    tile_recv,
    land_send,
    land_recv,
    tips_send,
    tips_recv,
    back_send,
    back_recv,
    own_sem,
    mated,
    ready,
    go,
):
    a = lax.axis_index("azim")
    p = lax.axis_index("plane")
    per = CHUNKS // azims
    tip_rows = per * TIPS
    back_rows = per * BACK
    chips = planes // 2
    core = lax.rem(p, 2)
    groups = (0, 1)
    arrived = (arrived0, arrived1)
    packed = (packed0, packed1)
    raw_cells = (cells0, cells1)

    small = [
        pltpu.make_async_copy(source, dest, small_sem.at[i])
        for i, (source, dest) in enumerate(
            (
                (destination_hbm, destination),
                (donor_hbm, donor),
                (receptor_hbm, receptor),
                (offset_y_hbm, offset_y),
                (offset_x_hbm, offset_x),
                (fraction_y_hbm, fraction_y),
                (fraction_x_hbm, fraction_x),
            )
        )
    ]
    large = [
        pltpu.make_async_copy(source, dest, large_sem.at[i])
        for i, (source, dest) in enumerate(
            [(state_hbm.at[f], state.at[f]) for f in range(FIELDS)]
            + [
                (speed_hbm, raw_coefs.at[0]),
                (sigma_hbm, raw_coefs.at[1]),
                (dissipation_hbm, raw_coefs.at[2]),
            ]
        )
    ]
    for copy in small:
        copy.start()
    for copy in large:
        copy.start()

    barrier = pltpu.get_barrier_semaphore()
    near = [(0, 1), (1, 0), (1, 1), (chips - 1, 0), (chips - 1, 1)]

    def plane_at(ahead, flip):
        return lax.rem(p // 2 + ahead, chips) * 2 + lax.rem(p + flip, 2)

    def remote(source, dest, send, recv, there):
        return pltpu.make_async_remote_copy(
            src_ref=source,
            dst_ref=dest,
            send_sem=send,
            recv_sem=recv,
            device_id=(a, there),
            device_id_type=MESH,
        )

    onward = (1 + core * (chips - 2), chips - 1 - core * (chips - 2))
    behind = (onward[1], onward[0])

    for ahead, flip in near:

        @pl.when(lax.rem(core + flip, 2) == 1)
        def _():
            pl.semaphore_signal(
                barrier, inc=1, device_id=(a, plane_at(ahead, flip)), device_id_type=MESH
            )

    for o in range(1, azims):
        pl.semaphore_signal(
            barrier, inc=1, device_id=(lax.rem(a + o, azims), p - core), device_id_type=MESH
        )

    @pl.when(core == 1)
    def _():
        pl.semaphore_signal(barrier, inc=1, device_id=(a, plane_at(0, 1)), device_id_type=MESH)

    def to_azim(source, dest, rows, send, recv, o):
        there = lax.rem(a + o, azims)
        return pltpu.make_async_remote_copy(
            src_ref=source.at[pl.ds(pl.multiple_of(there * rows, 8), rows), :],
            dst_ref=dest.at[pl.ds(pl.multiple_of(a * rows, 8), rows), :],
            send_sem=send.at[o],
            recv_sem=recv.at[o],
            device_id=(there, p),
            device_id_type=MESH,
        )

    def own_azim(source, dest, rows, index):
        at = pl.ds(pl.multiple_of(a * rows, 8), rows)
        return pltpu.make_async_copy(source.at[at, :], dest.at[at, :], own_sem.at[index])

    def raw_copy(f):
        g = 0 if f < GROUPS[0][1] else 1
        return remote(
            cells.at[f, 0:SPREAD, :],
            raw_cells[g].at[f - GROUPS[g][0], 0:SPREAD, :],
            raw_send.at[f],
            raw_recv.at[f],
            plane_at(onward[g], 0),
        )

    def table_copies(g):
        there = plane_at(onward[g], 0)
        return (
            remote(integers_out, integers_in.at[g], table_send.at[2 * g], table_recv.at[2 * g], there),
            remote(
                reals_out, reals_in.at[g], table_send.at[2 * g + 1], table_recv.at[2 * g + 1], there
            ),
        )

    def tile_copy(g, place, owner, ahead, flip):
        index = g * PLACES + place
        return remote(
            packed[g].at[place],
            arrived[g].at[owner],
            tile_send.at[index],
            tile_recv.at[index],
            plane_at(ahead, flip),
        )

    def land_copy(index, owner, ahead, flip):
        return remote(
            landing.at[index],
            landing_in.at[owner],
            land_send.at[index],
            land_recv.at[index],
            plane_at(ahead, flip),
        )

    def direct_copy(g, flip):
        return tile_copy(g, flip, p, behind[g], flip)

    def relay_copy(g, u):
        return tile_copy(g, 2 + u, plane_at(behind[g], 0), (1 - u // 2) * onward[g], u - 2 * (u // 2))

    def mate_copy(g):
        return tile_copy(g, 6, p, 0, 1)

    spot = lax.broadcasted_iota(jnp.int32, (1, LANES), 1)
    for copy in small:
        copy.wait()
    for line, source in enumerate((destination, donor, receptor, offset_y, offset_x)):
        value = jnp.zeros((1, LANES), jnp.int32)
        for e in range(SLOTS):
            value = jnp.where(spot == e, source[e], value)
        integers_out[line : line + 1, :] = value
    for line, source in enumerate((fraction_y, fraction_x)):
        value = jnp.zeros((1, LANES), jnp.float32)
        for e in range(SLOTS):
            value = jnp.where(spot == e, source[e], value)
        reals_out[line : line + 1, :] = value

    def send_tables():
        for g in groups:
            for copy in table_copies(g):
                copy.start()

    @pl.when(core == 1)
    def _():
        pl.semaphore_wait(barrier, len(near))
        pl.semaphore_signal(mated, inc=1, device_id=(a, plane_at(0, 1)), device_id_type=MESH)
        for ahead in (1, chips - 1):
            pl.semaphore_signal(ready, inc=1, device_id=(a, plane_at(ahead, 1)), device_id_type=MESH)
        send_tables()

    for f in ORDER:
        large[f].wait()
        spread_twice(state.at[f], cells.at[f])

        @pl.when(core == 1)
        def _():
            raw_copy(f).start()

    @pl.when(core == 0)
    def _():
        pl.semaphore_wait(mated, 1)
        pl.semaphore_wait(ready, 2)
        send_tables()
        for f in ORDER:
            raw_copy(f).start()

    for copy in large[FIELDS:]:
        copy.wait()
    spread(raw_coefs, coefs)

    def one_part(part, carry):
        eliminate(cells, coefs, solved, tips, part)
        return carry

    lax.fori_loop(0, CHUNKS // 8, one_part, 0)

    def search(named, target, base):
        seen = jnp.int32(0)
        found = [jnp.int32(-1)] * CAP
        for e in range(SLOTS):
            match = named(e) == target
            for k in range(CAP):
                found[k] = jnp.where(match & (seen == k), e, found[k])
            seen = seen + jnp.where(match, 1, 0)
        for k in range(CAP):
            entries[base + k] = found[k]

    lane = lax.broadcasted_iota(jnp.int32, (CHUNKS, LANES), 1)
    high_half = lane >= TILE
    wide = lax.broadcasted_iota(jnp.int32, (LANES, 2 * LANES), 1)
    second = wide // LANES
    wide_lane = wide & (LANES - 1)
    from_lane = lax.broadcasted_iota(jnp.int32, (LANES, 2 * LANES), 0)

    def places_of(base, receptor_of):
        places = jnp.full((1, LANES), -1, jnp.int32)
        for k in range(CAP):
            entry = entries[base + k]
            place = jnp.where(entry >= 0, receptor_of(jnp.maximum(entry, 0)), -1)
            places = jnp.where(spot == k, place, places)
        return places

    def fill(base, table, blocks, dests):
        donor_of, oy_of, ox_of, fy_of, fx_of = table
        for k in range(CAP):
            e = jnp.maximum(entries[base + k], 0)
            row = donor_of(e)
            ox = ox_of(e)
            oy = oy_of(e)
            fx = fx_of(e)
            fy = fy_of(e)
            start = row + ROWS * (oy >> 1)
            odd = (oy & 1) == 1
            even_first = jnp.where(odd, 0.0, 1.0 - fy)
            even_second = jnp.where(odd, fy, 0.0)
            odd_weight = jnp.where(odd, 1.0 - fy, fy)
            pick = (wide_lane & TILE) + ((wide_lane + ox + second) & (TILE - 1))
            chosen = jnp.where(from_lane == pick, 1.0, 0.0).astype(jnp.bfloat16)
            values = []
            for source, f in blocks:
                here = source[f, pl.ds(start, CHUNKS, stride=ROWS), :]
                after = source[f, pl.ds(start + ROWS, CHUNKS, stride=ROWS), :]
                between = pltpu.roll(jnp.where(high_half, here, after), TILE, 1)
                values.append(even_first * here + even_second * after + odd_weight * between)
            value = jnp.concatenate(values, axis=0)
            high = value.astype(jnp.bfloat16)
            rest = value - high.astype(jnp.float32)
            middle = rest.astype(jnp.bfloat16)
            low = (rest - middle.astype(jnp.float32)).astype(jnp.bfloat16)
            moved = jnp.dot(
                jnp.concatenate([high, middle, low], axis=1),
                jnp.concatenate([chosen, chosen, chosen], axis=0),
                preferred_element_type=jnp.float32,
            )
            mixed = (1.0 - fx) * moved[:, :LANES] + fx * moved[:, LANES:]
            for n, (dest, place, f) in enumerate(dests):
                dest[place, k, f] = mixed[n * CHUNKS : (n + 1) * CHUNKS]

    own_table = tuple(
        functools.partial(lambda ref, e: ref[e], ref)
        for ref in (donor, offset_y, offset_x, fraction_y, fraction_x)
    )
    for g in groups:

        def find(flip, carry, g=g):
            search(lambda e: destination[e], plane_at(behind[g], flip), (2 * g + flip) * CAP)
            return carry

        lax.fori_loop(0, 2, find, 0)

    def find_near(flip, carry):
        search(lambda e: destination[e], plane_at(0, flip), (4 + flip) * CAP)
        return carry

    lax.fori_loop(0, 2, find_near, 0)
    for index in range(4):
        landing[index] = places_of(index * CAP, lambda e: receptor[e])
    landing[4] = places_of(5 * CAP, lambda e: receptor[e])
    landing[5] = places_of(4 * CAP, lambda e: receptor[e])
    near_land = [land_copy(2 * g + flip, p, behind[g], flip) for g in groups for flip in range(2)]
    near_land.append(land_copy(4, p, 0, 1))
    for copy in near_land:
        copy.start()
    own_land = pltpu.make_async_copy(landing.at[5], landing_in.at[p], own_sem.at[3])
    own_land.start()

    def widths(g):
        return range(GROUPS[g][1] - GROUPS[g][0])

    for g in groups:

        def fill_direct(flip, carry, g=g):
            fill(
                (2 * g + flip) * CAP,
                own_table,
                [(cells, GROUPS[g][0] + f) for f in widths(g)],
                [(packed[g], flip, f) for f in widths(g)],
            )
            return carry

        lax.fori_loop(0, 2, fill_direct, 0)

    @pl.when(core == 0)
    def _():
        pl.semaphore_wait(barrier, 2 * azims - 1)
        pl.semaphore_signal(go, inc=1, device_id=(a, plane_at(0, 1)), device_id_type=MESH)

    @pl.when(core == 1)
    def _():
        pl.semaphore_wait(go, 1)

    tip_copies = [to_azim(tips, tips_in, tip_rows, tips_send, tips_recv, o) for o in range(1, azims)]
    for copy in tip_copies:
        copy.start()
    own_tips = own_azim(tips, tips_in, tip_rows, 0)
    own_tips.start()

    def fill_near(flip, carry):
        fill(
            (4 + flip) * CAP,
            own_table,
            [(cells, f) for f in range(FIELDS)],
            [(packed[g], 7 - flip, f) for g in groups for f in widths(g)],
        )
        return carry

    lax.fori_loop(0, 2, fill_near, 0)
    own_tiles = [
        pltpu.make_async_copy(packed[g].at[7], arrived[g].at[p], own_sem.at[4 + g]) for g in groups
    ]
    for g in groups:
        mate_copy(g).start()
        own_tiles[g].start()

    for f in ORDER[:4]:
        raw_copy(f).wait_send()
    for flip in range(2):
        for g in groups:
            direct_copy(g, flip).start()
    raw_copy(ORDER[4]).wait_send()

    fetches = []
    for g in groups:
        for copy in table_copies(g):
            copy.wait()
        fetches.append(pltpu.make_async_copy(integers_in.at[g], integers.at[g], table_sem.at[2 * g]))
        fetches.append(pltpu.make_async_copy(reals_in.at[g], reals.at[g], table_sem.at[2 * g + 1]))
    for copy in fetches:
        copy.start()
    for copy in fetches:
        copy.wait()
    for g in groups:

        def find_relay(u, carry, g=g):
            target = plane_at((1 - u // 2) * onward[g], u - 2 * (u // 2))
            search(lambda e: integers[g, 0, e], target, (6 + 4 * g + u) * CAP)
            return carry

        lax.fori_loop(0, 4, find_relay, 0)
    far_land = []
    for u in range(2):
        landing[6 + u] = places_of((6 + u) * CAP, lambda e: integers[0, 2, e])
        far_land.append(land_copy(6 + u, plane_at(behind[0], 0), onward[0], u))
        far_land[-1].start()

    relay_own = [
        pltpu.make_async_copy(
            packed[g].at[4], arrived[g].at[plane_at(behind[g], 0)], own_sem.at[6 + g]
        )
        for g in groups
    ]
    def fill_relay(g, u):
        fill(
            (6 + 4 * g + u) * CAP,
            (
                lambda e: integers[g, 1, e],
                lambda e: integers[g, 3, e],
                lambda e: integers[g, 4, e],
                lambda e: reals[g, 0, e],
                lambda e: reals[g, 1, e],
            ),
            [(raw_cells[g], f) for f in widths(g)],
            [(packed[g], 2 + u, f) for f in widths(g)],
        )

    def pass_on():
        for g in groups:
            for f in widths(g):
                raw_copy(GROUPS[g][0] + f).wait_recv()
                raw_cells[g][f, SPREAD:, :] = raw_cells[g][f, 0:SPREAD, :]

            def fill_onward(u, carry, g=g):
                fill_relay(g, u)
                relay_copy(g, u).start()
                return carry

            lax.fori_loop(0, 2, fill_onward, 0)

    pl.when(core == 1)(pass_on)

    own_tips.wait()
    for copy in tip_copies:
        copy.wait()

    for v in range(TIPS):
        value = tips_in[pl.ds(v, CHUNKS, stride=TIPS), :]
        ping[v, 0:CHUNKS, :] = value
        ping[v, CHUNKS : 2 * CHUNKS, :] = value

    source, dest = ping, pong
    step = 1
    while step < azims:

        def level(part, carry, source=source, dest=dest, shift=step * per):
            row = pl.multiple_of(part * 8, 8)
            left = [source[COLS * i : COLS * (i + 1), pl.ds(row, 8), :] for i in range(4)]
            right = [source[COLS * i : COLS * (i + 1), pl.ds(row + shift, 8), :] for i in range(4)]
            for i, value in enumerate(merge(left, right)):
                dest[COLS * i : COLS * (i + 1), pl.ds(row, 8), :] = value
                dest[COLS * i : COLS * (i + 1), pl.ds(row + CHUNKS, 8), :] = value
            return carry

        lax.fori_loop(0, CHUNKS // 8, level, 0)
        source, dest = dest, source
        step *= 2

    def last(part, carry):
        row = pl.multiple_of(part * 8, 8)
        block = [source[COLS * i : COLS * (i + 1), pl.ds(row, 8), :] for i in range(4)]
        values = close(block)
        for i in range(2):
            firsts[FIELDS * i : FIELDS * (i + 1), pl.ds(row, 8), :] = values[i]
            firsts[FIELDS * i : FIELDS * (i + 1), pl.ds(row + CHUNKS, 8), :] = values[i]
            for f in range(FIELDS):
                answers[pl.ds(part * 8 * BACK + i * FIELDS + f, 8, stride=BACK), :] = values[2 + i][f]
        return carry

    lax.fori_loop(0, CHUNKS // 8, last, 0)
    for v in range(2 * FIELDS):
        answers[pl.ds(2 * FIELDS + v, CHUNKS, stride=BACK), :] = firsts[v, per : per + CHUNKS, :]

    back_copies = [
        to_azim(answers, borders, back_rows, back_send, back_recv, o) for o in range(1, azims)
    ]
    for copy in back_copies:
        copy.start()
    own_back = own_azim(answers, borders, back_rows, 1)
    own_back.start()
    pl.when(core == 0)(pass_on)

    for g in groups:

        def fill_chip(u, carry, g=g):
            fill_relay(g, u)
            return carry

        lax.fori_loop(2, 4, fill_chip, 0)
        relay_own[g].start()
        relay_copy(g, 3).start()

    own_back.wait()
    for copy in back_copies:
        copy.wait()

    def compose(part, carry):
        at = pl.ds(pl.multiple_of(part * 8, 8), 8)

        def border(i, f):
            return borders[pl.ds(part * 8 * BACK + i * FIELDS + f, 8, stride=BACK), :]

        for f in range(FIELDS):
            outside = [border(i, f) for i in range(4)]
            for r in range(ROWS):
                value = solved[r, f, at, :]
                for i in range(4):
                    value = value - solved[r, FIELDS + i, at, :] * outside[i]
                result[f, r // 8, pl.ds(part * 64 + r % 8, 8, stride=8), :] = value
        return carry

    lax.fori_loop(0, CHUNKS // 8, compose, 0)

    def move(c, carry):
        at = pl.ds(pl.multiple_of(c * LANES, LANES), LANES)
        row = pl.multiple_of(c * 8, 8)
        for f in range(FIELDS):
            update[f, 0:8, at] = result[f, 0, pl.ds(row, 8), :] - state[f, 0:8, at]
            update[f, 8:12, at] = result[f, 1, pl.ds(row, 4), :] - state[f, 8:12, at]
        return carry

    lax.fori_loop(0, CHUNKS, move, 0, unroll=4)

    for copy in [own_land] + own_tiles + relay_own + near_land + far_land:
        copy.wait()
    for g in groups:
        mate_copy(g).wait()
        for flip in range(2):
            direct_copy(g, flip).wait()
        for u in (3, 0, 1):
            relay_copy(g, u).wait()


def finish_kernel(landing, arrived0, arrived1, update, state, fringe, out_hbm, out, rows, cells, total, places, counts, sems):
    planes = landing.shape[0]
    fetch = pltpu.make_async_copy(landing, places, sems.at[FIELDS])
    fetch.start()
    for r in range(ROWS + 1):
        counts[r] = 0.0
    total[...] = jnp.zeros(total.shape, jnp.float32)
    fetch.wait()

    def add(slot, carry):
        d = slot // CAP
        k = slot - d * CAP
        row = places[d, 0, k]

        row = jnp.where(row >= 0, row, ROWS)
        for (low, high), source in zip(GROUPS, (arrived0, arrived1)):
            total[row, low:high] = total[row, low:high] + source[d, k]
        counts[row] = counts[row] + 1.0
        return carry

    lax.fori_loop(0, planes * CAP, add, 0, unroll=4)

    for b in range(2):
        line = lax.broadcasted_iota(jnp.int32, (8, LANES), 0) + 8 * b
        number = jnp.zeros((8, LANES), jnp.float32)
        for r in range(8 * b, min(8 * b + 8, ROWS)):
            number = jnp.where(line == r, counts[r], number)
        rows[2 * b] = number
        rows[2 * b + 1] = 1.0 / (number + 1.0)

    copies = []
    for f in range(FIELDS):
        for r in range(ROWS):
            cells[r // 8, pl.ds(r % 8, CHUNKS, stride=8), :] = total[r, f]

        def move(c, carry, f=f):
            at = pl.ds(pl.multiple_of(c * LANES, LANES), LANES)
            row = pl.multiple_of(c * 8, 8)
            for b, (low, high) in enumerate(((0, 8), (8, ROWS))):
                size = high - low
                q = state[f, low:high, at]
                relaxed = (cells[b, pl.ds(row, size), :] - rows[2 * b, 0:size, :] * q) * rows[
                    2 * b + 1, 0:size, :
                ]
                out[f, low:high, at] = jnp.where(
                    fringe[low:high, at] == 1, relaxed, update[f, low:high, at]
                )
            return carry

        lax.fori_loop(0, CHUNKS, move, 0, unroll=4)
        copy = pltpu.make_async_copy(out.at[f], out_hbm.at[f], sems.at[f])
        copy.start()
        copies.append(copy)
    for copy in copies:
        copy.wait()


def f32(*shape):
    return jax.ShapeDtypeStruct(shape, jnp.float32)


def local(
    state,
    speed,
    sigma,
    dissipation,
    fringe,
    destination,
    donor,
    receptor,
    offset_y,
    offset_x,
    fraction_y,
    fraction_x,
):
    azims = lax.axis_size("azim")
    planes = lax.axis_size("plane")
    vmem = pl.BlockSpec(memory_space=pltpu.VMEM)
    hbm = pl.BlockSpec(memory_space=pltpu.HBM)
    number = pltpu.VMEM
    wide0, wide1 = (high - low for low, high in GROUPS)
    arrived0, arrived1, landing_in, update = pl.pallas_call(
        functools.partial(exchange_kernel, azims, planes),
        out_shape=(
            f32(planes, CAP, wide0, CHUNKS, LANES),
            f32(planes, CAP, wide1, CHUNKS, LANES),
            jax.ShapeDtypeStruct((planes, 1, LANES), jnp.int32),
            f32(FIELDS, ROWS, CELLS),
        ),
        in_specs=[hbm] * 11,
        out_specs=(vmem,) * 4,
        scratch_shapes=[pltpu.SMEM((SLOTS,), jnp.int32)] * 5
        + [pltpu.SMEM((SLOTS,), jnp.float32)] * 2
        + [
            pltpu.SMEM((14 * CAP,), jnp.int32),
            pltpu.SMEM((2, 8, LANES), jnp.int32),
            pltpu.SMEM((2, 8, LANES), jnp.float32),
            number((FIELDS, ROWS, CELLS), jnp.float32),
            number((3, ROWS, CELLS), jnp.float32),
            number((FIELDS, 2, CHUNKS * 8, LANES), jnp.float32),
            number((FIELDS, 2 * SPREAD, LANES), jnp.float32),
            number((wide0, 2 * SPREAD, LANES), jnp.float32),
            number((wide1, 2 * SPREAD, LANES), jnp.float32),
            number((3, 2, CHUNKS * 8, LANES), jnp.float32),
            number((PLACES, CAP, wide0, CHUNKS, LANES), jnp.float32),
            number((PLACES, CAP, wide1, CHUNKS, LANES), jnp.float32),
            number((8, 1, LANES), jnp.int32),
            number((8, LANES), jnp.int32),
            number((8, LANES), jnp.float32),
            number((2, 8, LANES), jnp.int32),
            number((2, 8, LANES), jnp.float32),
            number((ROWS, COLS, CHUNKS, LANES), jnp.float32),
            number((CHUNKS * TIPS, LANES), jnp.float32),
            number((CHUNKS * TIPS, LANES), jnp.float32),
            number((TIPS, 2 * CHUNKS, LANES), jnp.float32),
            number((TIPS, 2 * CHUNKS, LANES), jnp.float32),
            number((2 * FIELDS, 2 * CHUNKS, LANES), jnp.float32),
            number((CHUNKS * BACK, LANES), jnp.float32),
            number((CHUNKS * BACK, LANES), jnp.float32),
            pltpu.SemaphoreType.DMA((7,)),
            pltpu.SemaphoreType.DMA((FIELDS + 3,)),
            pltpu.SemaphoreType.DMA((FIELDS,)),
            pltpu.SemaphoreType.DMA((FIELDS,)),
            pltpu.SemaphoreType.DMA((4,)),
            pltpu.SemaphoreType.DMA((4,)),
            pltpu.SemaphoreType.DMA((4,)),
            pltpu.SemaphoreType.DMA((2 * PLACES,)),
            pltpu.SemaphoreType.DMA((2 * PLACES,)),
            pltpu.SemaphoreType.DMA((8,)),
            pltpu.SemaphoreType.DMA((8,)),
            pltpu.SemaphoreType.DMA((azims,)),
            pltpu.SemaphoreType.DMA((azims,)),
            pltpu.SemaphoreType.DMA((azims,)),
            pltpu.SemaphoreType.DMA((azims,)),
            pltpu.SemaphoreType.DMA((8,)),
            pltpu.SemaphoreType.REGULAR,
            pltpu.SemaphoreType.REGULAR,
            pltpu.SemaphoreType.REGULAR,
        ],
        compiler_params=pltpu.CompilerParams(
            collective_id=0, has_side_effects=True, vmem_limit_bytes=40 * 2**20
        ),
        name="exchange",
    )(
        *(
            pltpu.with_memory_space_constraint(value, pltpu.HBM)
            for value in (
                destination.reshape(SLOTS),
                donor,
                receptor,
                offset_y,
                offset_x,
                fraction_y,
                fraction_x,
                state,
                speed,
                sigma,
                dissipation,
            )
        )
    )
    return pl.pallas_call(
        finish_kernel,
        out_shape=f32(FIELDS, ROWS, CELLS),
        in_specs=[vmem] * 6,
        out_specs=hbm,
        scratch_shapes=[
            number((FIELDS, ROWS, CELLS), jnp.float32),
            number((4, 8, LANES), jnp.float32),
            number((2, CHUNKS * 8, LANES), jnp.float32),
            number((ROWS + 1, FIELDS, CHUNKS, LANES), jnp.float32),
            pltpu.SMEM((planes, 1, LANES), jnp.int32),
            pltpu.SMEM((ROWS + 1,), jnp.float32),
            pltpu.SemaphoreType.DMA((FIELDS + 1,)),
        ],
        compiler_params=pltpu.CompilerParams(vmem_limit_bytes=32 * 2**20),
        name="finish",
    )(landing_in, arrived0, arrived1, update, state, fringe)


def solution(mesh):
    in_specs = (
        P(None, "azim", "plane"),
        P("azim", "plane"),
        P("azim", "plane"),
        P("azim", "plane"),
        P("azim", "plane"),
        P(("azim", "plane"), None),
        P(("azim", "plane")),
        P(("azim", "plane")),
        P(("azim", "plane")),
        P(("azim", "plane")),
        P(("azim", "plane")),
        P(("azim", "plane")),
    )
    out_specs = P(None, "azim", "plane")
    return jax.shard_map(local, mesh=mesh, in_specs=in_specs, out_specs=out_specs, check_vma=False)
```

```python
import functools

import jax
import jax.numpy as jnp
from jax import lax
from jax.experimental import pallas as pl
from jax.experimental.pallas import tpu as pltpu
from jax.sharding import PartitionSpec as P

TILE = 64
CAP = 4
FIELDS = 5
ROWS = 12
CELLS = TILE * TILE
LANES = 128
CHUNKS = CELLS // LANES
SLOTS = 16
COLS = FIELDS + 4
TIPS = 4 * COLS
BACK = 4 * FIELDS
MESH = pl.DeviceIdType.MESH
GROUPS = ((0, 3), (3, FIELDS))
PLACES = 8
ORDER = (0, 3, 1, 4, 2)
SPREAD = CHUNKS * ROWS
TIP_ROW = {0: 0, 1: 1, ROWS - 2: 2, ROWS - 1: 3}


def spread(source, dest):
    def move(c, carry):
        lane = pl.multiple_of(c * LANES, LANES)
        row = pl.multiple_of(c * 8, 8)
        for f in range(source.shape[0]):
            dest[f, 0, pl.ds(row, 8), :] = source[f, 0:8, pl.ds(lane, LANES)]
            dest[f, 1, pl.ds(row, 4), :] = source[f, 8:12, pl.ds(lane, LANES)]
        return carry

    lax.fori_loop(0, CHUNKS, move, 0, unroll=4)


def spread_twice(source, dest):
    def move(j, carry):
        lane = pl.multiple_of(j * 2 * LANES, 2 * LANES)
        row = pl.multiple_of(j * 2 * ROWS, 8)
        value = jnp.concatenate(
            [source[:, pl.ds(lane, LANES)], source[:, pl.ds(lane + LANES, LANES)]], axis=0
        )
        dest[pl.ds(row, 2 * ROWS), :] = value
        dest[pl.ds(row + SPREAD, 2 * ROWS), :] = value
        return carry

    lax.fori_loop(0, CHUNKS // 2, move, 0, unroll=4)


def eliminate(cells, coefs, solved, tips, part):
    base = part * 64
    at = pl.ds(pl.multiple_of(part * 8, 8), 8)

    def load(ref, lead, r):
        return ref[lead, r // 8, pl.ds(base + r % 8, 8, stride=8), :]

    def load_cells(k, r):
        return cells[k, pl.ds(part * 8 * ROWS + r, 8, stride=ROWS), :]

    upper1 = []
    upper2 = []
    fields1 = fields2 = None
    for r in range(ROWS):
        c = load(coefs, 0, r)
        s = load(coefs, 1, r)
        d = load(coefs, 2, r)
        half = 0.5 * c
        common = -s - 4.0 * d
        a1 = common - half
        e1 = common + half
        centre = 1.0 + (2.0 * s + 10.0 * d)
        weight = 1.0 + 4.0 * d
        if r == 0:
            pivot, u1_top = centre, e1
        elif r == 1:
            pivot = centre - a1 * upper1[0]
            u1_top = e1 - a1 * upper2[0]
        else:
            a1 = a1 - d * upper1[r - 2]
            pivot = centre - d * upper2[r - 2] - a1 * upper1[r - 1]
            u1_top = e1 - a1 * upper2[r - 1]
        inverse = 1.0 / pivot
        upper1.append(u1_top * inverse)
        upper2.append(d * inverse)
        now = []
        for k in range(FIELDS + 2):
            if k < FIELDS:
                value = weight * load_cells(k, r)
            elif r == 0:
                now.append((d if k == FIELDS else a1) * inverse)
                continue
            elif r == 1 and k == FIELDS + 1:
                value = d
            else:
                value = None
            if r >= 1:
                term = a1 * fields1[k]
                value = -term if value is None else value - term
            if r >= 2:
                value = value - d * fields2[k]
            now.append(value * inverse)
        for k in range(FIELDS + 2):
            solved[r, k, at, :] = now[k]
        fields2, fields1 = fields1, now

    later1 = later2 = None
    for r in range(ROWS - 1, -1, -1):
        now = []
        for k in range(COLS):
            if k < FIELDS + 2:
                value = solved[r, k, at, :]
            elif r == ROWS - 1:
                value = upper1[r] if k == FIELDS + 2 else upper2[r]
            elif r == ROWS - 2 and k == FIELDS + 2:
                value = upper2[r]
            else:
                value = None
            if r < ROWS - 1:
                term = upper1[r] * later1[k]
                value = -term if value is None else value - term
            if r < ROWS - 2:
                value = value - upper2[r] * later2[k]
            now.append(value)
        for k in range(COLS):
            solved[r, k, at, :] = now[k]
        if r in TIP_ROW:
            for k in range(COLS):
                tips[pl.ds(part * 8 * TIPS + TIP_ROW[r] * COLS + k, 8, stride=TIPS), :] = now[k]
        later2, later1 = later1, now


def merge(left, right):
    def pair(matrix, columns):
        return [matrix[i][0] * columns[0] + matrix[i][1] * columns[1] for i in range(2)]

    gs = slice(0, FIELDS)
    ws = slice(FIELDS, FIELDS + 2)
    vs = slice(FIELDS + 2, FIELDS + 4)
    left_v = [[left[i][FIELDS + 2 + m] for m in range(2)] for i in range(4)]
    right_w = [[right[i][FIELDS + m] for m in range(2)] for i in range(4)]
    nothing = jnp.zeros((2,) + left[0].shape[1:], jnp.float32)
    product = [
        [sum(right_w[i][m] * left_v[2 + m][j] for m in range(2)) for j in range(2)]
        for i in range(2)
    ]
    m00, m01 = 1.0 - product[0][0], -product[0][1]
    m10, m11 = -product[1][0], 1.0 - product[1][1]
    scale = 1.0 / (m00 * m11 - m01 * m10)
    inverse = [[m11 * scale, -m01 * scale], [-m10 * scale, m00 * scale]]
    known = [jnp.concatenate([left[2 + i][gs], left[2 + i][ws]], axis=0) for i in range(2)]
    through = pair(right_w[:2], known)
    raw = [
        jnp.concatenate(
            [right[i][gs] - through[i][gs], -through[i][FIELDS:], right[i][vs]], axis=0
        )
        for i in range(2)
    ]
    inner_a = pair(inverse, raw)
    from_a = pair(left_v[2:], inner_a)
    inner_b = [
        jnp.concatenate([left[2 + i][gs], left[2 + i][ws], nothing], axis=0) - from_a[i]
        for i in range(2)
    ]
    from_a = pair(left_v[:2], inner_a)
    outer_a = [
        jnp.concatenate([left[i][gs], left[i][ws], nothing], axis=0) - from_a[i] for i in range(2)
    ]
    from_b = pair(right_w[2:], inner_b)
    outer_b = [
        jnp.concatenate([right[2 + i][gs], nothing, right[2 + i][vs]], axis=0) - from_b[i]
        for i in range(2)
    ]
    return outer_a + outer_b


def close(block):
    matrix = []
    for i in range(4):
        line = [block[i][FIELDS + 2], block[i][FIELDS + 3], block[i][FIELDS], block[i][FIELDS + 1]]
        line[i] = 1.0 + line[i]
        matrix.append(line)
    values = [block[i][0:FIELDS] for i in range(4)]
    for p in range(4):
        scale = 1.0 / matrix[p][p]
        for c in range(p + 1, 4):
            matrix[p][c] = matrix[p][c] * scale
        values[p] = values[p] * scale
        for r in range(p + 1, 4):
            for c in range(p + 1, 4):
                matrix[r][c] = matrix[r][c] - matrix[r][p] * matrix[p][c]
            values[r] = values[r] - matrix[r][p] * values[p]
    for r in range(2, -1, -1):
        for c in range(r + 1, 4):
            values[r] = values[r] - matrix[r][c] * values[c]
    return values


def exchange_kernel(
    azims,
    planes,
    destination_hbm,
    donor_hbm,
    receptor_hbm,
    offset_y_hbm,
    offset_x_hbm,
    fraction_y_hbm,
    fraction_x_hbm,
    state_hbm,
    speed_hbm,
    sigma_hbm,
    dissipation_hbm,
    arrived0,
    arrived1,
    landing_in,
    update,
    destination,
    donor,
    receptor,
    offset_y,
    offset_x,
    fraction_y,
    fraction_x,
    entries,
    integers,
    reals,
    state,
    raw_coefs,
    result,
    cells,
    cells0,
    cells1,
    coefs,
    packed0,
    packed1,
    landing,
    integers_out,
    reals_out,
    integers_in,
    reals_in,
    solved,
    tips,
    tips_in,
    ping,
    pong,
    firsts,
    answers,
    borders,
    small_sem,
    large_sem,
    raw_send,
    raw_recv,
    table_send,
    table_recv,
    table_sem,
    tile_send,
    tile_recv,
    land_send,
    land_recv,
    tips_send,
    tips_recv,
    back_send,
    back_recv,
    own_sem,
    mated,
    ready,
    go,
):
    a = lax.axis_index("azim")
    p = lax.axis_index("plane")
    per = CHUNKS // azims
    tip_rows = per * TIPS
    back_rows = per * BACK
    chips = planes // 2
    core = lax.rem(p, 2)
    groups = (0, 1)
    arrived = (arrived0, arrived1)
    packed = (packed0, packed1)
    raw_cells = (cells0, cells1)

    small = [
        pltpu.make_async_copy(source, dest, small_sem.at[i])
        for i, (source, dest) in enumerate(
            (
                (destination_hbm, destination),
                (donor_hbm, donor),
                (receptor_hbm, receptor),
                (offset_y_hbm, offset_y),
                (offset_x_hbm, offset_x),
                (fraction_y_hbm, fraction_y),
                (fraction_x_hbm, fraction_x),
            )
        )
    ]
    large = [
        pltpu.make_async_copy(source, dest, large_sem.at[i])
        for i, (source, dest) in enumerate(
            [(state_hbm.at[f], state.at[f]) for f in range(FIELDS)]
            + [
                (speed_hbm, raw_coefs.at[0]),
                (sigma_hbm, raw_coefs.at[1]),
                (dissipation_hbm, raw_coefs.at[2]),
            ]
        )
    ]
    for copy in small:
        copy.start()
    for copy in large:
        copy.start()

    barrier = pltpu.get_barrier_semaphore()
    near = [(0, 1), (1, 0), (1, 1), (chips - 1, 0), (chips - 1, 1)]

    def plane_at(ahead, flip):
        return lax.rem(p // 2 + ahead, chips) * 2 + lax.rem(p + flip, 2)

    def remote(source, dest, send, recv, there):
        return pltpu.make_async_remote_copy(
            src_ref=source,
            dst_ref=dest,
            send_sem=send,
            recv_sem=recv,
            device_id=(a, there),
            device_id_type=MESH,
        )

    onward = (1 + core * (chips - 2), chips - 1 - core * (chips - 2))
    behind = (onward[1], onward[0])

    for ahead, flip in near:

        @pl.when(lax.rem(core + flip, 2) == 1)
        def _():
            pl.semaphore_signal(
                barrier, inc=1, device_id=(a, plane_at(ahead, flip)), device_id_type=MESH
            )

    for o in range(1, azims):
        pl.semaphore_signal(
            barrier, inc=1, device_id=(lax.rem(a + o, azims), p - core), device_id_type=MESH
        )

    @pl.when(core == 1)
    def _():
        pl.semaphore_signal(barrier, inc=1, device_id=(a, plane_at(0, 1)), device_id_type=MESH)

    def to_azim(source, dest, rows, send, recv, o):
        there = lax.rem(a + o, azims)
        return pltpu.make_async_remote_copy(
            src_ref=source.at[pl.ds(pl.multiple_of(there * rows, 8), rows), :],
            dst_ref=dest.at[pl.ds(pl.multiple_of(a * rows, 8), rows), :],
            send_sem=send.at[o],
            recv_sem=recv.at[o],
            device_id=(there, p),
            device_id_type=MESH,
        )

    def own_azim(source, dest, rows, index):
        at = pl.ds(pl.multiple_of(a * rows, 8), rows)
        return pltpu.make_async_copy(source.at[at, :], dest.at[at, :], own_sem.at[index])

    def raw_copy(f):
        g = 0 if f < GROUPS[0][1] else 1
        return remote(
            cells.at[f, 0:SPREAD, :],
            raw_cells[g].at[f - GROUPS[g][0], 0:SPREAD, :],
            raw_send.at[f],
            raw_recv.at[f],
            plane_at(onward[g], 0),
        )

    def table_copies(g):
        there = plane_at(onward[g], 0)
        return (
            remote(integers_out, integers_in.at[g], table_send.at[2 * g], table_recv.at[2 * g], there),
            remote(
                reals_out, reals_in.at[g], table_send.at[2 * g + 1], table_recv.at[2 * g + 1], there
            ),
        )

    def tile_copy(g, place, owner, ahead, flip):
        index = g * PLACES + place
        return remote(
            packed[g].at[place],
            arrived[g].at[owner],
            tile_send.at[index],
            tile_recv.at[index],
            plane_at(ahead, flip),
        )

    def land_copy(index, owner, ahead, flip):
        return remote(
            landing.at[index],
            landing_in.at[owner],
            land_send.at[index],
            land_recv.at[index],
            plane_at(ahead, flip),
        )

    def direct_copy(g, flip):
        return tile_copy(g, flip, p, behind[g], flip)

    def relay_copy(g, u):
        return tile_copy(g, 2 + u, plane_at(behind[g], 0), (1 - u // 2) * onward[g], u - 2 * (u // 2))

    def mate_copy(g):
        return tile_copy(g, 6, p, 0, 1)

    spot = lax.broadcasted_iota(jnp.int32, (1, LANES), 1)
    for copy in small:
        copy.wait()
    for line, source in enumerate((destination, donor, receptor, offset_y, offset_x)):
        value = jnp.zeros((1, LANES), jnp.int32)
        for e in range(SLOTS):
            value = jnp.where(spot == e, source[e], value)
        integers_out[line : line + 1, :] = value
    for line, source in enumerate((fraction_y, fraction_x)):
        value = jnp.zeros((1, LANES), jnp.float32)
        for e in range(SLOTS):
            value = jnp.where(spot == e, source[e], value)
        reals_out[line : line + 1, :] = value

    def send_tables():
        for g in groups:
            for copy in table_copies(g):
                copy.start()

    @pl.when(core == 1)
    def _():
        pl.semaphore_wait(barrier, len(near))
        pl.semaphore_signal(mated, inc=1, device_id=(a, plane_at(0, 1)), device_id_type=MESH)
        for ahead in (1, chips - 1):
            pl.semaphore_signal(ready, inc=1, device_id=(a, plane_at(ahead, 1)), device_id_type=MESH)
        send_tables()

    for f in ORDER:
        large[f].wait()
        spread_twice(state.at[f], cells.at[f])

        @pl.when(core == 1)
        def _():
            raw_copy(f).start()

    @pl.when(core == 0)
    def _():
        pl.semaphore_wait(mated, 1)
        pl.semaphore_wait(ready, 2)
        send_tables()
        for f in ORDER:
            raw_copy(f).start()

    for copy in large[FIELDS:]:
        copy.wait()
    spread(raw_coefs, coefs)

    def one_part(part, carry):
        eliminate(cells, coefs, solved, tips, part)
        return carry

    lax.fori_loop(0, CHUNKS // 8, one_part, 0)

    def search(named, target, base):
        seen = jnp.int32(0)
        found = [jnp.int32(-1)] * CAP
        for e in range(SLOTS):
            match = named(e) == target
            for k in range(CAP):
                found[k] = jnp.where(match & (seen == k), e, found[k])
            seen = seen + jnp.where(match, 1, 0)
        for k in range(CAP):
            entries[base + k] = found[k]

    lane = lax.broadcasted_iota(jnp.int32, (CHUNKS, LANES), 1)
    high_half = lane >= TILE
    wide = lax.broadcasted_iota(jnp.int32, (LANES, 2 * LANES), 1)
    second = wide // LANES
    wide_lane = wide & (LANES - 1)
    from_lane = lax.broadcasted_iota(jnp.int32, (LANES, 2 * LANES), 0)

    def places_of(base, receptor_of):
        places = jnp.full((1, LANES), -1, jnp.int32)
        for k in range(CAP):
            entry = entries[base + k]
            place = jnp.where(entry >= 0, receptor_of(jnp.maximum(entry, 0)), -1)
            places = jnp.where(spot == k, place, places)
        return places

    def fill(base, table, blocks, dests):
        donor_of, oy_of, ox_of, fy_of, fx_of = table
        for k in range(CAP):
            e = jnp.maximum(entries[base + k], 0)
            row = donor_of(e)
            ox = ox_of(e)
            oy = oy_of(e)
            fx = fx_of(e)
            fy = fy_of(e)
            start = row + ROWS * (oy >> 1)
            odd = (oy & 1) == 1
            even_first = jnp.where(odd, 0.0, 1.0 - fy)
            even_second = jnp.where(odd, fy, 0.0)
            odd_weight = jnp.where(odd, 1.0 - fy, fy)
            pick = (wide_lane & TILE) + ((wide_lane + ox + second) & (TILE - 1))
            chosen = jnp.where(from_lane == pick, 1.0, 0.0).astype(jnp.bfloat16)
            values = []
            for source, f in blocks:
                here = source[f, pl.ds(start, CHUNKS, stride=ROWS), :]
                after = source[f, pl.ds(start + ROWS, CHUNKS, stride=ROWS), :]
                between = pltpu.roll(jnp.where(high_half, here, after), TILE, 1)
                values.append(even_first * here + even_second * after + odd_weight * between)
            value = jnp.concatenate(values, axis=0)
            high = value.astype(jnp.bfloat16)
            rest = value - high.astype(jnp.float32)
            middle = rest.astype(jnp.bfloat16)
            low = (rest - middle.astype(jnp.float32)).astype(jnp.bfloat16)
            moved = jnp.dot(
                jnp.concatenate([high, middle, low], axis=1),
                jnp.concatenate([chosen, chosen, chosen], axis=0),
                preferred_element_type=jnp.float32,
            )
            mixed = (1.0 - fx) * moved[:, :LANES] + fx * moved[:, LANES:]
            for n, (dest, place, f) in enumerate(dests):
                dest[place, k, f] = mixed[n * CHUNKS : (n + 1) * CHUNKS]

    own_table = tuple(
        functools.partial(lambda ref, e: ref[e], ref)
        for ref in (donor, offset_y, offset_x, fraction_y, fraction_x)
    )
    for g in groups:

        def find(flip, carry, g=g):
            search(lambda e: destination[e], plane_at(behind[g], flip), (2 * g + flip) * CAP)
            return carry

        lax.fori_loop(0, 2, find, 0)

    def find_near(flip, carry):
        search(lambda e: destination[e], plane_at(0, flip), (4 + flip) * CAP)
        return carry

    lax.fori_loop(0, 2, find_near, 0)
    for index in range(4):
        landing[index] = places_of(index * CAP, lambda e: receptor[e])
    landing[4] = places_of(5 * CAP, lambda e: receptor[e])
    landing[5] = places_of(4 * CAP, lambda e: receptor[e])
    near_land = [land_copy(2 * g + flip, p, behind[g], flip) for g in groups for flip in range(2)]
    near_land.append(land_copy(4, p, 0, 1))
    for copy in near_land:
        copy.start()
    own_land = pltpu.make_async_copy(landing.at[5], landing_in.at[p], own_sem.at[3])
    own_land.start()

    def widths(g):
        return range(GROUPS[g][1] - GROUPS[g][0])

    for g in groups:

        def fill_direct(flip, carry, g=g):
            fill(
                (2 * g + flip) * CAP,
                own_table,
                [(cells, GROUPS[g][0] + f) for f in widths(g)],
                [(packed[g], flip, f) for f in widths(g)],
            )
            return carry

        lax.fori_loop(0, 2, fill_direct, 0)

    @pl.when(core == 0)
    def _():
        pl.semaphore_wait(barrier, 2 * azims - 1)
        pl.semaphore_signal(go, inc=1, device_id=(a, plane_at(0, 1)), device_id_type=MESH)

    @pl.when(core == 1)
    def _():
        pl.semaphore_wait(go, 1)

    tip_copies = [to_azim(tips, tips_in, tip_rows, tips_send, tips_recv, o) for o in range(1, azims)]
    for copy in tip_copies:
        copy.start()
    own_tips = own_azim(tips, tips_in, tip_rows, 0)
    own_tips.start()

    def fill_near(flip, carry):
        fill(
            (4 + flip) * CAP,
            own_table,
            [(cells, f) for f in range(FIELDS)],
            [(packed[g], 7 - flip, f) for g in groups for f in widths(g)],
        )
        return carry

    lax.fori_loop(0, 2, fill_near, 0)
    own_tiles = [
        pltpu.make_async_copy(packed[g].at[7], arrived[g].at[p], own_sem.at[4 + g]) for g in groups
    ]
    for g in groups:
        mate_copy(g).start()
        own_tiles[g].start()

    for f in ORDER[:4]:
        raw_copy(f).wait_send()
    for flip in range(2):
        for g in groups:
            direct_copy(g, flip).start()
    raw_copy(ORDER[4]).wait_send()

    fetches = []
    for g in groups:
        for copy in table_copies(g):
            copy.wait()
        fetches.append(pltpu.make_async_copy(integers_in.at[g], integers.at[g], table_sem.at[2 * g]))
        fetches.append(pltpu.make_async_copy(reals_in.at[g], reals.at[g], table_sem.at[2 * g + 1]))
    for copy in fetches:
        copy.start()
    for copy in fetches:
        copy.wait()
    for g in groups:

        def find_relay(u, carry, g=g):
            target = plane_at((1 - u // 2) * onward[g], u - 2 * (u // 2))
            search(lambda e: integers[g, 0, e], target, (6 + 4 * g + u) * CAP)
            return carry

        lax.fori_loop(0, 4, find_relay, 0)
    far_land = []
    for u in range(2):
        landing[6 + u] = places_of((6 + u) * CAP, lambda e: integers[0, 2, e])
        far_land.append(land_copy(6 + u, plane_at(behind[0], 0), onward[0], u))
        far_land[-1].start()

    relay_own = [
        pltpu.make_async_copy(
            packed[g].at[4], arrived[g].at[plane_at(behind[g], 0)], own_sem.at[6 + g]
        )
        for g in groups
    ]
    def fill_relay(g, u):
        fill(
            (6 + 4 * g + u) * CAP,
            (
                lambda e: integers[g, 1, e],
                lambda e: integers[g, 3, e],
                lambda e: integers[g, 4, e],
                lambda e: reals[g, 0, e],
                lambda e: reals[g, 1, e],
            ),
            [(raw_cells[g], f) for f in widths(g)],
            [(packed[g], 2 + u, f) for f in widths(g)],
        )

    def pass_on():
        for g in groups:
            for f in widths(g):
                raw_copy(GROUPS[g][0] + f).wait_recv()
                raw_cells[g][f, SPREAD:, :] = raw_cells[g][f, 0:SPREAD, :]

            def fill_onward(u, carry, g=g):
                fill_relay(g, u)
                relay_copy(g, u).start()
                return carry

            lax.fori_loop(0, 2, fill_onward, 0)

    pl.when(core == 1)(pass_on)

    own_tips.wait()
    for copy in tip_copies:
        copy.wait()

    for v in range(TIPS):
        value = tips_in[pl.ds(v, CHUNKS, stride=TIPS), :]
        ping[v, 0:CHUNKS, :] = value
        ping[v, CHUNKS : 2 * CHUNKS, :] = value

    source, dest = ping, pong
    step = 1
    while step < azims:

        def level(part, carry, source=source, dest=dest, shift=step * per):
            row = pl.multiple_of(part * 8, 8)
            left = [source[COLS * i : COLS * (i + 1), pl.ds(row, 8), :] for i in range(4)]
            right = [source[COLS * i : COLS * (i + 1), pl.ds(row + shift, 8), :] for i in range(4)]
            for i, value in enumerate(merge(left, right)):
                dest[COLS * i : COLS * (i + 1), pl.ds(row, 8), :] = value
                dest[COLS * i : COLS * (i + 1), pl.ds(row + CHUNKS, 8), :] = value
            return carry

        lax.fori_loop(0, CHUNKS // 8, level, 0)
        source, dest = dest, source
        step *= 2

    def last(part, carry):
        row = pl.multiple_of(part * 8, 8)
        block = [source[COLS * i : COLS * (i + 1), pl.ds(row, 8), :] for i in range(4)]
        values = close(block)
        for i in range(2):
            firsts[FIELDS * i : FIELDS * (i + 1), pl.ds(row, 8), :] = values[i]
            firsts[FIELDS * i : FIELDS * (i + 1), pl.ds(row + CHUNKS, 8), :] = values[i]
            for f in range(FIELDS):
                answers[pl.ds(part * 8 * BACK + i * FIELDS + f, 8, stride=BACK), :] = values[2 + i][f]
        return carry

    lax.fori_loop(0, CHUNKS // 8, last, 0)
    for v in range(2 * FIELDS):
        answers[pl.ds(2 * FIELDS + v, CHUNKS, stride=BACK), :] = firsts[v, per : per + CHUNKS, :]

    back_copies = [
        to_azim(answers, borders, back_rows, back_send, back_recv, o) for o in range(1, azims)
    ]
    for copy in back_copies:
        copy.start()
    own_back = own_azim(answers, borders, back_rows, 1)
    own_back.start()
    pl.when(core == 0)(pass_on)

    for g in groups:

        def fill_chip(u, carry, g=g):
            fill_relay(g, u)
            return carry

        lax.fori_loop(2, 4, fill_chip, 0)
        relay_own[g].start()
        relay_copy(g, 3).start()

    own_back.wait()
    for copy in back_copies:
        copy.wait()

    def compose(part, carry):
        at = pl.ds(pl.multiple_of(part * 8, 8), 8)

        def border(i, f):
            return borders[pl.ds(part * 8 * BACK + i * FIELDS + f, 8, stride=BACK), :]

        for f in range(FIELDS):
            outside = [border(i, f) for i in range(4)]
            for r in range(ROWS):
                value = solved[r, f, at, :]
                for i in range(4):
                    value = value - solved[r, FIELDS + i, at, :] * outside[i]
                result[f, r // 8, pl.ds(part * 64 + r % 8, 8, stride=8), :] = value
        return carry

    lax.fori_loop(0, CHUNKS // 8, compose, 0)

    def move(c, carry):
        at = pl.ds(pl.multiple_of(c * LANES, LANES), LANES)
        row = pl.multiple_of(c * 8, 8)
        for f in range(FIELDS):
            update[f, 0:8, at] = result[f, 0, pl.ds(row, 8), :] - state[f, 0:8, at]
            update[f, 8:12, at] = result[f, 1, pl.ds(row, 4), :] - state[f, 8:12, at]
        return carry

    lax.fori_loop(0, CHUNKS, move, 0, unroll=4)

    for copy in [own_land] + own_tiles + relay_own + near_land + far_land:
        copy.wait()
    for g in groups:
        mate_copy(g).wait()
        for flip in range(2):
            direct_copy(g, flip).wait()
        for u in (3, 0, 1):
            relay_copy(g, u).wait()


def finish_kernel(landing, arrived0, arrived1, update, state, fringe, out_hbm, out, rows, cells, total, places, counts, sems):
    planes = landing.shape[0]
    fetch = pltpu.make_async_copy(landing, places, sems.at[FIELDS])
    fetch.start()
    for r in range(ROWS + 1):
        counts[r] = 0.0
    total[...] = jnp.zeros(total.shape, jnp.float32)
    fetch.wait()

    def add(slot, carry):
        d = slot // CAP
        k = slot - d * CAP
        row = places[d, 0, k]

        row = jnp.where(row >= 0, row, ROWS)
        for (low, high), source in zip(GROUPS, (arrived0, arrived1)):
            total[row, low:high] = total[row, low:high] + source[d, k]
        counts[row] = counts[row] + 1.0
        return carry

    lax.fori_loop(0, planes * CAP, add, 0, unroll=8)

    for b in range(2):
        line = lax.broadcasted_iota(jnp.int32, (8, LANES), 0) + 8 * b
        number = jnp.zeros((8, LANES), jnp.float32)
        for r in range(8 * b, min(8 * b + 8, ROWS)):
            number = jnp.where(line == r, counts[r], number)
        rows[2 * b] = number
        rows[2 * b + 1] = 1.0 / (number + 1.0)

    copies = []
    for f in range(FIELDS):
        for r in range(ROWS):
            cells[r // 8, pl.ds(r % 8, CHUNKS, stride=8), :] = total[r, f]

        def move(c, carry, f=f):
            at = pl.ds(pl.multiple_of(c * LANES, LANES), LANES)
            row = pl.multiple_of(c * 8, 8)
            for b, (low, high) in enumerate(((0, 8), (8, ROWS))):
                size = high - low
                q = state[f, low:high, at]
                relaxed = (cells[b, pl.ds(row, size), :] - rows[2 * b, 0:size, :] * q) * rows[
                    2 * b + 1, 0:size, :
                ]
                out[f, low:high, at] = jnp.where(
                    fringe[low:high, at] == 1, relaxed, update[f, low:high, at]
                )
            return carry

        lax.fori_loop(0, CHUNKS, move, 0, unroll=8)
        copy = pltpu.make_async_copy(out.at[f], out_hbm.at[f], sems.at[f])
        copy.start()
        copies.append(copy)
    for copy in copies:
        copy.wait()


def f32(*shape):
    return jax.ShapeDtypeStruct(shape, jnp.float32)


def local(
    state,
    speed,
    sigma,
    dissipation,
    fringe,
    destination,
    donor,
    receptor,
    offset_y,
    offset_x,
    fraction_y,
    fraction_x,
):
    azims = lax.axis_size("azim")
    planes = lax.axis_size("plane")
    vmem = pl.BlockSpec(memory_space=pltpu.VMEM)
    hbm = pl.BlockSpec(memory_space=pltpu.HBM)
    number = pltpu.VMEM
    wide0, wide1 = (high - low for low, high in GROUPS)
    arrived0, arrived1, landing_in, update = pl.pallas_call(
        functools.partial(exchange_kernel, azims, planes),
        out_shape=(
            f32(planes, CAP, wide0, CHUNKS, LANES),
            f32(planes, CAP, wide1, CHUNKS, LANES),
            jax.ShapeDtypeStruct((planes, 1, LANES), jnp.int32),
            f32(FIELDS, ROWS, CELLS),
        ),
        in_specs=[hbm] * 11,
        out_specs=(vmem,) * 4,
        scratch_shapes=[pltpu.SMEM((SLOTS,), jnp.int32)] * 5
        + [pltpu.SMEM((SLOTS,), jnp.float32)] * 2
        + [
            pltpu.SMEM((14 * CAP,), jnp.int32),
            pltpu.SMEM((2, 8, LANES), jnp.int32),
            pltpu.SMEM((2, 8, LANES), jnp.float32),
            number((FIELDS, ROWS, CELLS), jnp.float32),
            number((3, ROWS, CELLS), jnp.float32),
            number((FIELDS, 2, CHUNKS * 8, LANES), jnp.float32),
            number((FIELDS, 2 * SPREAD, LANES), jnp.float32),
            number((wide0, 2 * SPREAD, LANES), jnp.float32),
            number((wide1, 2 * SPREAD, LANES), jnp.float32),
            number((3, 2, CHUNKS * 8, LANES), jnp.float32),
            number((PLACES, CAP, wide0, CHUNKS, LANES), jnp.float32),
            number((PLACES, CAP, wide1, CHUNKS, LANES), jnp.float32),
            number((8, 1, LANES), jnp.int32),
            number((8, LANES), jnp.int32),
            number((8, LANES), jnp.float32),
            number((2, 8, LANES), jnp.int32),
            number((2, 8, LANES), jnp.float32),
            number((ROWS, COLS, CHUNKS, LANES), jnp.float32),
            number((CHUNKS * TIPS, LANES), jnp.float32),
            number((CHUNKS * TIPS, LANES), jnp.float32),
            number((TIPS, 2 * CHUNKS, LANES), jnp.float32),
            number((TIPS, 2 * CHUNKS, LANES), jnp.float32),
            number((2 * FIELDS, 2 * CHUNKS, LANES), jnp.float32),
            number((CHUNKS * BACK, LANES), jnp.float32),
            number((CHUNKS * BACK, LANES), jnp.float32),
            pltpu.SemaphoreType.DMA((7,)),
            pltpu.SemaphoreType.DMA((FIELDS + 3,)),
            pltpu.SemaphoreType.DMA((FIELDS,)),
            pltpu.SemaphoreType.DMA((FIELDS,)),
            pltpu.SemaphoreType.DMA((4,)),
            pltpu.SemaphoreType.DMA((4,)),
            pltpu.SemaphoreType.DMA((4,)),
            pltpu.SemaphoreType.DMA((2 * PLACES,)),
            pltpu.SemaphoreType.DMA((2 * PLACES,)),
            pltpu.SemaphoreType.DMA((8,)),
            pltpu.SemaphoreType.DMA((8,)),
            pltpu.SemaphoreType.DMA((azims,)),
            pltpu.SemaphoreType.DMA((azims,)),
            pltpu.SemaphoreType.DMA((azims,)),
            pltpu.SemaphoreType.DMA((azims,)),
            pltpu.SemaphoreType.DMA((8,)),
            pltpu.SemaphoreType.REGULAR,
            pltpu.SemaphoreType.REGULAR,
            pltpu.SemaphoreType.REGULAR,
        ],
        compiler_params=pltpu.CompilerParams(
            collective_id=0, has_side_effects=True, vmem_limit_bytes=40 * 2**20
        ),
        name="exchange",
    )(
        *(
            pltpu.with_memory_space_constraint(value, pltpu.HBM)
            for value in (
                destination.reshape(SLOTS),
                donor,
                receptor,
                offset_y,
                offset_x,
                fraction_y,
                fraction_x,
                state,
                speed,
                sigma,
                dissipation,
            )
        )
    )
    return pl.pallas_call(
        finish_kernel,
        out_shape=f32(FIELDS, ROWS, CELLS),
        in_specs=[vmem] * 6,
        out_specs=hbm,
        scratch_shapes=[
            number((FIELDS, ROWS, CELLS), jnp.float32),
            number((4, 8, LANES), jnp.float32),
            number((2, CHUNKS * 8, LANES), jnp.float32),
            number((ROWS + 1, FIELDS, CHUNKS, LANES), jnp.float32),
            pltpu.SMEM((planes, 1, LANES), jnp.int32),
            pltpu.SMEM((ROWS + 1,), jnp.float32),
            pltpu.SemaphoreType.DMA((FIELDS + 1,)),
        ],
        compiler_params=pltpu.CompilerParams(vmem_limit_bytes=32 * 2**20),
        name="finish",
    )(landing_in, arrived0, arrived1, update, state, fringe)


def solution(mesh):
    in_specs = (
        P(None, "azim", "plane"),
        P("azim", "plane"),
        P("azim", "plane"),
        P("azim", "plane"),
        P("azim", "plane"),
        P(("azim", "plane"), None),
        P(("azim", "plane")),
        P(("azim", "plane")),
        P(("azim", "plane")),
        P(("azim", "plane")),
        P(("azim", "plane")),
        P(("azim", "plane")),
    )
    out_specs = P(None, "azim", "plane")
    return jax.shard_map(local, mesh=mesh, in_specs=in_specs, out_specs=out_specs, check_vma=False)
```
